512 devices in a mesh: group: 2 (over y_lo), gx: 32 (over y_hi, z), gy: 8 (over x, core).
Axes of the slice: x: 4, y: 8 (y_hi: 4, y_lo: 2; y = y_hi * 2 + y_lo), z: 8, core: 2. Of those that a mesh axis runs over, the one named last changes fastest.
Arguments:
- les_state: float32 [5, 256, 96, 1024], P(None, 'gx', 'group', 'gy'), may hold values from -0.5 to 1.25, as said below
- wave_state: float32 [3, 256, 2048], P(None, 'gx', ('group', 'gy')), may hold values from -6 to 6
- restriction_ops: bfloat16 [1536, 4, 128], replicated, may hold values from -0.15625 to 0.15625
- pair_owner: int32 [16, 256, 4], P(('group', 'gy'), 'gx'), may hold values from 0 to 31, all different within a row; in each aligned block of 8 rows (0 to 7, 8 to 15, ..., all dimensions but the last counted through in order) at most 2 rows name the same one
- pair_slot: int32 [16, 256, 4], P(('group', 'gy'), 'gx'), may hold values from 0 to 7
- pair_weight: int32 [16, 256, 4], P(('group', 'gy'), 'gx'), may hold values from 0 to 3
- tile_mask: int32 [16, 256], P(('group', 'gy'), 'gx'), may hold values 0 or 1
Outputs:
- les_next: float32 [5, 256, 96, 1024], P(None, 'gx', 'group', 'gy')
- wave_next: float32 [3, 256, 2048], P(None, 'gx', ('group', 'gy'))
The draws below stay inside these ranges and needn't reach their ends.
Inputs may be any that keep to these rules, and one draw needn't show every extreme that they name: `les_state`: density and pressure lie in 0.75 to 1.25, the velocities in -0.5 to 0.5. `pair_owner`: each tile names 4 different owners; among the tiles of one device at most 2 pairs name the same owner, and some device reaches 2.
All inputs are finite; a program needn't handle non-finite values. No bound on the sum of `tile_mask` on one device may be relied on, other than what follows from the above.
Results may differ from the reference program's by a relative error of at most 0.00075.
Values may be sent and summed in bfloat16 or wider, within the bound.
A program may use at most 64 MiB of HBM per device.

```python
import math
import jax
import jax.numpy as jnp
import numpy as np
from jax import lax

CX = 8
CZ = 48
CY = 128
AX = 8
AR = 128
K = 4
NW = 4
CAP = 2
TILE_IN = 1536
ROWS = 16
NX = 256
NZ = 96
NY = 1024
NAX = 256
NAR = 2048
N_GROUP = 2
N_GX = 32
N_GY = 8


def draw_les_state(key, part):
    unit_draw = jax.random.uniform(key, (5, NX, NZ, NY), jnp.float32)
    low_end = jnp.array([0.75, -0.5, -0.5, -0.5, 0.75], jnp.float32)[:, None, None, None]
    high_end = jnp.array([1.25, 0.5, 0.5, 0.5, 1.25], jnp.float32)[:, None, None, None]
    return low_end + (high_end - low_end) * unit_draw


def with_ends(entries, key, least, top_value):
    place = [jax.random.randint(jax.random.fold_in(key, axis), (), 0, length) for axis, length in enumerate(entries.shape)]
    main_axis = entries.shape.index(max(entries.shape))
    next_to = place[:main_axis] + [(place[main_axis] + 1) % entries.shape[main_axis]] + place[main_axis + 1:]
    return entries.at[tuple(place)].set(least).at[tuple(next_to)].set(top_value)


def levels(rng, shape, pieces, low, top_value):
    factor_of = 1.0
    for position, parts in pieces:
        steps = jax.random.uniform(jax.random.fold_in(jax.random.fold_in(rng, 6), position), (parts,), jnp.float32, low / len(pieces), top_value / len(pieces))
        factor_of = factor_of * jnp.repeat(jnp.exp(steps), shape[position] // parts).reshape((-1,) + (1,) * (len(shape) - 1 - position))
    return factor_of


def deal_out(stream_key, own, number, rows, count, top, limit, skew):
    sequence = jax.random.permutation(stream_key, count)
    packed, ordinary = portions_of(count, rows * top, limit, skew, True), portions_of(count, rows * top, limit, skew, False)
    places = jnp.arange(count)

    def named(lengths, rotation):
        used = int((lengths > 0).sum())
        fixed = max(1, used // 4)
        passed = fixed + (places - fixed + rotation * (used - fixed)) % max(1, count - fixed)
        return jnp.zeros((count,), jnp.int32).at[sequence[jnp.where(places < fixed, places, passed)]].set(jnp.asarray(lengths, jnp.int32))

    lengths = jnp.where(number % 4 == 0, named(packed, number // 4), named(ordinary, number - number // 4 - 1))
    mixed = jax.random.permutation(jax.random.fold_in(own, 3), count)
    donor, receiver = mixed[0:count // 2 * 2:2], mixed[1:count // 2 * 2:2]
    slack = jnp.minimum(lengths[donor] - 1, limit - lengths[receiver]) // 2
    slack = jnp.where((donor == sequence[0]) | (receiver == sequence[0]) | (lengths[receiver] == 0), 0, jnp.maximum(slack, 0))
    passed = jax.random.randint(jax.random.fold_in(own, 4), (count // 2,), 0, 1 << 20) % (slack + 1)
    lengths = lengths.at[donor].add(-passed).at[receiver].add(passed)
    labels = jnp.searchsorted(jnp.cumsum(lengths), jnp.arange(rows * top), side="right").astype(jnp.int32)
    grid = labels.reshape(top, rows).T
    grid = grid[jax.random.permutation(jax.random.fold_in(own, 1), rows)]
    rotation = jax.random.randint(jax.random.fold_in(own, 2), (rows, 1), 0, top)
    return jnp.take_along_axis(grid, (jnp.arange(top)[None, :] + rotation) % top, axis=1)


def portions_of(count, total, bound, lean, full):
    portions = [(1 << 20) // math.isqrt(rank ** lean) + 1 for rank in range(1, count + 1)]
    largest = bound if full else min(bound, max(-(-total // count), total * portions[0] // sum(portions)))
    least = 1 if total - largest >= count - 1 else 0
    holding, spare = [largest] + [least] * (count - 1), total - largest - least * (count - 1)
    while spare > 0:
        candidates = [i for i in range(1, count) if holding[i] < largest] or [i for i in range(1, count) if holding[i] < bound]
        pool, budget = sum([portions[i] for i in candidates]), spare
        for i in candidates:
            extra = min(bound - holding[i], max(1, budget * portions[i] // pool), spare)
            holding[i] = holding[i] + extra
            spare = spare - extra
    return np.array(holding)


def normal_values(own_key, dims, spread, limit, cuts=(), kind=jnp.bfloat16):
    loudness = levels(own_key, dims, cuts, -0.22, 0.18) if cuts else 1.0
    drawn = jax.random.normal(own_key, dims, jnp.float32) * spread * loudness
    return jnp.minimum(jnp.maximum(drawn, -limit), limit).astype(kind)


def setup_inputs(seed: int = 0) -> dict:
    splits = jax.random.split(jax.random.key(seed), 8)
    les_state = draw_les_state(jax.random.fold_in(splits[7], 71), 0)
    wave_state = normal_values(splits[1], (3, NAX, NAR), 1.0, 6.0, ((1, 32), (2, 16)), jnp.float32)
    restriction_ops = normal_values(splits[2], (TILE_IN, NW, AR), TILE_IN ** -0.5, 0.15625)
    pair_owner_keys = jax.random.split(jax.random.fold_in(splits[3], 1), ROWS * NX // CX)
    pair_owner_turns = jax.random.permutation(jax.random.fold_in(splits[3], 3), ROWS * NX // CX)
    pair_owner = jax.vmap(lambda own, number: deal_out(jax.random.fold_in(splits[3], 2), own, number, CX, N_GX, K, CAP, 2))(pair_owner_keys, pair_owner_turns).reshape((ROWS, NX, K))
    pair_slot = with_ends(jax.random.randint(splits[4], (ROWS, NX, K), 0, AX), jax.random.fold_in(splits[4], 1), 0, AX - 1).astype(jnp.int32)
    pair_weight = with_ends(jax.random.randint(splits[5], (ROWS, NX, K), 0, NW), jax.random.fold_in(splits[5], 1), 0, NW - 1).astype(jnp.int32)
    tile_mask = with_ends((jax.random.randint(splits[6], (ROWS, NX), 0, 4) < 3).astype(jnp.int32), jax.random.fold_in(splits[6], 1), 0, 1)
    return {"les_state": les_state, "wave_state": wave_state, "restriction_ops": restriction_ops, "pair_owner": pair_owner, "pair_slot": pair_slot, "pair_weight": pair_weight, "tile_mask": tile_mask}


GAMMA = 1.4
VISCOSITY = 0.05
LES_STEP = 0.2
WAVE_STEP = 0.3


def window(array_in, offsets, margin):
    picker = tuple(slice(margin + shift_by, array_in.shape[axis_id] - margin + shift_by) for axis_id, shift_by in enumerate(offsets))
    return array_in[picker]


def shifted(dim_count, axis_id, amount):
    return tuple(amount if which_axis == axis_id else 0 for which_axis in range(dim_count))


def central_four(array_in, axis_id):
    dim_count = array_in.ndim
    ahead_one = window(array_in, shifted(dim_count, axis_id, 1), 2)
    behind_one = window(array_in, shifted(dim_count, axis_id, -1), 2)
    ahead_two = window(array_in, shifted(dim_count, axis_id, 2), 2)
    behind_two = window(array_in, shifted(dim_count, axis_id, -2), 2)
    return (8.0 * (ahead_one - behind_one) - (ahead_two - behind_two)) / 12.0


def les_tendency(block_in):
    density = block_in[0]
    velocity = (block_in[1], block_in[2], block_in[3])
    pressure = block_in[4]
    middle = (0, 0, 0)
    centred = [window(component, middle, 2) for component in velocity]
    rho_mid = window(density, middle, 2)
    press_mid = window(pressure, middle, 2)
    divergence = central_four(velocity[0], 0) + central_four(velocity[1], 1) + central_four(velocity[2], 2)

    def advect(quantity):
        return centred[0] * central_four(quantity, 0) + centred[1] * central_four(quantity, 1) + centred[2] * central_four(quantity, 2)

    rate_list = [-advect(density) - rho_mid * divergence]
    for axis_id in range(3):
        component = velocity[axis_id]
        laplace = -6.0 * centred[axis_id]
        for other_axis in range(3):
            laplace = laplace + window(component, shifted(3, other_axis, 1), 2) + window(component, shifted(3, other_axis, -1), 2)
        rate_list.append(-advect(component) - central_four(pressure, axis_id) / rho_mid + VISCOSITY * laplace)
    rate_list.append(-advect(pressure) - GAMMA * press_mid * divergence)
    return jnp.stack(rate_list)


def lighthill(block_in):
    density = block_in[0]
    velocity = (block_in[1], block_in[2], block_in[3])
    summed = jnp.zeros(window(density, (0, 0, 0), 2).shape, jnp.float32)
    for row_axis in range(3):
        for col_axis in range(row_axis, 3):
            stress = density * velocity[row_axis] * velocity[col_axis]
            if row_axis == col_axis:
                piece_term = (window(stress, shifted(3, row_axis, 2), 2) - 2.0 * window(stress, (0, 0, 0), 2) + window(stress, shifted(3, row_axis, -2), 2)) / 4.0
            else:
                both_up = tuple(a + b for a, b in zip(shifted(3, row_axis, 1), shifted(3, col_axis, 1)))
                up_down = tuple(a + b for a, b in zip(shifted(3, row_axis, 1), shifted(3, col_axis, -1)))
                down_up = tuple(a + b for a, b in zip(shifted(3, row_axis, -1), shifted(3, col_axis, 1)))
                both_down = tuple(a + b for a, b in zip(shifted(3, row_axis, -1), shifted(3, col_axis, -1)))
                piece_term = 2.0 * (window(stress, both_up, 2) - window(stress, up_down, 2) - window(stress, down_up, 2) + window(stress, both_down, 2)) / 4.0
            summed = summed + piece_term
    return summed


def wave_tendency(block_in, wave_source, radius):
    pressure = block_in[0]
    axial = block_in[1]
    radial = block_in[2]
    radial_mid = window(radial, (0, 0), 2)
    press_rate = wave_source - central_four(axial, 0) - central_four(radial, 1) - radial_mid / radius[None, :]
    return jnp.stack([press_rate, -central_four(pressure, 0), -central_four(pressure, 1)])


def reference(les_state, wave_state, restriction_ops, pair_owner, pair_slot, pair_weight, tile_mask):
    wrap_pad = ((0, 0), (2, 2), (2, 2), (2, 2))
    padded = jnp.pad(les_state, wrap_pad, mode="wrap")
    first_rate = les_tendency(padded)
    predictor = les_state + LES_STEP * first_rate
    pad_pred = jnp.pad(predictor, wrap_pad, mode="wrap")
    second_rate = les_tendency(pad_pred)
    les_next = les_state + (0.5 * LES_STEP) * (first_rate + second_rate)
    source = lighthill(pad_pred)
    halved = source.reshape(NX, NZ // 2, 2, NY).sum(axis=2)
    halved = halved.reshape(NX, NZ // 2, NY // 2, 2).sum(axis=3)
    tiles_grid = halved.reshape(NX, N_GROUP, CZ // 2, N_GY, CY // 2).transpose(1, 3, 0, 2, 4).reshape(ROWS, NX, TILE_IN)
    tile_rows = (tiles_grid * tile_mask.astype(jnp.float32)[:, :, None]).astype(jnp.bfloat16)
    products = jnp.dot(tile_rows.reshape(ROWS * NX, TILE_IN), restriction_ops.reshape(TILE_IN, NW * AR), preferred_element_type=jnp.float32).reshape(ROWS, NX, NW, AR)
    pick_op = (pair_weight[..., None] == jnp.arange(NW).astype(jnp.int32)).astype(jnp.float32)
    pair_values = jnp.einsum("rxkw,rxwa->rxka", pick_op, products, precision=lax.Precision.HIGHEST)
    line_id = (pair_owner * AX + pair_slot).astype(jnp.int32)
    row_id = jnp.broadcast_to(jnp.arange(ROWS).astype(jnp.int32)[:, None, None], line_id.shape)
    source_grid = jnp.zeros((NAX, ROWS, AR), jnp.float32).at[line_id, row_id].add(pair_values)
    wave_source = source_grid.reshape(NAX, NAR)
    radius = jnp.arange(NAR).astype(jnp.float32) + 0.5
    zero_pad = ((0, 0), (2, 2), (2, 2))
    current = wave_state
    for step_id in range(2):
        first_wave = wave_tendency(jnp.pad(current, zero_pad), wave_source, radius)
        second_wave = wave_tendency(jnp.pad(current + WAVE_STEP * first_wave, zero_pad), wave_source, radius)
        current = current + (0.5 * WAVE_STEP) * (first_wave + second_wave)
    return les_next, current
```

```python
import functools

import jax
import jax.numpy as jnp
from jax import lax
from jax.experimental import pallas as pl
from jax.experimental.pallas import tpu as pltpu
from jax.sharding import PartitionSpec as P

MESH = pl.DeviceIdType.MESH
VISCOSITY = 0.05
LES_STEP = 0.2
WAVE_STEP = 0.3
CX, CZ, CY = 8, 48, 128
ZT = CZ // 8
OFFSETS = (1.0, 0.0, 0.0, 0.0, 1.0)
STATE_SCALE = (130816.0, 65408.0, 65408.0, 65408.0, 130816.0)
PRED_SCALE = (24576.0,) * 5


def encode(value, offset, scale):
    return ((value - offset) * scale + 32768.5).astype(jnp.int32)


def decode(code, offset, scale):
    return code.astype(jnp.float32) * (1.0 / scale) + (offset - 32768.0 / scale)


def pair_words(first, second, offset, scale):
    return (encode(first, offset, scale) << 16) | encode(second, offset, scale)


def split_words(words, offset, scale):
    first = decode(lax.shift_right_logical(words, 16), offset, scale)
    return first, decode(words & 0xFFFF, offset, scale)


def lanes():
    return lax.broadcasted_iota(jnp.int32, (8, 128), 1)


def rows():
    return lax.broadcasted_iota(jnp.int32, (8, 128), 0)


def roll_lane(tile, shift):
    shift = shift % tile.shape[1]
    return pltpu.roll(tile, shift, 1) if shift else tile


def roll_row(tile, shift):
    shift = shift % tile.shape[0]
    return pltpu.roll(tile, shift, 0) if shift else tile


def y_shifts(tile, low, high, slot, reach):
    lane = lanes()
    low, high = roll_lane(low, 126 - 2 * slot), roll_lane(high, -2 * slot)
    shifts = []
    for s in reach:
        before = roll_lane(jnp.where(lane >= 128 - s, low, tile), s)
        after = roll_lane(jnp.where(lane < s, high, tile), -s)
        shifts.append((before, after))
    return shifts


def rate_tile(buf, x, zt, low, high):
    base = 8 + 8 * zt

    def at(f, dx, dz):
        return buf[f, x + (2 + dx), pl.ds(base + dz, 8), :]

    centre, grads, laps = [], [], []
    for f in range(5):
        c = at(f, 0, 0)
        xm1, xp1, zm1, zp1 = at(f, -1, 0), at(f, 1, 0), at(f, 0, -1), at(f, 0, 1)
        (ym1, yp1), (ym2, yp2) = y_shifts(c, low, high, f * ZT + zt, (1, 2))
        dx = 8.0 * (xp1 - xm1) - (at(f, 2, 0) - at(f, -2, 0))
        dz = 8.0 * (zp1 - zm1) - (at(f, 0, 2) - at(f, 0, -2))
        dy = 8.0 * (yp1 - ym1) - (yp2 - ym2)
        centre.append(c)
        grads.append((dx, dz, dy))
        laps.append(((xm1 + xp1) + (zm1 + zp1)) + (ym1 + yp1) - 6.0 * c if 1 <= f <= 3 else None)
    rho, u0, u1, u2, p = centre
    div = grads[1][0] + grads[2][1] + grads[3][2]
    inverse = 1.0 / rho

    def advect(f):
        return u0 * grads[f][0] + u1 * grads[f][1] + u2 * grads[f][2]

    twelfth = -1.0 / 12.0
    rates = [(advect(0) + rho * div) * twelfth]
    for d in range(3):
        rates.append((advect(1 + d) + grads[4][d] * inverse) * twelfth + VISCOSITY * laps[1 + d])
    rates.append((advect(4) + 1.4 * (p * div)) * twelfth)
    return centre, rates


def packed_products(tile):
    momentum = tile * roll_lane(tile, -36)
    return (
        momentum * roll_lane(tile, -12),
        momentum * roll_lane(tile, -24),
        momentum * roll_lane(tile, -36),
    )


def wave_rates(state, source, inverse_radius):
    p, ux, ur = state

    def d(f, axis):
        size = f.shape[axis]
        one = pltpu.roll(f, size - 1, axis) - pltpu.roll(f, 1, axis)
        two = pltpu.roll(f, size - 2, axis) - pltpu.roll(f, 2, axis)
        return (8.0 * one - two) * (1.0 / 12.0)

    return (source - d(ux, 0) - d(ur, 1) - ur * inverse_radius, -d(p, 0), -d(p, 1))


def kernel(
    sizes, far_order,
    les_ref, wave_ref, ops_ref, owner_ref, slot_ref, weight_ref, mask_ref,
    les_out, wave_out,
    state, pred, base_sum, s00, s11, s22, s01, s02, s12,
    xs1, xr1, xs2, xr2, zs1, zr1, zs2, zr2, ys1, yr1, ys2, yr2,
    exz_s, exz_r, ezy_s, ezy_r, ezy_x,
    light, ops_raw, ops_wide, ops_mat, spread, weight_tiles,
    sent, received, own_source, near_source, near_wave,
    local_sems, send1, recv1, send2, recv2, wave_send, wave_recv, all_send, all_recv, src_send, src_recv, gossip,
):
    n_group, n_gx, n_gy = sizes
    g, gx, gy = lax.axis_index("group"), lax.axis_index("gx"), lax.axis_index("gy")
    rank = g * n_gy + gy
    n_rank = n_group * n_gy
    gx_low, gx_high = lax.rem(gx + (n_gx - 1), n_gx), lax.rem(gx + 1, n_gx)
    gy_low, gy_high = lax.rem(gy + (n_gy - 1), n_gy), lax.rem(gy + 1, n_gy)
    other = 1 - g
    lane, row = lanes(), rows()

    def remote(src, dst, send_sem, recv_sem, device):
        return pltpu.make_async_remote_copy(
            src_ref=src, dst_ref=dst, send_sem=send_sem, recv_sem=recv_sem, device_id=device, device_id_type=MESH
        )

    barrier = pltpu.get_barrier_semaphore()
    for device in ((g, gx_low, gy), (g, gx_high, gy), (other, gx, gy), (g, gx, gy_low), (g, gx, gy_high)):
        pl.semaphore_signal(barrier, inc=1, device_id=device, device_id_type=MESH)

    load_les = pltpu.make_async_copy(les_ref, state.at[:, 2:10, 8:56, :], local_sems.at[0])
    load_les.start()
    load_ops = pltpu.make_async_copy(ops_ref, ops_raw, local_sems.at[1])
    load_ops.start()
    load_les.wait()

    def gossip_send(r):
        if r < gossip.shape[0]:
            d = 1 << r
            for target in (lax.rem(gx + d, n_gx), lax.rem(gx + (n_gx - d), n_gx)):
                pl.semaphore_signal(gossip.at[r], inc=1, device_id=(g, target, gy), device_id_type=MESH)

    def gossip_wait(r):
        if r < gossip.shape[0]:
            pl.semaphore_wait(gossip.at[r], 2)

    def x_pack(buf, out, scales, layer):
        for f in range(5):
            for side, first in ((0, 2), (1, 8)):
                out[side, f] = pair_words(
                    buf[f, first, 8:56, :], buf[f, first + 1, 8:56, :], OFFSETS[f], scales[f]
                )

    def x_unpack(buf, words, scales):
        for f in range(5):
            for side, first in ((0, 0), (1, 10)):
                one, two = split_words(words[side, f], OFFSETS[f], scales[f])
                buf[f, first, 8:56, :] = one
                buf[f, first + 1, 8:56, :] = two

    def ends(buf, f, x):
        return jnp.where(row < 4, buf[f, x + 2, 8:16, :], buf[f, x + 2, 48:56, :])

    def z_pack(buf, out, scales):
        for f in range(5):
            for j in range(2):
                a = pair_words(ends(buf, f, 2 * j), ends(buf, f, 2 * j + 4), OFFSETS[f], scales[f])
                b = pair_words(ends(buf, f, 2 * j + 1), ends(buf, f, 2 * j + 5), OFFSETS[f], scales[f])
                out[2 * f + j] = jnp.where((row < 2) | (row >= 6), a, roll_row(b, 4))

    def z_unpack(buf, words, scales):
        for f in range(5):
            for j in range(2):
                word = words[2 * f + j]
                for i, part in enumerate((word, roll_row(word, 4))):
                    for x, tile in zip((2 * j + i, 2 * j + i + 4), split_words(part, OFFSETS[f], scales[f])):
                        buf[f, x + 2, 0:8, :] = tile
                        buf[f, x + 2, 56:64, :] = tile

    def y_add(packed, tile, slot):
        here = (lane >> 1) == slot
        return (
            jnp.where(here, roll_lane(tile, 2 * slot), packed[0]),
            jnp.where(here, roll_lane(tile, 2 * slot + 2), packed[1]),
        )

    def y_pack(x, carry):
        packed = (jnp.zeros((8, 128), jnp.float32),) * 2
        for f in range(5):
            for zt in range(ZT):
                packed = y_add(packed, state[f, x + 2, pl.ds(8 + 8 * zt, 8), :], f * ZT + zt)
        ys1[0, x] = packed[0]
        ys1[1, x] = packed[1]
        return carry

    x_pack(state, xs1, STATE_SCALE, 0)
    pl.semaphore_wait(barrier, 5)
    gossip_send(0)
    first = [
        remote(xs1.at[0], xr1.at[1], send1.at[0], recv1.at[1], (g, gx_low, gy)),
        remote(xs1.at[1], xr1.at[0], send1.at[1], recv1.at[0], (g, gx_high, gy)),
        remote(zs1, zr1, send1.at[2], recv1.at[2], (other, gx, gy)),
        remote(ys1.at[0], yr1.at[1], send1.at[3], recv1.at[4], (g, gx, gy_low)),
        remote(ys1.at[1], yr1.at[0], send1.at[4], recv1.at[3], (g, gx, gy_high)),
    ]
    first[0].start()
    first[1].start()
    z_pack(state, zs1, STATE_SCALE)
    first[2].start()
    lax.fori_loop(0, CX, y_pack, 0)
    first[3].start()
    first[4].start()

    load_ops.wait()

    def widen(i, carry):
        part = pl.ds(pl.multiple_of(i * 512, 512), 512)
        ops_wide[...] = ops_raw[part, :].astype(jnp.float32)
        for w in range(4):
            ops_mat[pl.ds(pl.multiple_of(i * 128, 128), 128), w * 128:(w + 1) * 128] = (
                ops_wide[pl.ds(w, 128, stride=4), :].astype(jnp.bfloat16)
            )
        return carry

    lax.fori_loop(0, 12, widen, 0)
    target = jnp.full((8, 128), -1, jnp.int32)
    for k in range(4):
        weights = jnp.zeros((8, 128), jnp.int32)
        for x in range(8):
            line = owner_ref[0, k, x] * 8 + slot_ref[0, k, x]
            target = jnp.where(((lane & 31) == k * 8 + x) & (lane < 96), line, target)
            weights = jnp.where(row == x, weight_ref[0, k, x], weights)
        weight_tiles[k] = weights
    for o in range(n_gx):
        spread[o * 8:(o + 1) * 8, :] = jnp.where(target == row + o * 8, 1.0, 0.0)

    gossip_wait(0)
    gossip_send(1)
    first[2].wait_recv()
    z_unpack(state, zr1, STATE_SCALE)
    first[3].wait_recv()
    first[4].wait_recv()

    def first_rate(x, carry):
        low, high = yr1[0, x], yr1[1, x]
        packed = (jnp.zeros((8, 128), jnp.float32),) * 2
        for zt in range(ZT):
            centre, rates = rate_tile(state, x, zt, low, high)
            part = pl.ds(8 * zt, 8)
            inner = pl.ds(8 + 8 * zt, 8)
            new = []
            for f in range(5):
                value = centre[f] + LES_STEP * rates[f]
                pred[f, x + 2, inner, :] = value
                base_sum[f, x, part, :] = centre[f] + (0.5 * LES_STEP) * rates[f]
                packed = y_add(packed, value, f * ZT + zt)
                new.append(value)
            rho, u0, u1, u2, _ = new
            m0, m1 = rho * u0, rho * u1
            s00[x + 2, part, :] = m0 * u0
            s01[x + 1, inner, :] = m0 * u1
            s02[x + 1, part, :] = m0 * u2
            s11[x, inner, :] = m1 * u1
            s12[x, inner, :] = m1 * u2
            s22[x, part, :] = rho * u2 * u2
        ys2[0, x] = packed[0]
        ys2[1, x] = packed[1]
        return carry

    lax.fori_loop(2, 6, first_rate, 0)
    gossip_wait(1)
    gossip_send(2)
    first[0].wait_recv()
    first[1].wait_recv()
    x_unpack(state, xr1, STATE_SCALE)
    lax.fori_loop(0, 4, lambda j, carry: first_rate(lax.rem(j + 6, 8), carry), 0)

    x_pack(pred, xs2, PRED_SCALE, 0)
    second = [
        remote(xs2.at[0], xr2.at[1], send2.at[0], recv2.at[1], (g, gx_low, gy)),
        remote(xs2.at[1], xr2.at[0], send2.at[1], recv2.at[0], (g, gx_high, gy)),
        remote(zs2, zr2, send2.at[2], recv2.at[2], (other, gx, gy)),
        remote(ys2.at[0], yr2.at[1, 1:9], send2.at[3], recv2.at[4], (g, gx, gy_low)),
        remote(ys2.at[1], yr2.at[0, 1:9], send2.at[4], recv2.at[3], (g, gx, gy_high)),
        remote(ezy_s.at[0], ezy_r.at[1], send2.at[5], recv2.at[6], (other, gx, gy_low)),
        remote(ezy_s.at[1], ezy_r.at[0], send2.at[6], recv2.at[5], (other, gx, gy_high)),
        remote(exz_s.at[0], exz_r.at[1], send2.at[7], recv2.at[8], (other, gx_low, gy)),
        remote(exz_s.at[1], exz_r.at[0], send2.at[8], recv2.at[7], (other, gx_high, gy)),
        remote(ys2.at[0, 0], yr2.at[1, 9], send2.at[9], recv2.at[12], (g, gx_low, gy_low)),
        remote(ys2.at[1, 0], yr2.at[0, 9], send2.at[10], recv2.at[11], (g, gx_low, gy_high)),
        remote(ys2.at[0, 7], yr2.at[1, 0], send2.at[11], recv2.at[10], (g, gx_high, gy_low)),
        remote(ys2.at[1, 7], yr2.at[0, 0], send2.at[12], recv2.at[9], (g, gx_high, gy_high)),
    ]
    second[0].start()
    second[1].start()
    z_pack(pred, zs2, PRED_SCALE)
    second[2].start()
    second[3].start()
    second[4].start()
    for side in range(2):
        x = 7 * side
        exz_s[side] = ends(pred, 0, x) * ends(pred, 1, x) * ends(pred, 2, x)
        edge = jnp.zeros((8, 128), jnp.float32)
        for x in range(8):
            here = (lane >= 12 * x) & (lane < 12 * x + 12)
            edge = jnp.where(here, roll_lane(packed_products(ys2[side, x])[1], 12 * x), edge)
        ezy_s[side] = edge
    for copy in second[5:]:
        copy.start()
    gossip_wait(2)
    gossip_send(3)

    second[2].wait_recv()
    z_unpack(pred, zr2, PRED_SCALE)
    for x in range(8):
        for part in (slice(0, 8), slice(56, 64)):
            rho, u0, u1, u2 = (pred[f, x + 2, part, :] for f in range(4))
            m1 = rho * u1
            s01[x + 1, part, :] = m1 * u0
            s11[x, part, :] = m1 * u1
            s12[x, part, :] = m1 * u2
    for i in (3, 4, 5, 6):
        second[i].wait_recv()
    for side in range(2):
        for x in range(8):
            ezy_x[side, x] = roll_lane(ezy_r[side], -12 * x)

    def lighthill(x, carry):
        cross, square = [], []
        for side in range(2):
            along_x = packed_products(yr2[side, x + 2])[0] - packed_products(yr2[side, x])[0]
            _, s12_halo, s22_halo = packed_products(yr2[side, x + 1])
            corner = ezy_x[side, x]
            next_tile = jnp.where(lane >= 10, roll_lane(corner, 10), roll_lane(s12_halo, -2))
            last_tile = jnp.where(lane < 2, roll_lane(corner, -10), roll_lane(s12_halo, 2))
            after = roll_row(jnp.where(row == 0, next_tile, s12_halo), -1)
            before = roll_row(jnp.where(row == 7, last_tile, s12_halo), 1)
            cross.append(along_x + (after - before))
            square.append(s22_halo)
        keep = mask_ref[0, x].astype(jnp.float32)
        for zt in range(ZT):
            part = pl.ds(8 * zt, 8)

            def z(ref, index, dz):
                return ref[index, pl.ds(8 + 8 * zt + dz, 8), :]

            direct = s00[x + 4, part, :] + s00[x, part, :] - 2.0 * s00[x + 2, part, :]
            direct = direct + (z(s11, x, 2) + z(s11, x, -2) - 2.0 * z(s11, x, 0))
            tile = s22[x, part, :]
            ((before, after),) = y_shifts(tile, square[0], square[1], zt, (2,))
            direct = direct + (before + after - 2.0 * tile)
            mixed = (z(s01, x + 2, 1) - z(s01, x + 2, -1)) - (z(s01, x, 1) - z(s01, x, -1))
            tile = (s02[x + 2, part, :] - s02[x, part, :]) + (z(s12, x, 1) - z(s12, x, -1))
            ((before, after),) = y_shifts(tile, cross[0], cross[1], zt, (1,))
            mixed = mixed + (after - before)
            light[pl.ds(pl.multiple_of(x * CZ + 8 * zt, 8), 8), :] = (0.25 * direct + 0.5 * mixed) * keep
        return carry

    lax.fori_loop(2, 6, lighthill, 0)
    second[0].wait_recv()
    second[1].wait_recv()
    x_unpack(pred, xr2, PRED_SCALE)
    for index in (0, 1, 10, 11):
        s00[index] = pred[0, index, 8:56, :] * pred[1, index, 8:56, :] * pred[1, index, 8:56, :]
    for index, layer in ((0, 1), (9, 10)):
        m0 = pred[0, layer, 8:56, :] * pred[1, layer, 8:56, :]
        s01[index, 8:56, :] = m0 * pred[2, layer, 8:56, :]
        s02[index] = m0 * pred[3, layer, 8:56, :]
    for i in range(7, 13):
        second[i].wait_recv()
    for side, index in ((0, 0), (1, 9)):
        s01[index, 0:8, :] = exz_r[side]
        s01[index, 56:64, :] = exz_r[side]
    lax.fori_loop(0, 4, lambda j, carry: lighthill(lax.rem(j + 6, 8), carry), 0)

    pieces = []
    for zp in range(12):
        one, two = (
            light[pl.ds(4 * zp + 2 * i, 8, stride=CZ), :] + light[pl.ds(4 * zp + 2 * i + 1, 8, stride=CZ), :]
            for i in range(2)
        )
        one = one + roll_lane(one, -1)
        two = two + roll_lane(two, 1)
        pieces.append(jnp.where((lane & 1) == 0, one, two))
    merged = jnp.concatenate(pieces, axis=0).astype(jnp.bfloat16)
    source_lane = lax.broadcasted_iota(jnp.int32, (128, 128), 0)
    target_lane = lax.broadcasted_iota(jnp.int32, (128, 128), 1)
    order = jnp.where(target_lane == (source_lane & 1) * 64 + (source_lane >> 1), 1.0, 0.0).astype(jnp.bfloat16)
    sorted_rows = jnp.dot(merged, order, preferred_element_type=jnp.float32)
    tile_rows = jnp.concatenate([sorted_rows[8 * i:8 * i + 8, :] for i in range(12)], axis=1).astype(jnp.bfloat16)
    products = jnp.dot(tile_rows, ops_mat[...], preferred_element_type=jnp.float32)
    pairs = []
    for k in range(4):
        chosen = jnp.zeros((8, 128), jnp.float32)
        for w in range(4):
            chosen = jnp.where(weight_tiles[k] == w, products[:, w * 128:(w + 1) * 128], chosen)
        pairs.append(chosen)
    values = jnp.concatenate(pairs, axis=0)
    high = values.astype(jnp.bfloat16).astype(jnp.float32)
    middle = (values - high).astype(jnp.bfloat16).astype(jnp.float32)
    rest = values - high - middle
    stacked = jnp.concatenate([high, middle, rest, jnp.zeros((32, 128), jnp.float32)], axis=0).astype(jnp.bfloat16)
    sent[...] = jnp.dot(spread[...].astype(jnp.bfloat16), stacked, preferred_element_type=jnp.float32)

    gossip_wait(3)
    all_copies = []
    for d in far_order:
        owner = lax.rem(gx + d, n_gx)
        copy = remote(
            sent.at[pl.ds(pl.multiple_of(owner * 8, 8), 8), :], received.at[gx],
            all_send.at[0], all_recv.at[0], (g, owner, gy),
        )
        copy.start()
    received[gx] = sent[pl.ds(pl.multiple_of(gx * 8, 8), 8), :]

    around = [(dx, dr) for dx in (-1, 0, 1) for dr in (-1, 0, 1) if (dx, dr) != (0, 0)]

    def neighbour(dx, dr):
        there = lax.rem(rank + (n_rank + dr), n_rank)
        return (there // n_gy, lax.rem(gx + (n_gx + dx), n_gx), lax.rem(there, n_gy))

    def slot_of(dx, dr):
        return around.index((dx, dr))

    for dx, dr in around:
        remote(
            wave_ref, near_wave.at[slot_of(-dx, -dr)], wave_send.at[0], wave_recv.at[0], neighbour(dx, dr)
        ).start()

    def second_rate(x, carry):
        low, high = yr2[0, x + 1], yr2[1, x + 1]
        for zt in range(ZT):
            _, rates = rate_tile(pred, x, zt, low, high)
            part = pl.ds(8 * zt, 8)
            for f in range(5):
                base_sum[f, x, part, :] = base_sum[f, x, part, :] + (0.5 * LES_STEP) * rates[f]
        return carry

    lax.fori_loop(0, CX, second_rate, 0)
    store_les = pltpu.make_async_copy(base_sum, les_out, local_sems.at[2])
    store_les.start()

    others = received.at[0:n_gx - 1]
    pltpu.make_async_copy(others, others, all_recv.at[0]).wait()
    own_source[...] = jnp.sum(received[...], axis=0)
    for dx, dr in around:
        remote(
            own_source, near_source.at[slot_of(-dx, -dr)], src_send.at[0], src_recv.at[0], neighbour(dx, dr)
        ).start()

    pltpu.make_async_copy(near_wave, near_wave, wave_recv.at[0]).wait()
    wide_row = lax.broadcasted_iota(jnp.int32, (24, 256), 0)
    wide_lane = lax.broadcasted_iota(jnp.int32, (24, 256), 1)

    def flag(yes):
        return yes.astype(jnp.int32).astype(jnp.float32)

    inside = jnp.where(wide_row < 8, flag(gx > 0), jnp.where(wide_row >= 16, flag(gx < n_gx - 1), 1.0))
    inside = inside * jnp.where(
        wide_lane < 128, 1.0, jnp.where(wide_lane < 192, flag(rank < n_rank - 1), flag(rank > 0))
    )
    column = jnp.where(wide_lane < 192, wide_lane, wide_lane - 256) + rank * 128
    inverse_radius = 1.0 / (column.astype(jnp.float32) + 0.5)

    def assemble(block):
        strips = []
        for dx in (-1, 0, 1):
            side = jnp.where(lane < 64, block(dx, 1), block(dx, -1))
            strips.append(jnp.concatenate([block(dx, 0), side], axis=1))
        return jnp.concatenate(strips, axis=0) * inside

    def wave_block(f):
        return lambda dx, dr: wave_ref[f] if (dx, dr) == (0, 0) else near_wave[slot_of(dx, dr), f]

    now = [assemble(wave_block(f)) for f in range(3)]
    pltpu.make_async_copy(near_source, near_source, src_recv.at[0]).wait()
    source = assemble(lambda dx, dr: own_source[...] if (dx, dr) == (0, 0) else near_source[slot_of(dx, dr)])
    for _ in range(2):
        rate_one = wave_rates(now, source, inverse_radius)
        ahead = [(v + WAVE_STEP * r) * inside for v, r in zip(now, rate_one)]
        rate_two = wave_rates(ahead, source, inverse_radius)
        now = [(v + (0.5 * WAVE_STEP) * (a + b)) * inside for v, a, b in zip(now, rate_one, rate_two)]
    for f in range(3):
        wave_out[f] = now[f][8:16, 0:128]

    for copy in first + second:
        copy.wait_send()
    pltpu.make_async_copy(others, others, all_send.at[0]).wait()
    pltpu.make_async_copy(near_wave, near_wave, wave_send.at[0]).wait()
    pltpu.make_async_copy(near_source, near_source, src_send.at[0]).wait()
    store_les.wait()


def on_device(sizes, les_state, wave_state, restriction_ops, pair_owner, pair_slot, pair_weight, tile_mask):
    n_gx = sizes[1]
    tile_len, op_count, width = restriction_ops.shape
    ops_flat = restriction_ops.reshape(tile_len * op_count, width)
    rounds = max(1, (n_gx // 2).bit_length() - 1)
    far_order = sorted(range(1, n_gx), key=lambda d: -(2 * min(d // 8, 4 - d // 8) + min(d % 8, 8 - d % 8)))
    f32, i32, bf16 = jnp.float32, jnp.int32, jnp.bfloat16
    vmem, dma = pltpu.VMEM, pltpu.SemaphoreType.DMA
    scratch = [
        vmem((5, 12, 64, 128), f32), vmem((5, 12, 64, 128), f32), vmem((5, 8, 48, 128), f32),
        vmem((12, 48, 128), f32), vmem((8, 64, 128), f32), vmem((8, 48, 128), f32),
        vmem((10, 64, 128), f32), vmem((10, 48, 128), f32), vmem((8, 64, 128), f32),
        vmem((2, 5, 48, 128), i32), vmem((2, 5, 48, 128), i32), vmem((2, 5, 48, 128), i32), vmem((2, 5, 48, 128), i32),
        vmem((10, 8, 128), i32), vmem((10, 8, 128), i32), vmem((10, 8, 128), i32), vmem((10, 8, 128), i32),
        vmem((2, 8, 8, 128), f32), vmem((2, 8, 8, 128), f32), vmem((2, 8, 8, 128), f32), vmem((2, 10, 8, 128), f32),
        vmem((2, 8, 128), f32), vmem((2, 8, 128), f32), vmem((2, 8, 128), f32), vmem((2, 8, 128), f32),
        vmem((2, 8, 8, 128), f32),
        vmem((CX * CZ, 128), f32), vmem((6144, 128), bf16), vmem((512, 128), f32), vmem((1536, 512), bf16),
        vmem((n_gx * 8, 128), f32), vmem((4, 8, 128), i32),
        vmem((n_gx * 8, 128), f32), vmem((n_gx, 8, 128), f32), vmem((8, 128), f32),
        vmem((8, 8, 128), f32), vmem((8, 3, 8, 128), f32),
        dma((3,)), dma((5,)), dma((5,)), dma((13,)), dma((13,)), dma((1,)), dma((1,)), dma((1,)), dma((1,)),
        dma((1,)), dma((1,)), pltpu.SemaphoreType.REGULAR((rounds,)),
    ]
    any_space = pl.BlockSpec(memory_space=pl.ANY)
    in_vmem = pl.BlockSpec(memory_space=pltpu.VMEM)
    in_smem = pl.BlockSpec(memory_space=pltpu.SMEM)
    return pl.pallas_call(
        functools.partial(kernel, sizes, far_order),
        out_shape=(
            jax.ShapeDtypeStruct(les_state.shape, f32),
            jax.ShapeDtypeStruct(wave_state.shape, f32),
        ),
        in_specs=[any_space, in_vmem, any_space, in_smem, in_smem, in_smem, in_smem],
        out_specs=(any_space, in_vmem),
        scratch_shapes=scratch,
        compiler_params=pltpu.CompilerParams(collective_id=0, has_side_effects=True),
        name="jet_step",
    )(les_state, wave_state, ops_flat, *(a.swapaxes(1, 2) for a in (pair_owner, pair_slot, pair_weight)), tile_mask)


def solution(mesh):
    sizes = (mesh.shape["group"], mesh.shape["gx"], mesh.shape["gy"])
    return jax.shard_map(
        functools.partial(on_device, sizes),
        mesh=mesh,
        in_specs=(
            P(None, "gx", "group", "gy"),
            P(None, "gx", ("group", "gy")),
            P(),
            P(("group", "gy"), "gx", None),
            P(("group", "gy"), "gx", None),
            P(("group", "gy"), "gx", None),
            P(("group", "gy"), "gx"),
        ),
        out_specs=(P(None, "gx", "group", "gy"), P(None, "gx", ("group", "gy"))),
        check_vma=False,
    )
```

```python
import functools

import jax
import jax.numpy as jnp
from jax import lax
from jax.experimental import pallas as pl
from jax.experimental.pallas import tpu as pltpu
from jax.sharding import PartitionSpec as P

MESH = pl.DeviceIdType.MESH
VISCOSITY = 0.05
LES_STEP = 0.2
WAVE_STEP = 0.3
CX, CZ, CY = 8, 48, 128
ZT = CZ // 8
OFFSETS = (1.0, 0.0, 0.0, 0.0, 1.0)
STATE_SCALE = (130816.0, 65408.0, 65408.0, 65408.0, 130816.0)
PRED_SCALE = (24576.0,) * 5


def encode(value, offset, scale):
    return ((value - offset) * scale + 32768.5).astype(jnp.int32)


def decode(code, offset, scale):
    return code.astype(jnp.float32) * (1.0 / scale) + (offset - 32768.0 / scale)


def pair_words(first, second, offset, scale):
    return (encode(first, offset, scale) << 16) | encode(second, offset, scale)


def split_words(words, offset, scale):
    first = decode(lax.shift_right_logical(words, 16), offset, scale)
    return first, decode(words & 0xFFFF, offset, scale)


def lanes():
    return lax.broadcasted_iota(jnp.int32, (8, 128), 1)


def rows():
    return lax.broadcasted_iota(jnp.int32, (8, 128), 0)


def roll_lane(tile, shift):
    shift = shift % tile.shape[1]
    return pltpu.roll(tile, shift, 1) if shift else tile


def roll_row(tile, shift):
    shift = shift % tile.shape[0]
    return pltpu.roll(tile, shift, 0) if shift else tile


def y_shifts(tile, halo, slot, reach):
    lane = lanes()
    halo = roll_lane(halo, -(4 * slot + 2))
    shifts = []
    for s in reach:
        before = roll_lane(jnp.where(lane >= 128 - s, halo, tile), s)
        after = roll_lane(jnp.where(lane < s, halo, tile), -s)
        shifts.append((before, after))
    return shifts


def rate_tile(buf, x, zt, halo):
    base = 8 + 8 * zt

    def at(f, dx, dz):
        return buf[f, x + (2 + dx), pl.ds(base + dz, 8), :]

    centre, grads, laps = [], [], []
    for f in range(5):
        c = at(f, 0, 0)
        xm1, xp1, zm1, zp1 = at(f, -1, 0), at(f, 1, 0), at(f, 0, -1), at(f, 0, 1)
        (ym1, yp1), (ym2, yp2) = y_shifts(c, halo, f * ZT + zt, (1, 2))
        dx = 8.0 * (xp1 - xm1) - (at(f, 2, 0) - at(f, -2, 0))
        dz = 8.0 * (zp1 - zm1) - (at(f, 0, 2) - at(f, 0, -2))
        dy = 8.0 * (yp1 - ym1) - (yp2 - ym2)
        centre.append(c)
        grads.append((dx, dz, dy))
        laps.append(((xm1 + xp1) + (zm1 + zp1)) + (ym1 + yp1) - 6.0 * c if 1 <= f <= 3 else None)
    rho, u0, u1, u2, p = centre
    div = grads[1][0] + grads[2][1] + grads[3][2]
    inverse = 1.0 / rho

    def advect(f):
        return u0 * grads[f][0] + u1 * grads[f][1] + u2 * grads[f][2]

    twelfth = -1.0 / 12.0
    rates = [(advect(0) + rho * div) * twelfth]
    for d in range(3):
        rates.append((advect(1 + d) + grads[4][d] * inverse) * twelfth + VISCOSITY * laps[1 + d])
    rates.append((advect(4) + 1.4 * (p * div)) * twelfth)
    return centre, rates


def packed_products(tile):
    momentum = tile * roll_lane(tile, -72)
    return (
        momentum * roll_lane(tile, -24),
        momentum * roll_lane(tile, -48),
        momentum * roll_lane(tile, -72),
    )


def wave_rates(state, source, inverse_radius):
    p, ux, ur = state

    def d(f, axis):
        size = f.shape[axis]
        one = pltpu.roll(f, size - 1, axis) - pltpu.roll(f, 1, axis)
        two = pltpu.roll(f, size - 2, axis) - pltpu.roll(f, 2, axis)
        return (8.0 * one - two) * (1.0 / 12.0)

    return (source - d(ux, 0) - d(ur, 1) - ur * inverse_radius, -d(p, 0), -d(p, 1))


def kernel(
    sizes, far_order,
    les_ref, wave_in, ops_ref, owner_in, slot_in, weight_in, mask_in,
    les_out, wave_out,
    state, pred, base_sum, s00, s11, s22, s01, s02, s12,
    wave_ref, owner_ref, slot_ref, weight_ref, mask_ref,
    xs1, xr1, xs2, xr2, zs1, zr1, zs2, zr2, ys1, yr1, ys2, yr2, ym2,
    exz_s, exz_r, ezy_s, ezy_r, ezy_x,
    light, ops_raw, ops_wide, ops_mat, spread, weight_tiles,
    sent, received, own_source, near_source, near_wave,
    local_sems, x_send, x_recv, send1, recv1, send2, recv2, wave_send, wave_recv, all_send, all_recv, src_send, src_recv, gossip,
):
    n_group, n_gx, n_gy = sizes
    g, gx, gy = lax.axis_index("group"), lax.axis_index("gx"), lax.axis_index("gy")
    rank = g * n_gy + gy
    n_rank = n_group * n_gy
    gx_low, gx_high = lax.rem(gx + (n_gx - 1), n_gx), lax.rem(gx + 1, n_gx)
    gy_low, gy_high = lax.rem(gy + (n_gy - 1), n_gy), lax.rem(gy + 1, n_gy)
    other = 1 - g
    lane, row = lanes(), rows()

    def remote(src, dst, send_sem, recv_sem, device):
        return pltpu.make_async_remote_copy(
            src_ref=src, dst_ref=dst, send_sem=send_sem, recv_sem=recv_sem, device_id=device, device_id_type=MESH
        )

    barrier = pltpu.get_barrier_semaphore()
    for device in ((g, gx_low, gy), (g, gx_high, gy), (other, gx, gy), (g, gx, gy_low), (g, gx, gy_high)):
        pl.semaphore_signal(barrier, inc=1, device_id=device, device_id_type=MESH)

    def load(src, dst, i):
        copy = pltpu.make_async_copy(src, dst, local_sems.at[i])
        copy.start()
        return copy

    load_faces = [
        load(les_ref.at[:, 0:2], state.at[:, 2:4, 8:56, :], 0),
        load(les_ref.at[:, 6:8], state.at[:, 8:10, 8:56, :], 1),
    ]
    load_inner = load(les_ref.at[:, 2:6], state.at[:, 4:8, 8:56, :], 2)
    load_small = [
        load(owner_in, owner_ref, 3),
        load(slot_in, slot_ref, 4),
        load(weight_in, weight_ref, 5),
        load(mask_in, mask_ref, 6),
        load(wave_in, wave_ref, 7),
    ]
    load_ops = load(ops_ref, ops_raw, 8)
    for copy in load_faces:
        copy.wait()

    def gossip_send(r):
        if r < gossip.shape[0]:
            d = 1 << r
            for target in (lax.rem(gx + d, n_gx), lax.rem(gx + (n_gx - d), n_gx)):
                pl.semaphore_signal(gossip.at[r], inc=1, device_id=(g, target, gy), device_id_type=MESH)

    def gossip_wait(r):
        if r < gossip.shape[0]:
            pl.semaphore_wait(gossip.at[r], 2)

    def x_pack(buf, out, scales, chunk):
        part = slice(8 + 24 * chunk, 32 + 24 * chunk)
        for f in range(5):
            for side, first in ((0, 2), (1, 8)):
                out[side, chunk, f] = pair_words(
                    buf[f, first, part, :], buf[f, first + 1, part, :], OFFSETS[f], scales[f]
                )

    def x_unpack(buf, words, scales, chunk):
        part = slice(8 + 24 * chunk, 32 + 24 * chunk)
        for f in range(5):
            for side, first in ((0, 0), (1, 10)):
                one, two = split_words(words[side, chunk, f], OFFSETS[f], scales[f])
                buf[f, first, part, :] = one
                buf[f, first + 1, part, :] = two

    def x_copies(sent_words, words, stage, chunk):
        first = 4 * stage + 2 * chunk
        return [
            remote(
                sent_words.at[0, chunk], words.at[1, chunk], x_send.at[first], x_recv.at[first + 1], (g, gx_low, gy)
            ),
            remote(
                sent_words.at[1, chunk], words.at[0, chunk], x_send.at[first + 1], x_recv.at[first], (g, gx_high, gy)
            ),
        ]

    def ends(buf, f, x):
        return jnp.where(row < 4, buf[f, x + 2, 8:16, :], buf[f, x + 2, 48:56, :])

    def z_pack(buf, out, scales):
        for f in range(5):
            for j in range(2):
                a = pair_words(ends(buf, f, 2 * j), ends(buf, f, 2 * j + 4), OFFSETS[f], scales[f])
                b = pair_words(ends(buf, f, 2 * j + 1), ends(buf, f, 2 * j + 5), OFFSETS[f], scales[f])
                out[2 * f + j] = jnp.where((row < 2) | (row >= 6), a, roll_row(b, 4))

    def z_unpack(buf, words, scales):
        for f in range(5):
            for j in range(2):
                word = words[2 * f + j]
                for i, part in enumerate((word, roll_row(word, 4))):
                    for x, tile in zip((2 * j + i, 2 * j + i + 4), split_words(part, OFFSETS[f], scales[f])):
                        buf[f, x + 2, 0:8, :] = tile
                        buf[f, x + 2, 56:64, :] = tile

    def y_add(packed, tile, slot):
        return jnp.where((lane >> 2) == slot, roll_lane(tile, 4 * slot + 2), packed)

    def y_merge(from_low, from_high):
        return jnp.where((lane & 2) == 0, from_low, from_high)

    def y_pack(x, carry):
        packed = jnp.zeros((8, 128), jnp.float32)
        for f in range(5):
            for zt in range(ZT):
                packed = y_add(packed, state[f, x + 2, pl.ds(8 + 8 * zt, 8), :], f * ZT + zt)
        ys1[x] = packed
        return carry

    x_pack(state, xs1, STATE_SCALE, 0)
    pl.semaphore_wait(barrier, 5)
    gossip_send(0)
    x_first = [x_copies(xs1, xr1, 0, chunk) for chunk in range(2)]
    x_second = [x_copies(xs2, xr2, 1, chunk) for chunk in range(2)]
    first = [
        remote(zs1, zr1, send1.at[0], recv1.at[0], (other, gx, gy)),
        remote(ys1, yr1.at[1], send1.at[1], recv1.at[2], (g, gx, gy_low)),
        remote(ys1, yr1.at[0], send1.at[2], recv1.at[1], (g, gx, gy_high)),
    ]
    for copy in x_first[0]:
        copy.start()
    x_pack(state, xs1, STATE_SCALE, 1)
    for copy in x_first[1]:
        copy.start()
    load_inner.wait()
    z_pack(state, zs1, STATE_SCALE)
    first[0].start()
    lax.fori_loop(0, CX, y_pack, 0)
    first[1].start()
    first[2].start()

    load_ops.wait()
    for copy in load_small:
        copy.wait()

    def widen(i, carry):
        part = pl.ds(pl.multiple_of(i * 512, 512), 512)
        ops_wide[...] = ops_raw[part, :].astype(jnp.float32)
        for w in range(4):
            ops_mat[pl.ds(pl.multiple_of(i * 128, 128), 128), w * 128:(w + 1) * 128] = (
                ops_wide[pl.ds(w, 128, stride=4), :].astype(jnp.bfloat16)
            )
        return carry

    lax.fori_loop(0, 12, widen, 0)
    target = jnp.full((8, 128), -1, jnp.int32)
    for k in range(4):
        weights = jnp.zeros((8, 128), jnp.int32)
        for x in range(8):
            line = owner_ref[0, k, x] * 8 + slot_ref[0, k, x]
            target = jnp.where(((lane & 31) == k * 8 + x) & (lane < 96), line, target)
            weights = jnp.where(row == x, weight_ref[0, k, x], weights)
        weight_tiles[k] = weights
    for o in range(n_gx):
        spread[o * 8:(o + 1) * 8, :] = jnp.where(target == row + o * 8, 1.0, 0.0)

    gossip_wait(0)
    gossip_send(1)
    first[0].wait_recv()
    z_unpack(state, zr1, STATE_SCALE)
    first[1].wait_recv()
    first[2].wait_recv()

    def first_rate(x, tiles):
        halo = y_merge(yr1[0, x], yr1[1, x])
        packed = jnp.zeros((8, 128), jnp.float32) if tiles[0] == 0 else ys2[x]
        for zt in tiles:
            centre, rates = rate_tile(state, x, zt, halo)
            part = pl.ds(8 * zt, 8)
            inner = pl.ds(8 + 8 * zt, 8)
            new = []
            for f in range(5):
                value = centre[f] + LES_STEP * rates[f]
                pred[f, x + 2, inner, :] = value
                base_sum[f, x, part, :] = centre[f] + (0.5 * LES_STEP) * rates[f]
                packed = y_add(packed, value, f * ZT + zt)
                new.append(value)
            rho, u0, u1, u2, _ = new
            m0, m1 = rho * u0, rho * u1
            s00[x + 2, part, :] = m0 * u0
            s01[x + 1, inner, :] = m0 * u1
            s02[x + 1, part, :] = m0 * u2
            s11[x, inner, :] = m1 * u1
            s12[x, inner, :] = m1 * u2
            s22[x, part, :] = rho * u2 * u2
        ys2[x] = packed

    def rate_inner(x, carry):
        first_rate(x, tuple(range(ZT)))
        return carry

    lax.fori_loop(2, 6, rate_inner, 0)
    gossip_wait(1)
    gossip_send(2)
    for chunk in range(2):
        for copy in x_first[chunk]:
            copy.wait_recv()
        x_unpack(state, xr1, STATE_SCALE, chunk)

        def rate_outer(j, carry):
            first_rate(lax.rem(j + 6, 8), tuple(range(3 * chunk, 3 * chunk + 3)))
            return carry

        lax.fori_loop(0, 4, rate_outer, 0)
        x_pack(pred, xs2, PRED_SCALE, chunk)
        for copy in x_second[chunk]:
            copy.start()

    second = [
        remote(zs2, zr2, send2.at[0], recv2.at[0], (other, gx, gy)),
        remote(ys2, yr2.at[1, 1:9], send2.at[1], recv2.at[2], (g, gx, gy_low)),
        remote(ys2, yr2.at[0, 1:9], send2.at[2], recv2.at[1], (g, gx, gy_high)),
        remote(ezy_s, ezy_r.at[1], send2.at[3], recv2.at[4], (other, gx, gy_low)),
        remote(ezy_s, ezy_r.at[0], send2.at[4], recv2.at[3], (other, gx, gy_high)),
        remote(exz_s.at[0], exz_r.at[1], send2.at[5], recv2.at[6], (other, gx_low, gy)),
        remote(exz_s.at[1], exz_r.at[0], send2.at[6], recv2.at[5], (other, gx_high, gy)),
        remote(ys2.at[0], yr2.at[1, 9], send2.at[7], recv2.at[10], (g, gx_low, gy_low)),
        remote(ys2.at[0], yr2.at[0, 9], send2.at[8], recv2.at[9], (g, gx_low, gy_high)),
        remote(ys2.at[7], yr2.at[1, 0], send2.at[9], recv2.at[8], (g, gx_high, gy_low)),
        remote(ys2.at[7], yr2.at[0, 0], send2.at[10], recv2.at[7], (g, gx_high, gy_high)),
    ]
    for side in range(2):
        x = 7 * side
        exz_s[side] = ends(pred, 0, x) * ends(pred, 1, x) * ends(pred, 2, x)
    for copy in second[5:]:
        copy.start()
    z_pack(pred, zs2, PRED_SCALE)
    for copy in second[:3]:
        copy.start()
    edge = jnp.zeros((8, 128), jnp.float32)
    for x in range(8):
        product = packed_products(ys2[x])[1]
        both = jnp.where(lane < 4, product, roll_lane(product, -16))
        edge = jnp.where((lane >> 3) == x, roll_lane(both, 8 * x), edge)
    ezy_s[...] = edge
    second[3].start()
    second[4].start()
    gossip_wait(2)
    gossip_send(3)

    second[0].wait_recv()
    z_unpack(pred, zr2, PRED_SCALE)
    for x in range(8):
        for part in (slice(0, 8), slice(56, 64)):
            rho, u0, u1, u2 = (pred[f, x + 2, part, :] for f in range(4))
            m1 = rho * u1
            s01[x + 1, part, :] = m1 * u0
            s11[x, part, :] = m1 * u1
            s12[x, part, :] = m1 * u2
    for copy in second[1:5]:
        copy.wait_recv()
    for x in range(8):
        ym2[x + 1] = y_merge(yr2[0, x + 1], yr2[1, x + 1])
    corners = y_merge(ezy_r[0], ezy_r[1])
    for x in range(8):
        ezy_x[x] = roll_lane(corners, -8 * x)

    def lighthill(x, carry):
        along_x = packed_products(ym2[x + 2])[0] - packed_products(ym2[x])[0]
        _, s12_halo, square = packed_products(ym2[x + 1])
        corner = ezy_x[x]
        next_tile = jnp.where(lane >= 20, roll_lane(corner, 20), roll_lane(s12_halo, -4))
        last_tile = jnp.where(lane < 4, roll_lane(corner, -4), roll_lane(s12_halo, 4))
        after = roll_row(jnp.where(row == 0, next_tile, s12_halo), -1)
        before = roll_row(jnp.where(row == 7, last_tile, s12_halo), 1)
        cross = along_x + (after - before)
        keep = mask_ref[0, x].astype(jnp.float32)
        for zt in range(ZT):
            part = pl.ds(8 * zt, 8)

            def z(ref, index, dz):
                return ref[index, pl.ds(8 + 8 * zt + dz, 8), :]

            direct = s00[x + 4, part, :] + s00[x, part, :] - 2.0 * s00[x + 2, part, :]
            direct = direct + (z(s11, x, 2) + z(s11, x, -2) - 2.0 * z(s11, x, 0))
            tile = s22[x, part, :]
            ((before, after),) = y_shifts(tile, square, zt, (2,))
            direct = direct + (before + after - 2.0 * tile)
            mixed = (z(s01, x + 2, 1) - z(s01, x + 2, -1)) - (z(s01, x, 1) - z(s01, x, -1))
            tile = (s02[x + 2, part, :] - s02[x, part, :]) + (z(s12, x, 1) - z(s12, x, -1))
            ((before, after),) = y_shifts(tile, cross, zt, (1,))
            mixed = mixed + (after - before)
            light[pl.ds(pl.multiple_of(x * CZ + 8 * zt, 8), 8), :] = (0.25 * direct + 0.5 * mixed) * keep
        return carry

    lax.fori_loop(2, 6, lighthill, 0)
    for chunk in range(2):
        for copy in x_second[chunk]:
            copy.wait_recv()
        x_unpack(pred, xr2, PRED_SCALE, chunk)
    for index in (0, 1, 10, 11):
        s00[index] = pred[0, index, 8:56, :] * pred[1, index, 8:56, :] * pred[1, index, 8:56, :]
    for index, layer in ((0, 1), (9, 10)):
        m0 = pred[0, layer, 8:56, :] * pred[1, layer, 8:56, :]
        s01[index, 8:56, :] = m0 * pred[2, layer, 8:56, :]
        s02[index] = m0 * pred[3, layer, 8:56, :]
    for copy in second[5:]:
        copy.wait_recv()
    for index in (0, 9):
        ym2[index] = y_merge(yr2[0, index], yr2[1, index])
    for side, index in ((0, 0), (1, 9)):
        s01[index, 0:8, :] = exz_r[side]
        s01[index, 56:64, :] = exz_r[side]
    lax.fori_loop(0, 4, lambda j, carry: lighthill(lax.rem(j + 6, 8), carry), 0)

    pieces = []
    for zp in range(12):
        one, two = (
            light[pl.ds(4 * zp + 2 * i, 8, stride=CZ), :] + light[pl.ds(4 * zp + 2 * i + 1, 8, stride=CZ), :]
            for i in range(2)
        )
        one = one + roll_lane(one, -1)
        two = two + roll_lane(two, 1)
        pieces.append(jnp.where((lane & 1) == 0, one, two))
    merged = jnp.concatenate(pieces, axis=0).astype(jnp.bfloat16)
    source_lane = lax.broadcasted_iota(jnp.int32, (128, 128), 0)
    target_lane = lax.broadcasted_iota(jnp.int32, (128, 128), 1)
    order = jnp.where(target_lane == (source_lane & 1) * 64 + (source_lane >> 1), 1.0, 0.0).astype(jnp.bfloat16)
    sorted_rows = jnp.dot(merged, order, preferred_element_type=jnp.float32)
    tile_rows = jnp.concatenate([sorted_rows[8 * i:8 * i + 8, :] for i in range(12)], axis=1).astype(jnp.bfloat16)
    products = jnp.dot(tile_rows, ops_mat[...], preferred_element_type=jnp.float32)
    pairs = []
    for k in range(4):
        chosen = jnp.zeros((8, 128), jnp.float32)
        for w in range(4):
            chosen = jnp.where(weight_tiles[k] == w, products[:, w * 128:(w + 1) * 128], chosen)
        pairs.append(chosen)
    values = jnp.concatenate(pairs, axis=0)
    high = values.astype(jnp.bfloat16).astype(jnp.float32)
    middle = (values - high).astype(jnp.bfloat16).astype(jnp.float32)
    rest = values - high - middle
    stacked = jnp.concatenate([high, middle, rest, jnp.zeros((32, 128), jnp.float32)], axis=0).astype(jnp.bfloat16)
    sent[...] = jnp.dot(spread[...].astype(jnp.bfloat16), stacked, preferred_element_type=jnp.float32)

    gossip_wait(3)
    all_copies = []
    for d in far_order:
        owner = lax.rem(gx + d, n_gx)
        copy = remote(
            sent.at[pl.ds(pl.multiple_of(owner * 8, 8), 8), :], received.at[gx],
            all_send.at[0], all_recv.at[0], (g, owner, gy),
        )
        copy.start()
    received[gx] = sent[pl.ds(pl.multiple_of(gx * 8, 8), 8), :]

    around = [(dx, dr) for dx in (-1, 0, 1) for dr in (-1, 0, 1) if (dx, dr) != (0, 0)]

    def neighbour(dx, dr):
        there = lax.rem(rank + (n_rank + dr), n_rank)
        return (there // n_gy, lax.rem(gx + (n_gx + dx), n_gx), lax.rem(there, n_gy))

    def slot_of(dx, dr):
        return around.index((dx, dr))

    for dx, dr in around:
        remote(
            wave_ref, near_wave.at[slot_of(-dx, -dr)], wave_send.at[0], wave_recv.at[0], neighbour(dx, dr)
        ).start()

    def second_rate(x, carry):
        halo = ym2[x + 1]
        for zt in range(ZT):
            _, rates = rate_tile(pred, x, zt, halo)
            part = pl.ds(8 * zt, 8)
            for f in range(5):
                base_sum[f, x, part, :] = base_sum[f, x, part, :] + (0.5 * LES_STEP) * rates[f]
        return carry

    lax.fori_loop(0, CX, second_rate, 0)
    store_les = pltpu.make_async_copy(base_sum, les_out, local_sems.at[0])
    store_les.start()

    others = received.at[0:n_gx - 1]
    pltpu.make_async_copy(others, others, all_recv.at[0]).wait()
    own_source[...] = jnp.sum(received[...], axis=0)
    for dx, dr in around:
        remote(
            own_source, near_source.at[slot_of(-dx, -dr)], src_send.at[0], src_recv.at[0], neighbour(dx, dr)
        ).start()

    pltpu.make_async_copy(near_wave, near_wave, wave_recv.at[0]).wait()
    wide_row = lax.broadcasted_iota(jnp.int32, (24, 256), 0)
    wide_lane = lax.broadcasted_iota(jnp.int32, (24, 256), 1)

    def flag(yes):
        return yes.astype(jnp.int32).astype(jnp.float32)

    inside = jnp.where(wide_row < 8, flag(gx > 0), jnp.where(wide_row >= 16, flag(gx < n_gx - 1), 1.0))
    inside = inside * jnp.where(
        wide_lane < 128, 1.0, jnp.where(wide_lane < 192, flag(rank < n_rank - 1), flag(rank > 0))
    )
    column = jnp.where(wide_lane < 192, wide_lane, wide_lane - 256) + rank * 128
    inverse_radius = 1.0 / (column.astype(jnp.float32) + 0.5)

    def assemble(block):
        strips = []
        for dx in (-1, 0, 1):
            side = jnp.where(lane < 64, block(dx, 1), block(dx, -1))
            strips.append(jnp.concatenate([block(dx, 0), side], axis=1))
        return jnp.concatenate(strips, axis=0) * inside

    def wave_block(f):
        return lambda dx, dr: wave_ref[f] if (dx, dr) == (0, 0) else near_wave[slot_of(dx, dr), f]

    now = [assemble(wave_block(f)) for f in range(3)]
    pltpu.make_async_copy(near_source, near_source, src_recv.at[0]).wait()
    source = assemble(lambda dx, dr: own_source[...] if (dx, dr) == (0, 0) else near_source[slot_of(dx, dr)])
    for _ in range(2):
        rate_one = wave_rates(now, source, inverse_radius)
        ahead = [(v + WAVE_STEP * r) * inside for v, r in zip(now, rate_one)]
        rate_two = wave_rates(ahead, source, inverse_radius)
        now = [(v + (0.5 * WAVE_STEP) * (a + b)) * inside for v, a, b in zip(now, rate_one, rate_two)]
    for f in range(3):
        wave_out[f] = now[f][8:16, 0:128]

    for copy in first + second + x_first[0] + x_first[1] + x_second[0] + x_second[1]:
        copy.wait_send()
    pltpu.make_async_copy(others, others, all_send.at[0]).wait()
    pltpu.make_async_copy(near_wave, near_wave, wave_send.at[0]).wait()
    pltpu.make_async_copy(near_source, near_source, src_send.at[0]).wait()
    store_les.wait()


def hand_on(les_in, wave_in, les_out, wave_out, les_buf, wave_buf, in_sems, out_sems):
    legs = [(wave_in, wave_buf, wave_out)] + [(les_in.at[f], les_buf.at[f], les_out.at[f]) for f in range(5)]
    into = [pltpu.make_async_copy(a, b, in_sems.at[i]) for i, (a, b, _) in enumerate(legs)]
    out = [pltpu.make_async_copy(b, c, out_sems.at[i]) for i, (_, b, c) in enumerate(legs)]
    for copy in into:
        copy.start()
    for one, two in zip(into, out):
        one.wait()
        two.start()
    for copy in out:
        copy.wait()


def on_device(sizes, les_state, wave_state, restriction_ops, pair_owner, pair_slot, pair_weight, tile_mask):
    n_gx = sizes[1]
    tile_len, op_count, width = restriction_ops.shape
    ops_flat = restriction_ops.reshape(tile_len * op_count, width)
    rounds = max(1, (n_gx // 2).bit_length() - 1)
    far_order = sorted(range(1, n_gx), key=lambda d: -(2 * min(d // 8, 4 - d // 8) + min(d % 8, 8 - d % 8)))
    f32, i32, bf16 = jnp.float32, jnp.int32, jnp.bfloat16
    vmem, smem, dma = pltpu.VMEM, pltpu.SMEM, pltpu.SemaphoreType.DMA
    scratch = [
        vmem((5, 12, 64, 128), f32), vmem((5, 12, 64, 128), f32), vmem((5, 8, 48, 128), f32),
        vmem((12, 48, 128), f32), vmem((8, 64, 128), f32), vmem((8, 48, 128), f32),
        vmem((10, 64, 128), f32), vmem((10, 48, 128), f32), vmem((8, 64, 128), f32),
        vmem((3, 8, 128), f32), smem((1, 4, 8), i32), smem((1, 4, 8), i32), smem((1, 4, 8), i32), smem((1, 8), i32),
        vmem((2, 2, 5, 24, 128), i32), vmem((2, 2, 5, 24, 128), i32),
        vmem((2, 2, 5, 24, 128), i32), vmem((2, 2, 5, 24, 128), i32),
        vmem((10, 8, 128), i32), vmem((10, 8, 128), i32), vmem((10, 8, 128), i32), vmem((10, 8, 128), i32),
        vmem((8, 8, 128), f32), vmem((2, 8, 8, 128), f32), vmem((8, 8, 128), f32), vmem((2, 10, 8, 128), f32),
        vmem((10, 8, 128), f32),
        vmem((2, 8, 128), f32), vmem((2, 8, 128), f32), vmem((8, 128), f32), vmem((2, 8, 128), f32),
        vmem((8, 8, 128), f32),
        vmem((CX * CZ, 128), f32), vmem((6144, 128), bf16), vmem((512, 128), f32), vmem((1536, 512), bf16),
        vmem((n_gx * 8, 128), f32), vmem((4, 8, 128), i32),
        vmem((n_gx * 8, 128), f32), vmem((n_gx, 8, 128), f32), vmem((8, 128), f32),
        vmem((8, 8, 128), f32), vmem((8, 3, 8, 128), f32),
        dma((9,)), dma((8,)), dma((8,)), dma((3,)), dma((3,)), dma((11,)), dma((11,)), dma((1,)), dma((1,)), dma((1,)), dma((1,)),
        dma((1,)), dma((1,)), pltpu.SemaphoreType.REGULAR((rounds,)),
    ]
    any_space = pl.BlockSpec(memory_space=pl.ANY)
    in_vmem = pl.BlockSpec(memory_space=pltpu.VMEM)
    results = pl.pallas_call(
        functools.partial(kernel, sizes, far_order),
        out_shape=(
            jax.ShapeDtypeStruct(les_state.shape, f32),
            jax.ShapeDtypeStruct(wave_state.shape, f32),
        ),
        in_specs=[any_space] * 7,
        out_specs=(any_space, in_vmem),
        scratch_shapes=scratch,
        compiler_params=pltpu.CompilerParams(collective_id=0, has_side_effects=True),
        name="jet_step",
    )(les_state, wave_state, ops_flat, *(a.swapaxes(1, 2) for a in (pair_owner, pair_slot, pair_weight)), tile_mask)
    return pl.pallas_call(
        hand_on,
        out_shape=tuple(jax.ShapeDtypeStruct(r.shape, f32) for r in results),
        in_specs=[any_space] * 2,
        out_specs=(any_space,) * 2,
        scratch_shapes=[vmem(les_state.shape, f32), vmem(wave_state.shape, f32), dma((6,)), dma((6,))],
        name="hand_on",
    )(*results)


def solution(mesh):
    sizes = (mesh.shape["group"], mesh.shape["gx"], mesh.shape["gy"])
    return jax.shard_map(
        functools.partial(on_device, sizes),
        mesh=mesh,
        in_specs=(
            P(None, "gx", "group", "gy"),
            P(None, "gx", ("group", "gy")),
            P(),
            P(("group", "gy"), "gx", None),
            P(("group", "gy"), "gx", None),
            P(("group", "gy"), "gx", None),
            P(("group", "gy"), "gx"),
        ),
        out_specs=(P(None, "gx", "group", "gy"), P(None, "gx", ("group", "gy"))),
        check_vma=False,
    )
```

```python
import functools

import jax
import jax.numpy as jnp
from jax import lax
from jax.experimental import pallas as pl
from jax.experimental.pallas import tpu as pltpu
from jax.sharding import PartitionSpec as P

MESH = pl.DeviceIdType.MESH
VISCOSITY = 0.05
LES_STEP = 0.2
WAVE_STEP = 0.3
CX, CZ, CY = 8, 48, 128
ZT = CZ // 8
CHUNKS = 3
CHUNK_ROWS = CZ // CHUNKS
CHUNK_TILES = ZT // CHUNKS
OFFSETS = (1.0, 0.0, 0.0, 0.0, 1.0)
STATE_SCALE = (130816.0, 65408.0, 65408.0, 65408.0, 130816.0)
PRED_SCALE = (24576.0,) * 5


def encode(value, offset, scale):
    return ((value - offset) * scale + 32768.5).astype(jnp.int32)


def decode(code, offset, scale):
    return code.astype(jnp.float32) * (1.0 / scale) + (offset - 32768.0 / scale)


def pair_words(first, second, offset, scale):
    return (encode(first, offset, scale) << 16) | encode(second, offset, scale)


def split_words(words, offset, scale):
    first = decode(lax.shift_right_logical(words, 16), offset, scale)
    return first, decode(words & 0xFFFF, offset, scale)


def lanes():
    return lax.broadcasted_iota(jnp.int32, (8, 128), 1)


def rows():
    return lax.broadcasted_iota(jnp.int32, (8, 128), 0)


def roll_lane(tile, shift):
    shift = shift % tile.shape[1]
    return pltpu.roll(tile, shift, 1) if shift else tile


def roll_row(tile, shift):
    shift = shift % tile.shape[0]
    return pltpu.roll(tile, shift, 0) if shift else tile


def y_shifts(tile, halo, slot, reach):
    lane = lanes()
    halo = roll_lane(halo, -(4 * slot + 2))
    shifts = []
    for s in reach:
        before = roll_lane(jnp.where(lane >= 128 - s, halo, tile), s)
        after = roll_lane(jnp.where(lane < s, halo, tile), -s)
        shifts.append((before, after))
    return shifts


def rate_tile(buf, x, zt, halo):
    base = 8 + 8 * zt

    def at(f, dx, dz):
        return buf[f, x + (2 + dx), pl.ds(base + dz, 8), :]

    centre, grads, laps = [], [], []
    for f in range(5):
        c = at(f, 0, 0)
        xm1, xp1, zm1, zp1 = at(f, -1, 0), at(f, 1, 0), at(f, 0, -1), at(f, 0, 1)
        (ym1, yp1), (ym2, yp2) = y_shifts(c, halo, f * ZT + zt, (1, 2))
        dx = 8.0 * (xp1 - xm1) - (at(f, 2, 0) - at(f, -2, 0))
        dz = 8.0 * (zp1 - zm1) - (at(f, 0, 2) - at(f, 0, -2))
        dy = 8.0 * (yp1 - ym1) - (yp2 - ym2)
        centre.append(c)
        grads.append((dx, dz, dy))
        laps.append(((xm1 + xp1) + (zm1 + zp1)) + (ym1 + yp1) - 6.0 * c if 1 <= f <= 3 else None)
    rho, u0, u1, u2, p = centre
    div = grads[1][0] + grads[2][1] + grads[3][2]
    inverse = 1.0 / rho

    def advect(f):
        return u0 * grads[f][0] + u1 * grads[f][1] + u2 * grads[f][2]

    twelfth = -1.0 / 12.0
    rates = [(advect(0) + rho * div) * twelfth]
    for d in range(3):
        rates.append((advect(1 + d) + grads[4][d] * inverse) * twelfth + VISCOSITY * laps[1 + d])
    rates.append((advect(4) + 1.4 * (p * div)) * twelfth)
    return centre, rates


def packed_products(tile):
    momentum = tile * roll_lane(tile, -72)
    return (
        momentum * roll_lane(tile, -24),
        momentum * roll_lane(tile, -48),
        momentum * roll_lane(tile, -72),
    )


def wave_rates(state, source, inverse_radius):
    p, ux, ur = state

    def d(f, axis):
        size = f.shape[axis]
        one = pltpu.roll(f, size - 1, axis) - pltpu.roll(f, 1, axis)
        two = pltpu.roll(f, size - 2, axis) - pltpu.roll(f, 2, axis)
        return (8.0 * one - two) * (1.0 / 12.0)

    return (source - d(ux, 0) - d(ur, 1) - ur * inverse_radius, -d(p, 0), -d(p, 1))


def kernel(
    sizes, far_order,
    les_ref, wave_in, ops_ref, owner_in, slot_in, weight_in, mask_in,
    les_out, wave_out,
    state, pred, base_sum, s00, s11, s22, s01, s02, s12,
    wave_ref, owner_ref, slot_ref, weight_ref, mask_ref,
    xs1, xr1, xs2, xr2, zs1, zr1, zs2, zr2, ys1, yr1, ys2, yr2, ym2,
    exz_s, exz_r, ezy_s, ezy_r, ezy_x,
    light, ops_raw, ops_wide, ops_mat, spread, labels, weight_tiles,
    sent, received, own_source, near_source, near_wave,
    local_sems, x_send, x_recv, send1, recv1, send2, recv2, wave_send, wave_recv, all_send, all_recv, src_send, src_recv, gossip,
):
    n_group, n_gx, n_gy = sizes
    g, gx, gy = lax.axis_index("group"), lax.axis_index("gx"), lax.axis_index("gy")
    rank = g * n_gy + gy
    n_rank = n_group * n_gy
    gx_low, gx_high = lax.rem(gx + (n_gx - 1), n_gx), lax.rem(gx + 1, n_gx)
    gy_low, gy_high = lax.rem(gy + (n_gy - 1), n_gy), lax.rem(gy + 1, n_gy)
    other = 1 - g
    lane, row = lanes(), rows()

    def remote(src, dst, send_sem, recv_sem, device):
        return pltpu.make_async_remote_copy(
            src_ref=src, dst_ref=dst, send_sem=send_sem, recv_sem=recv_sem, device_id=device, device_id_type=MESH
        )

    barrier = pltpu.get_barrier_semaphore()
    for device in ((g, gx_low, gy), (g, gx_high, gy), (other, gx, gy), (g, gx, gy_low), (g, gx, gy_high)):
        pl.semaphore_signal(barrier, inc=1, device_id=device, device_id_type=MESH)

    def load(src, dst, i):
        copy = pltpu.make_async_copy(src, dst, local_sems.at[i])
        copy.start()
        return copy

    load_faces = [
        load(les_ref.at[:, 0:2], state.at[:, 2:4, 8:56, :], 0),
        load(les_ref.at[:, 6:8], state.at[:, 8:10, 8:56, :], 1),
    ]
    load_inner = load(les_ref.at[:, 2:6], state.at[:, 4:8, 8:56, :], 2)
    load_small = [
        load(owner_in, owner_ref, 3),
        load(slot_in, slot_ref, 4),
        load(weight_in, weight_ref, 5),
        load(mask_in, mask_ref, 6),
        load(wave_in, wave_ref, 7),
    ]
    load_ops = load(ops_ref, ops_raw, 8)
    for copy in load_faces:
        copy.wait()

    def gossip_send(r):
        if r < gossip.shape[0]:
            d = 1 << r
            for target in (lax.rem(gx + d, n_gx), lax.rem(gx + (n_gx - d), n_gx)):
                pl.semaphore_signal(gossip.at[r], inc=1, device_id=(g, target, gy), device_id_type=MESH)

    def gossip_wait(r):
        if r < gossip.shape[0]:
            pl.semaphore_wait(gossip.at[r], 2)

    def x_pack(buf, out, scales, chunk):
        part = slice(8 + CHUNK_ROWS * chunk, 8 + CHUNK_ROWS * (chunk + 1))
        for f in range(5):
            for side, first in ((0, 2), (1, 8)):
                out[side, chunk, f] = pair_words(
                    buf[f, first, part, :], buf[f, first + 1, part, :], OFFSETS[f], scales[f]
                )

    def x_unpack(buf, words, scales, chunk):
        part = slice(8 + CHUNK_ROWS * chunk, 8 + CHUNK_ROWS * (chunk + 1))
        for f in range(5):
            for side, first in ((0, 0), (1, 10)):
                one, two = split_words(words[side, chunk, f], OFFSETS[f], scales[f])
                buf[f, first, part, :] = one
                buf[f, first + 1, part, :] = two

    def x_copies(sent_words, words, stage, chunk):
        first = 2 * (CHUNKS * stage + chunk)
        return [
            remote(
                sent_words.at[0, chunk], words.at[1, chunk], x_send.at[first], x_recv.at[first + 1], (g, gx_low, gy)
            ),
            remote(
                sent_words.at[1, chunk], words.at[0, chunk], x_send.at[first + 1], x_recv.at[first], (g, gx_high, gy)
            ),
        ]

    def ends(buf, f, x):
        return jnp.where(row < 4, buf[f, x + 2, 8:16, :], buf[f, x + 2, 48:56, :])

    def z_pack(buf, out, scales):
        for f in range(5):
            for j in range(2):
                a = pair_words(ends(buf, f, 2 * j), ends(buf, f, 2 * j + 4), OFFSETS[f], scales[f])
                b = pair_words(ends(buf, f, 2 * j + 1), ends(buf, f, 2 * j + 5), OFFSETS[f], scales[f])
                out[2 * f + j] = jnp.where((row < 2) | (row >= 6), a, roll_row(b, 4))

    def z_unpack(buf, words, scales):
        for f in range(5):
            for j in range(2):
                word = words[2 * f + j]
                for i, part in enumerate((word, roll_row(word, 4))):
                    for x, tile in zip((2 * j + i, 2 * j + i + 4), split_words(part, OFFSETS[f], scales[f])):
                        buf[f, x + 2, 0:8, :] = tile
                        buf[f, x + 2, 56:64, :] = tile

    def y_add(packed, tile, slot):
        return jnp.where((lane >> 2) == slot, roll_lane(tile, 4 * slot + 2), packed)

    def y_merge(from_low, from_high):
        return jnp.where((lane & 2) == 0, from_low, from_high)

    def y_pack(x, carry):
        packed = jnp.zeros((8, 128), jnp.float32)
        for f in range(5):
            for zt in range(ZT):
                packed = y_add(packed, state[f, x + 2, pl.ds(8 + 8 * zt, 8), :], f * ZT + zt)
        ys1[x] = packed
        return carry

    x_pack(state, xs1, STATE_SCALE, 0)
    pl.semaphore_wait(barrier, 5)
    gossip_send(0)
    x_first = [x_copies(xs1, xr1, 0, chunk) for chunk in range(CHUNKS)]
    x_second = [x_copies(xs2, xr2, 1, chunk) for chunk in range(CHUNKS)]
    first = [
        remote(zs1, zr1, send1.at[0], recv1.at[0], (other, gx, gy)),
        remote(ys1, yr1.at[1], send1.at[1], recv1.at[2], (g, gx, gy_low)),
        remote(ys1, yr1.at[0], send1.at[2], recv1.at[1], (g, gx, gy_high)),
    ]
    for copy in x_first[0]:
        copy.start()
    for chunk in range(1, CHUNKS):
        x_pack(state, xs1, STATE_SCALE, chunk)
        for copy in x_first[chunk]:
            copy.start()
    load_inner.wait()
    z_pack(state, zs1, STATE_SCALE)
    first[0].start()
    lax.fori_loop(0, CX, y_pack, 0)
    first[1].start()
    first[2].start()

    load_ops.wait()
    for copy in load_small:
        copy.wait()

    def widen(i, carry):
        part = pl.ds(pl.multiple_of(i * 512, 512), 512)
        ops_wide[...] = ops_raw[part, :].astype(jnp.float32)
        for w in range(4):
            ops_mat[pl.ds(pl.multiple_of(i * 128, 128), 128), w * 128:(w + 1) * 128] = (
                ops_wide[pl.ds(w, 128, stride=4), :].astype(jnp.bfloat16)
            )
        return carry

    lax.fori_loop(0, 12, widen, 0)
    pair_lane = lane & 31
    owners = jnp.full((8, 128), -99, jnp.int32)
    first_slot, second_slot, seen = (jnp.zeros((8, 128), jnp.int32) for _ in range(3))
    for k in range(4):
        weights = jnp.zeros((8, 128), jnp.int32)
        for x in range(8):
            owner = owner_ref[0, k, x]
            owners = jnp.where((pair_lane == k * 8 + x) & (lane < 96), owner, owners)
            hit = lane == owner
            first_slot = jnp.where(hit & (seen == 0), slot_ref[0, k, x] + 1, first_slot)
            second_slot = jnp.where(hit & (seen == 1), slot_ref[0, k, x] + 1, second_slot)
            seen = jnp.where(hit, seen + 1, seen)
            weights = jnp.where(row == x, weight_ref[0, k, x], weights)
        weight_tiles[k] = weights
    rank_of = jnp.zeros((8, 128), jnp.int32)
    for k in range(4):
        for x in range(8):
            earlier = (owners == owner_ref[0, k, x]) & (pair_lane > k * 8 + x)
            rank_of = rank_of + jnp.where(earlier, 1, 0)
    own_lane = 8 * lax.rem(gx, 16)
    first_slot = pltpu.roll(first_slot.astype(jnp.float32), own_lane + 1, 1)
    second_slot = pltpu.roll(second_slot.astype(jnp.float32), own_lane + 5, 1)
    first_here = (row == 7) & (lane >= own_lane) & (lane < own_lane + 3)
    second_here = (row == 7) & (lane >= own_lane + 4) & (lane < own_lane + 7)
    for d in range(n_gx):
        near = (owners >= d - 1) & (owners <= d + 1)
        spread[d * 8:(d + 1) * 8, :] = jnp.where(near & (owners - (d - 1) + 4 * rank_of == row), 1.0, 0.0)
        slots = jnp.where(second_here, roll_lane(second_slot, -d), 0.0)
        labels[d * 8:(d + 1) * 8, :] = jnp.where(first_here, roll_lane(first_slot, -d), slots)

    gossip_wait(0)
    gossip_send(1)
    first[0].wait_recv()
    z_unpack(state, zr1, STATE_SCALE)
    first[1].wait_recv()
    first[2].wait_recv()

    def first_rate(x, tiles):
        halo = y_merge(yr1[0, x], yr1[1, x])
        packed = jnp.zeros((8, 128), jnp.float32) if tiles[0] == 0 else ys2[x]
        for zt in tiles:
            centre, rates = rate_tile(state, x, zt, halo)
            part = pl.ds(8 * zt, 8)
            inner = pl.ds(8 + 8 * zt, 8)
            new = []
            for f in range(5):
                value = centre[f] + LES_STEP * rates[f]
                pred[f, x + 2, inner, :] = value
                base_sum[f, x, part, :] = centre[f] + (0.5 * LES_STEP) * rates[f]
                packed = y_add(packed, value, f * ZT + zt)
                new.append(value)
            rho, u0, u1, u2, _ = new
            m0, m1 = rho * u0, rho * u1
            s00[x + 2, part, :] = m0 * u0
            s01[x + 1, inner, :] = m0 * u1
            s02[x + 1, part, :] = m0 * u2
            s11[x, inner, :] = m1 * u1
            s12[x, inner, :] = m1 * u2
            s22[x, part, :] = rho * u2 * u2
        ys2[x] = packed

    def rate_inner(x, carry):
        first_rate(x, tuple(range(ZT)))
        return carry

    lax.fori_loop(2, 6, rate_inner, 0)
    gossip_wait(1)
    gossip_send(2)
    for chunk in range(CHUNKS):
        for copy in x_first[chunk]:
            copy.wait_recv()
        x_unpack(state, xr1, STATE_SCALE, chunk)
        for x in (6, 7, 0, 1):
            first_rate(x, tuple(range(CHUNK_TILES * chunk, CHUNK_TILES * (chunk + 1))))
        x_pack(pred, xs2, PRED_SCALE, chunk)
        for copy in x_second[chunk]:
            copy.start()

    second = [
        remote(zs2, zr2, send2.at[0], recv2.at[0], (other, gx, gy)),
        remote(ys2, yr2.at[1, 1:9], send2.at[1], recv2.at[2], (g, gx, gy_low)),
        remote(ys2, yr2.at[0, 1:9], send2.at[2], recv2.at[1], (g, gx, gy_high)),
        remote(ezy_s, ezy_r.at[1], send2.at[3], recv2.at[4], (other, gx, gy_low)),
        remote(ezy_s, ezy_r.at[0], send2.at[4], recv2.at[3], (other, gx, gy_high)),
        remote(exz_s.at[0], exz_r.at[1], send2.at[5], recv2.at[6], (other, gx_low, gy)),
        remote(exz_s.at[1], exz_r.at[0], send2.at[6], recv2.at[5], (other, gx_high, gy)),
        remote(ys2.at[0], yr2.at[1, 9], send2.at[7], recv2.at[10], (g, gx_low, gy_low)),
        remote(ys2.at[0], yr2.at[0, 9], send2.at[8], recv2.at[9], (g, gx_low, gy_high)),
        remote(ys2.at[7], yr2.at[1, 0], send2.at[9], recv2.at[8], (g, gx_high, gy_low)),
        remote(ys2.at[7], yr2.at[0, 0], send2.at[10], recv2.at[7], (g, gx_high, gy_high)),
    ]
    for side in range(2):
        x = 7 * side
        exz_s[side] = ends(pred, 0, x) * ends(pred, 1, x) * ends(pred, 2, x)
    for copy in second[5:]:
        copy.start()
    z_pack(pred, zs2, PRED_SCALE)
    for copy in second[:3]:
        copy.start()
    edge = jnp.zeros((8, 128), jnp.float32)
    for x in range(8):
        product = packed_products(ys2[x])[1]
        both = jnp.where(lane < 4, product, roll_lane(product, -16))
        edge = jnp.where((lane >> 3) == x, roll_lane(both, 8 * x), edge)
    ezy_s[...] = edge
    second[3].start()
    second[4].start()
    gossip_wait(2)
    gossip_send(3)

    second[0].wait_recv()
    z_unpack(pred, zr2, PRED_SCALE)
    for x in range(8):
        for part in (slice(0, 8), slice(56, 64)):
            rho, u0, u1, u2 = (pred[f, x + 2, part, :] for f in range(4))
            m1 = rho * u1
            s01[x + 1, part, :] = m1 * u0
            s11[x, part, :] = m1 * u1
            s12[x, part, :] = m1 * u2
    for copy in second[1:5]:
        copy.wait_recv()
    for x in range(8):
        ym2[x + 1] = y_merge(yr2[0, x + 1], yr2[1, x + 1])
    corners = y_merge(ezy_r[0], ezy_r[1])
    for x in range(8):
        ezy_x[x] = roll_lane(corners, -8 * x)

    def lighthill(x, carry):
        along_x = packed_products(ym2[x + 2])[0] - packed_products(ym2[x])[0]
        _, s12_halo, square = packed_products(ym2[x + 1])
        corner = ezy_x[x]
        next_tile = jnp.where(lane >= 20, roll_lane(corner, 20), roll_lane(s12_halo, -4))
        last_tile = jnp.where(lane < 4, roll_lane(corner, -4), roll_lane(s12_halo, 4))
        after = roll_row(jnp.where(row == 0, next_tile, s12_halo), -1)
        before = roll_row(jnp.where(row == 7, last_tile, s12_halo), 1)
        cross = along_x + (after - before)
        keep = mask_ref[0, x].astype(jnp.float32)
        for zt in range(ZT):
            part = pl.ds(8 * zt, 8)

            def z(ref, index, dz):
                return ref[index, pl.ds(8 + 8 * zt + dz, 8), :]

            direct = s00[x + 4, part, :] + s00[x, part, :] - 2.0 * s00[x + 2, part, :]
            direct = direct + (z(s11, x, 2) + z(s11, x, -2) - 2.0 * z(s11, x, 0))
            tile = s22[x, part, :]
            ((before, after),) = y_shifts(tile, square, zt, (2,))
            direct = direct + (before + after - 2.0 * tile)
            mixed = (z(s01, x + 2, 1) - z(s01, x + 2, -1)) - (z(s01, x, 1) - z(s01, x, -1))
            tile = (s02[x + 2, part, :] - s02[x, part, :]) + (z(s12, x, 1) - z(s12, x, -1))
            ((before, after),) = y_shifts(tile, cross, zt, (1,))
            mixed = mixed + (after - before)
            light[pl.ds(pl.multiple_of(x * CZ + 8 * zt, 8), 8), :] = (0.25 * direct + 0.5 * mixed) * keep
        return carry

    lax.fori_loop(2, 6, lighthill, 0)
    for chunk in range(CHUNKS):
        for copy in x_second[chunk]:
            copy.wait_recv()
        x_unpack(pred, xr2, PRED_SCALE, chunk)
    for index in (0, 1, 10, 11):
        s00[index] = pred[0, index, 8:56, :] * pred[1, index, 8:56, :] * pred[1, index, 8:56, :]
    for index, layer in ((0, 1), (9, 10)):
        m0 = pred[0, layer, 8:56, :] * pred[1, layer, 8:56, :]
        s01[index, 8:56, :] = m0 * pred[2, layer, 8:56, :]
        s02[index] = m0 * pred[3, layer, 8:56, :]
    for copy in second[5:]:
        copy.wait_recv()
    for index in (0, 9):
        ym2[index] = y_merge(yr2[0, index], yr2[1, index])
    for side, index in ((0, 0), (1, 9)):
        s01[index, 0:8, :] = exz_r[side]
        s01[index, 56:64, :] = exz_r[side]
    lax.fori_loop(0, 4, lambda j, carry: lighthill(lax.rem(j + 6, 8), carry), 0)

    pieces = []
    for zp in range(12):
        one, two = (
            light[pl.ds(4 * zp + 2 * i, 8, stride=CZ), :] + light[pl.ds(4 * zp + 2 * i + 1, 8, stride=CZ), :]
            for i in range(2)
        )
        one = one + roll_lane(one, -1)
        two = two + roll_lane(two, 1)
        pieces.append(jnp.where((lane & 1) == 0, one, two))
    merged = jnp.concatenate(pieces, axis=0).astype(jnp.bfloat16)
    source_lane = lax.broadcasted_iota(jnp.int32, (128, 128), 0)
    target_lane = lax.broadcasted_iota(jnp.int32, (128, 128), 1)
    order = jnp.where(target_lane == (source_lane & 1) * 64 + (source_lane >> 1), 1.0, 0.0).astype(jnp.bfloat16)
    sorted_rows = jnp.dot(merged, order, preferred_element_type=jnp.float32)
    tile_rows = jnp.concatenate([sorted_rows[8 * i:8 * i + 8, :] for i in range(12)], axis=1).astype(jnp.bfloat16)
    products = jnp.dot(tile_rows, ops_mat[...], preferred_element_type=jnp.float32)
    pairs = []
    for k in range(4):
        chosen = jnp.zeros((8, 128), jnp.float32)
        for w in range(4):
            chosen = jnp.where(weight_tiles[k] == w, products[:, w * 128:(w + 1) * 128], chosen)
        pairs.append(chosen)
    values = jnp.concatenate(pairs, axis=0)
    high = values.astype(jnp.bfloat16).astype(jnp.float32)
    middle = (values - high).astype(jnp.bfloat16).astype(jnp.float32)
    rest = values - high - middle
    stacked = jnp.concatenate([high, middle, rest, jnp.zeros((32, 128), jnp.float32)], axis=0).astype(jnp.bfloat16)
    sent[...] = labels[...] + jnp.dot(spread[...].astype(jnp.bfloat16), stacked, preferred_element_type=jnp.float32)

    gossip_wait(3)
    all_copies = []
    for d in far_order:
        owner = lax.rem(gx + d, n_gx)
        copy = remote(
            sent.at[pl.ds(pl.multiple_of(owner * 8, 8), 8), :], received.at[gx],
            all_send.at[0], all_recv.at[0], (g, owner, gy),
        )
        copy.start()
    received[gx] = sent[pl.ds(pl.multiple_of(gx * 8, 8), 8), :]

    around = [(dx, dr) for dx in (-1, 0, 1) for dr in (-1, 0, 1) if (dx, dr) != (0, 0)]

    def neighbour(dx, dr):
        there = lax.rem(rank + (n_rank + dr), n_rank)
        return (there // n_gy, lax.rem(gx + (n_gx + dx), n_gx), lax.rem(there, n_gy))

    def slot_of(dx, dr):
        return around.index((dx, dr))

    for dx, dr in around:
        remote(
            wave_ref, near_wave.at[slot_of(-dx, -dr)], wave_send.at[0], wave_recv.at[0], neighbour(dx, dr)
        ).start()

    def second_rate(x, carry):
        halo = ym2[x + 1]
        for zt in range(ZT):
            _, rates = rate_tile(pred, x, zt, halo)
            part = pl.ds(8 * zt, 8)
            for f in range(5):
                base_sum[f, x, part, :] = base_sum[f, x, part, :] + (0.5 * LES_STEP) * rates[f]
        return carry

    lax.fori_loop(0, CX, second_rate, 0)
    store_les = pltpu.make_async_copy(base_sum, les_out, local_sems.at[0])
    store_les.start()

    others = received.at[0:n_gx - 1]
    pltpu.make_async_copy(others, others, all_recv.at[0]).wait()
    tags = jnp.concatenate([jnp.sum(received[h:h + 16], axis=0)[7:8, :] for h in (0, 16)], axis=1)
    tags = jnp.broadcast_to(tags, (24, 256))
    line = lax.broadcasted_iota(jnp.int32, (24, 256), 0)
    column = lax.broadcasted_iota(jnp.int32, (24, 256), 1)
    lands = tags + (8 * (column & 3) - 1 - line).astype(jnp.float32)
    gather = jnp.where((tags > 0.5) & (jnp.abs(lands) < 0.5), 1.0, 0.0).astype(jnp.bfloat16)
    arrived = received[...].reshape(n_gx * 8, 128)
    high = arrived.astype(jnp.bfloat16).astype(jnp.float32)
    middle = (arrived - high).astype(jnp.bfloat16).astype(jnp.float32)
    source_lines = jnp.zeros((24, 128), jnp.float32)
    for part in (arrived - high - middle, middle, high):
        source_lines = source_lines + jnp.dot(gather, part.astype(jnp.bfloat16), preferred_element_type=jnp.float32)
    own_source[...] = source_lines
    for i, dr in ((0, -1), (1, 1)):
        remote(own_source, near_source.at[1 - i], src_send.at[0], src_recv.at[0], neighbour(0, dr)).start()

    pltpu.make_async_copy(near_wave, near_wave, wave_recv.at[0]).wait()
    wide_row = lax.broadcasted_iota(jnp.int32, (24, 256), 0)
    wide_lane = lax.broadcasted_iota(jnp.int32, (24, 256), 1)

    def flag(yes):
        return yes.astype(jnp.int32).astype(jnp.float32)

    inside = jnp.where(wide_row < 8, flag(gx > 0), jnp.where(wide_row >= 16, flag(gx < n_gx - 1), 1.0))
    inside = inside * jnp.where(
        wide_lane < 128, 1.0, jnp.where(wide_lane < 192, flag(rank < n_rank - 1), flag(rank > 0))
    )
    column = jnp.where(wide_lane < 192, wide_lane, wide_lane - 256) + rank * 128
    inverse_radius = 1.0 / (column.astype(jnp.float32) + 0.5)

    def assemble(block):
        strips = []
        for dx in (-1, 0, 1):
            side = jnp.where(lane < 64, block(dx, 1), block(dx, -1))
            strips.append(jnp.concatenate([block(dx, 0), side], axis=1))
        return jnp.concatenate(strips, axis=0) * inside

    def wave_block(f):
        return lambda dx, dr: wave_ref[f] if (dx, dr) == (0, 0) else near_wave[slot_of(dx, dr), f]

    now = [assemble(wave_block(f)) for f in range(3)]
    pltpu.make_async_copy(near_source, near_source, src_recv.at[0]).wait()
    beside = jnp.where(wide_lane[:, 0:128] < 64, near_source[1], near_source[0])
    source = jnp.concatenate([own_source[...], beside], axis=1) * inside
    for _ in range(2):
        rate_one = wave_rates(now, source, inverse_radius)
        ahead = [(v + WAVE_STEP * r) * inside for v, r in zip(now, rate_one)]
        rate_two = wave_rates(ahead, source, inverse_radius)
        now = [(v + (0.5 * WAVE_STEP) * (a + b)) * inside for v, a, b in zip(now, rate_one, rate_two)]
    for f in range(3):
        wave_out[f] = now[f][8:16, 0:128]

    for copy in sum(x_first + x_second, first + second):
        copy.wait_send()
    pltpu.make_async_copy(others, others, all_send.at[0]).wait()
    pltpu.make_async_copy(near_wave, near_wave, wave_send.at[0]).wait()
    pltpu.make_async_copy(near_source, near_source, src_send.at[0]).wait()
    store_les.wait()


def hand_on(les_in, wave_in, les_out, wave_out, les_buf, wave_buf, in_sems, out_sems):
    legs = [(wave_in, wave_buf, wave_out)] + [(les_in.at[f], les_buf.at[f], les_out.at[f]) for f in range(5)]
    into = [pltpu.make_async_copy(a, b, in_sems.at[i]) for i, (a, b, _) in enumerate(legs)]
    out = [pltpu.make_async_copy(b, c, out_sems.at[i]) for i, (_, b, c) in enumerate(legs)]
    for copy in into:
        copy.start()
    for one, two in zip(into, out):
        one.wait()
        two.start()
    for copy in out:
        copy.wait()


def on_device(sizes, les_state, wave_state, restriction_ops, pair_owner, pair_slot, pair_weight, tile_mask):
    n_gx = sizes[1]
    tile_len, op_count, width = restriction_ops.shape
    ops_flat = restriction_ops.reshape(tile_len * op_count, width)
    rounds = max(1, (n_gx // 2).bit_length() - 1)
    far_order = sorted(range(1, n_gx), key=lambda d: -(2 * min(d // 8, 4 - d // 8) + min(d % 8, 8 - d % 8)))
    f32, i32, bf16 = jnp.float32, jnp.int32, jnp.bfloat16
    vmem, smem, dma = pltpu.VMEM, pltpu.SMEM, pltpu.SemaphoreType.DMA
    scratch = [
        vmem((5, 12, 64, 128), f32), vmem((5, 12, 64, 128), f32), vmem((5, 8, 48, 128), f32),
        vmem((12, 48, 128), f32), vmem((8, 64, 128), f32), vmem((8, 48, 128), f32),
        vmem((10, 64, 128), f32), vmem((10, 48, 128), f32), vmem((8, 64, 128), f32),
        vmem((3, 8, 128), f32), smem((1, 4, 8), i32), smem((1, 4, 8), i32), smem((1, 4, 8), i32), smem((1, 8), i32),
        vmem((2, CHUNKS, 5, CHUNK_ROWS, 128), i32), vmem((2, CHUNKS, 5, CHUNK_ROWS, 128), i32),
        vmem((2, CHUNKS, 5, CHUNK_ROWS, 128), i32), vmem((2, CHUNKS, 5, CHUNK_ROWS, 128), i32),
        vmem((10, 8, 128), i32), vmem((10, 8, 128), i32), vmem((10, 8, 128), i32), vmem((10, 8, 128), i32),
        vmem((8, 8, 128), f32), vmem((2, 8, 8, 128), f32), vmem((8, 8, 128), f32), vmem((2, 10, 8, 128), f32),
        vmem((10, 8, 128), f32),
        vmem((2, 8, 128), f32), vmem((2, 8, 128), f32), vmem((8, 128), f32), vmem((2, 8, 128), f32),
        vmem((8, 8, 128), f32),
        vmem((CX * CZ, 128), f32), vmem((6144, 128), bf16), vmem((512, 128), f32), vmem((1536, 512), bf16),
        vmem((n_gx * 8, 128), f32), vmem((n_gx * 8, 128), f32), vmem((4, 8, 128), i32),
        vmem((n_gx * 8, 128), f32), vmem((n_gx, 8, 128), f32), vmem((24, 128), f32),
        vmem((2, 24, 128), f32), vmem((8, 3, 8, 128), f32),
        dma((9,)), dma((4 * CHUNKS,)), dma((4 * CHUNKS,)), dma((3,)), dma((3,)), dma((11,)), dma((11,)), dma((1,)), dma((1,)), dma((1,)), dma((1,)),
        dma((1,)), dma((1,)), pltpu.SemaphoreType.REGULAR((rounds,)),
    ]
    any_space = pl.BlockSpec(memory_space=pl.ANY)
    in_vmem = pl.BlockSpec(memory_space=pltpu.VMEM)
    results = pl.pallas_call(
        functools.partial(kernel, sizes, far_order),
        out_shape=(
            jax.ShapeDtypeStruct(les_state.shape, f32),
            jax.ShapeDtypeStruct(wave_state.shape, f32),
        ),
        in_specs=[any_space] * 7,
        out_specs=(any_space, in_vmem),
        scratch_shapes=scratch,
        compiler_params=pltpu.CompilerParams(collective_id=0, has_side_effects=True),
        name="jet_step",
    )(les_state, wave_state, ops_flat, *(a.swapaxes(1, 2) for a in (pair_owner, pair_slot, pair_weight)), tile_mask)
    return pl.pallas_call(
        hand_on,
        out_shape=tuple(jax.ShapeDtypeStruct(r.shape, f32) for r in results),
        in_specs=[any_space] * 2,
        out_specs=(any_space,) * 2,
        scratch_shapes=[vmem(les_state.shape, f32), vmem(wave_state.shape, f32), dma((6,)), dma((6,))],
        name="hand_on",
    )(*results)


def solution(mesh):
    sizes = (mesh.shape["group"], mesh.shape["gx"], mesh.shape["gy"])
    return jax.shard_map(
        functools.partial(on_device, sizes),
        mesh=mesh,
        in_specs=(
            P(None, "gx", "group", "gy"),
            P(None, "gx", ("group", "gy")),
            P(),
            P(("group", "gy"), "gx", None),
            P(("group", "gy"), "gx", None),
            P(("group", "gy"), "gx", None),
            P(("group", "gy"), "gx"),
        ),
        out_specs=(P(None, "gx", "group", "gy"), P(None, "gx", ("group", "gy"))),
        check_vma=False,
    )
```

```python
import functools

import jax
import jax.numpy as jnp
from jax import lax
from jax.experimental import pallas as pl
from jax.experimental.pallas import tpu as pltpu
from jax.sharding import PartitionSpec as P

MESH = pl.DeviceIdType.MESH
VISCOSITY = 0.05
LES_STEP = 0.2
WAVE_STEP = 0.3
CX, CZ, CY = 8, 48, 128
ZT = CZ // 8
CHUNKS = 3
CHUNK_ROWS = CZ // CHUNKS
CHUNK_TILES = ZT // CHUNKS
OFFSETS = (1.0, 0.0, 0.0, 0.0, 1.0)
STATE_SCALE = (130816.0, 65408.0, 65408.0, 65408.0, 130816.0)
PRED_SCALE = (24576.0,) * 5


def encode(value, offset, scale):
    return ((value - offset) * scale + 32768.5).astype(jnp.int32)


def decode(code, offset, scale):
    return code.astype(jnp.float32) * (1.0 / scale) + (offset - 32768.0 / scale)


def pair_words(first, second, offset, scale):
    return (encode(first, offset, scale) << 16) | encode(second, offset, scale)


def split_words(words, offset, scale):
    first = decode(lax.shift_right_logical(words, 16), offset, scale)
    return first, decode(words & 0xFFFF, offset, scale)


def lanes():
    return lax.broadcasted_iota(jnp.int32, (8, 128), 1)


def rows():
    return lax.broadcasted_iota(jnp.int32, (8, 128), 0)


def roll_lane(tile, shift):
    shift = shift % tile.shape[1]
    return pltpu.roll(tile, shift, 1) if shift else tile


def roll_row(tile, shift):
    shift = shift % tile.shape[0]
    return pltpu.roll(tile, shift, 0) if shift else tile


def y_shifts(tile, halo, slot, reach):
    lane = lanes()
    halo = roll_lane(halo, -(4 * slot + 2))
    shifts = []
    for s in reach:
        before = roll_lane(jnp.where(lane >= 128 - s, halo, tile), s)
        after = roll_lane(jnp.where(lane < s, halo, tile), -s)
        shifts.append((before, after))
    return shifts


def rate_tile(buf, x, zt, halo):
    base = 8 + 8 * zt

    def at(f, dx, dz):
        return buf[f, x + (2 + dx), pl.ds(base + dz, 8), :]

    centre, grads, laps = [], [], []
    for f in range(5):
        c = at(f, 0, 0)
        xm1, xp1, zm1, zp1 = at(f, -1, 0), at(f, 1, 0), at(f, 0, -1), at(f, 0, 1)
        (ym1, yp1), (ym2, yp2) = y_shifts(c, halo, f * ZT + zt, (1, 2))
        dx = 8.0 * (xp1 - xm1) - (at(f, 2, 0) - at(f, -2, 0))
        dz = 8.0 * (zp1 - zm1) - (at(f, 0, 2) - at(f, 0, -2))
        dy = 8.0 * (yp1 - ym1) - (yp2 - ym2)
        centre.append(c)
        grads.append((dx, dz, dy))
        laps.append(((xm1 + xp1) + (zm1 + zp1)) + (ym1 + yp1) - 6.0 * c if 1 <= f <= 3 else None)
    rho, u0, u1, u2, p = centre
    div = grads[1][0] + grads[2][1] + grads[3][2]
    inverse = 1.0 / rho

    def advect(f):
        return u0 * grads[f][0] + u1 * grads[f][1] + u2 * grads[f][2]

    twelfth = -1.0 / 12.0
    rates = [(advect(0) + rho * div) * twelfth]
    for d in range(3):
        rates.append((advect(1 + d) + grads[4][d] * inverse) * twelfth + VISCOSITY * laps[1 + d])
    rates.append((advect(4) + 1.4 * (p * div)) * twelfth)
    return centre, rates


def packed_products(tile):
    momentum = tile * roll_lane(tile, -72)
    return (
        momentum * roll_lane(tile, -24),
        momentum * roll_lane(tile, -48),
        momentum * roll_lane(tile, -72),
    )


def wave_rates(state, source, inverse_radius):
    p, ux, ur = state

    def d(f, axis):
        size = f.shape[axis]
        one = pltpu.roll(f, size - 1, axis) - pltpu.roll(f, 1, axis)
        two = pltpu.roll(f, size - 2, axis) - pltpu.roll(f, 2, axis)
        return (8.0 * one - two) * (1.0 / 12.0)

    return (source - d(ux, 0) - d(ur, 1) - ur * inverse_radius, -d(p, 0), -d(p, 1))


def kernel(
    sizes, far_order,
    les_ref, wave_in, ops_ref, owner_in, slot_in, weight_in, mask_in,
    les_out, wave_out,
    state, pred, base_sum, s00, s11, s22, s01, s02, s12,
    wave_ref, owner_ref, slot_ref, weight_ref, mask_ref,
    xs1, xr1, xs2, xr2, zs1, zr1, zs2, zr2, ys1, yr1, ys2, yr2, ym2,
    exz_s, exz_r, ezy_s, ezy_r, ezy_x,
    light, ops_raw, ops_wide, ops_mat, spread, labels, weight_tiles,
    sent, received, own_source, near_source, near_wave,
    local_sems, x_send, x_recv, send1, recv1, send2, recv2, wave_send, wave_recv, all_send, all_recv, src_send, src_recv, gossip,
):
    n_group, n_gx, n_gy = sizes
    g, gx, gy = lax.axis_index("group"), lax.axis_index("gx"), lax.axis_index("gy")
    rank = g * n_gy + gy
    n_rank = n_group * n_gy
    gx_low, gx_high = lax.rem(gx + (n_gx - 1), n_gx), lax.rem(gx + 1, n_gx)
    gy_low, gy_high = lax.rem(gy + (n_gy - 1), n_gy), lax.rem(gy + 1, n_gy)
    other = 1 - g
    lane, row = lanes(), rows()

    def remote(src, dst, send_sem, recv_sem, device):
        return pltpu.make_async_remote_copy(
            src_ref=src, dst_ref=dst, send_sem=send_sem, recv_sem=recv_sem, device_id=device, device_id_type=MESH
        )

    barrier = pltpu.get_barrier_semaphore()
    for device in ((g, gx_low, gy), (g, gx_high, gy), (other, gx, gy), (g, gx, gy_low), (g, gx, gy_high)):
        pl.semaphore_signal(barrier, inc=1, device_id=device, device_id_type=MESH)

    def load(src, dst, i):
        copy = pltpu.make_async_copy(src, dst, local_sems.at[i])
        copy.start()
        return copy

    def face_rows(chunk):
        return slice(CHUNK_ROWS * chunk, CHUNK_ROWS * (chunk + 1)), slice(
            8 + CHUNK_ROWS * chunk, 8 + CHUNK_ROWS * (chunk + 1)
        )

    load_faces = []
    for chunk in range(CHUNKS):
        theirs, mine = face_rows(chunk)
        load_faces.append(
            [
                load(les_ref.at[:, 0:2, theirs], state.at[:, 2:4, mine, :], 7 + 2 * chunk),
                load(les_ref.at[:, 6:8, theirs], state.at[:, 8:10, mine, :], 8 + 2 * chunk),
            ]
        )
    load_inner = load(les_ref.at[:, 2:6], state.at[:, 4:8, 8:56, :], 0)
    load_small = [
        load(owner_in, owner_ref, 1),
        load(slot_in, slot_ref, 2),
        load(weight_in, weight_ref, 3),
        load(mask_in, mask_ref, 4),
        load(wave_in, wave_ref, 5),
    ]
    load_ops = load(ops_ref, ops_raw, 6)
    for copy in load_faces[0]:
        copy.wait()

    def gossip_send(r):
        if r < gossip.shape[0]:
            d = 1 << r
            for target in (lax.rem(gx + d, n_gx), lax.rem(gx + (n_gx - d), n_gx)):
                pl.semaphore_signal(gossip.at[r], inc=1, device_id=(g, target, gy), device_id_type=MESH)

    def gossip_wait(r):
        if r < gossip.shape[0]:
            pl.semaphore_wait(gossip.at[r], 2)

    def x_pack(buf, out, scales, chunk):
        part = slice(8 + CHUNK_ROWS * chunk, 8 + CHUNK_ROWS * (chunk + 1))
        for f in range(5):
            for side, first in ((0, 2), (1, 8)):
                out[side, chunk, f] = pair_words(
                    buf[f, first, part, :], buf[f, first + 1, part, :], OFFSETS[f], scales[f]
                )

    def x_unpack(buf, words, scales, chunk):
        part = slice(8 + CHUNK_ROWS * chunk, 8 + CHUNK_ROWS * (chunk + 1))
        for f in range(5):
            for side, first in ((0, 0), (1, 10)):
                one, two = split_words(words[side, chunk, f], OFFSETS[f], scales[f])
                buf[f, first, part, :] = one
                buf[f, first + 1, part, :] = two

    def x_copies(sent_words, words, stage, chunk):
        first = 2 * (CHUNKS * stage + chunk)
        return [
            remote(
                sent_words.at[0, chunk], words.at[1, chunk], x_send.at[first], x_recv.at[first + 1], (g, gx_low, gy)
            ),
            remote(
                sent_words.at[1, chunk], words.at[0, chunk], x_send.at[first + 1], x_recv.at[first], (g, gx_high, gy)
            ),
        ]

    def ends(buf, f, x):
        return jnp.where(row < 4, buf[f, x + 2, 8:16, :], buf[f, x + 2, 48:56, :])

    def z_pack(buf, out, scales):
        for f in range(5):
            for j in range(2):
                a = pair_words(ends(buf, f, 2 * j), ends(buf, f, 2 * j + 4), OFFSETS[f], scales[f])
                b = pair_words(ends(buf, f, 2 * j + 1), ends(buf, f, 2 * j + 5), OFFSETS[f], scales[f])
                out[2 * f + j] = jnp.where((row < 2) | (row >= 6), a, roll_row(b, 4))

    def z_unpack(buf, words, scales):
        for f in range(5):
            for j in range(2):
                word = words[2 * f + j]
                for i, part in enumerate((word, roll_row(word, 4))):
                    for x, tile in zip((2 * j + i, 2 * j + i + 4), split_words(part, OFFSETS[f], scales[f])):
                        buf[f, x + 2, 0:8, :] = tile
                        buf[f, x + 2, 56:64, :] = tile

    def y_add(packed, tile, slot):
        return jnp.where((lane >> 2) == slot, roll_lane(tile, 4 * slot + 2), packed)

    def y_merge(from_low, from_high):
        return jnp.where((lane & 2) == 0, from_low, from_high)

    def y_pack(x, carry):
        packed = jnp.zeros((8, 128), jnp.float32)
        for f in range(5):
            for zt in range(ZT):
                packed = y_add(packed, state[f, x + 2, pl.ds(8 + 8 * zt, 8), :], f * ZT + zt)
        ys1[x] = packed
        return carry

    x_pack(state, xs1, STATE_SCALE, 0)
    pl.semaphore_wait(barrier, 5)
    gossip_send(0)
    x_first = [x_copies(xs1, xr1, 0, chunk) for chunk in range(CHUNKS)]
    x_second = [x_copies(xs2, xr2, 1, chunk) for chunk in range(CHUNKS)]
    first = [
        remote(zs1, zr1, send1.at[0], recv1.at[0], (other, gx, gy)),
        remote(ys1, yr1.at[1], send1.at[1], recv1.at[2], (g, gx, gy_low)),
        remote(ys1, yr1.at[0], send1.at[2], recv1.at[1], (g, gx, gy_high)),
    ]
    for copy in x_first[0]:
        copy.start()
    for chunk in range(1, CHUNKS):
        for copy in load_faces[chunk]:
            copy.wait()
        x_pack(state, xs1, STATE_SCALE, chunk)
        for copy in x_first[chunk]:
            copy.start()
    load_inner.wait()
    z_pack(state, zs1, STATE_SCALE)
    first[0].start()
    lax.fori_loop(0, CX, y_pack, 0)
    first[1].start()
    first[2].start()

    load_ops.wait()
    for copy in load_small:
        copy.wait()

    def widen(i, carry):
        part = pl.ds(pl.multiple_of(i * 512, 512), 512)
        ops_wide[...] = ops_raw[part, :].astype(jnp.float32)
        for w in range(4):
            ops_mat[pl.ds(pl.multiple_of(i * 128, 128), 128), w * 128:(w + 1) * 128] = (
                ops_wide[pl.ds(w, 128, stride=4), :].astype(jnp.bfloat16)
            )
        return carry

    lax.fori_loop(0, 12, widen, 0)
    pair_lane = lane & 31
    owners = jnp.full((8, 128), -99, jnp.int32)
    first_slot, second_slot, seen = (jnp.zeros((8, 128), jnp.int32) for _ in range(3))
    for k in range(4):
        weights = jnp.zeros((8, 128), jnp.int32)
        for x in range(8):
            owner = owner_ref[0, k, x]
            owners = jnp.where((pair_lane == k * 8 + x) & (lane < 96), owner, owners)
            hit = lane == owner
            first_slot = jnp.where(hit & (seen == 0), slot_ref[0, k, x] + 1, first_slot)
            second_slot = jnp.where(hit & (seen == 1), slot_ref[0, k, x] + 1, second_slot)
            seen = jnp.where(hit, seen + 1, seen)
            weights = jnp.where(row == x, weight_ref[0, k, x], weights)
        weight_tiles[k] = weights
    rank_of = jnp.zeros((8, 128), jnp.int32)
    for k in range(4):
        for x in range(8):
            earlier = (owners == owner_ref[0, k, x]) & (pair_lane > k * 8 + x)
            rank_of = rank_of + jnp.where(earlier, 1, 0)
    own_lane = 8 * lax.rem(gx, 16)
    first_slot = pltpu.roll(first_slot.astype(jnp.float32), own_lane + 1, 1)
    second_slot = pltpu.roll(second_slot.astype(jnp.float32), own_lane + 5, 1)
    first_here = (row == 7) & (lane >= own_lane) & (lane < own_lane + 3)
    second_here = (row == 7) & (lane >= own_lane + 4) & (lane < own_lane + 7)
    for d in range(n_gx):
        near = (owners >= d - 1) & (owners <= d + 1)
        spread[d * 8:(d + 1) * 8, :] = jnp.where(near & (owners - (d - 1) + 4 * rank_of == row), 1.0, 0.0)
        slots = jnp.where(second_here, roll_lane(second_slot, -d), 0.0)
        labels[d * 8:(d + 1) * 8, :] = jnp.where(first_here, roll_lane(first_slot, -d), slots)

    gossip_wait(0)
    gossip_send(1)
    first[0].wait_recv()
    z_unpack(state, zr1, STATE_SCALE)
    first[1].wait_recv()
    first[2].wait_recv()

    def first_rate(x, tiles):
        halo = y_merge(yr1[0, x], yr1[1, x])
        packed = jnp.zeros((8, 128), jnp.float32) if tiles[0] == 0 else ys2[x]
        for zt in tiles:
            centre, rates = rate_tile(state, x, zt, halo)
            part = pl.ds(8 * zt, 8)
            inner = pl.ds(8 + 8 * zt, 8)
            new = []
            for f in range(5):
                value = centre[f] + LES_STEP * rates[f]
                pred[f, x + 2, inner, :] = value
                base_sum[f, x, part, :] = centre[f] + (0.5 * LES_STEP) * rates[f]
                packed = y_add(packed, value, f * ZT + zt)
                new.append(value)
            rho, u0, u1, u2, _ = new
            m0, m1 = rho * u0, rho * u1
            s00[x + 2, part, :] = m0 * u0
            s01[x + 1, inner, :] = m0 * u1
            s02[x + 1, part, :] = m0 * u2
            s11[x, inner, :] = m1 * u1
            s12[x, inner, :] = m1 * u2
            s22[x, part, :] = rho * u2 * u2
        ys2[x] = packed

    def rate_inner(x, carry):
        first_rate(x, tuple(range(ZT)))
        return carry

    second = [
        remote(zs2, zr2, send2.at[0], recv2.at[0], (other, gx, gy)),
        remote(ys2, yr2.at[1, 1:9], send2.at[1], recv2.at[2], (g, gx, gy_low)),
        remote(ys2, yr2.at[0, 1:9], send2.at[2], recv2.at[1], (g, gx, gy_high)),
        remote(ezy_s, ezy_r.at[1], send2.at[3], recv2.at[4], (other, gx, gy_low)),
        remote(ezy_s, ezy_r.at[0], send2.at[4], recv2.at[3], (other, gx, gy_high)),
        remote(exz_s.at[0], exz_r.at[1], send2.at[5], recv2.at[6], (other, gx_low, gy)),
        remote(exz_s.at[1], exz_r.at[0], send2.at[6], recv2.at[5], (other, gx_high, gy)),
        remote(ys2.at[0], yr2.at[1, 9], send2.at[7], recv2.at[10], (g, gx_low, gy_low)),
        remote(ys2.at[0], yr2.at[0, 9], send2.at[8], recv2.at[9], (g, gx_low, gy_high)),
        remote(ys2.at[7], yr2.at[1, 0], send2.at[9], recv2.at[8], (g, gx_high, gy_low)),
        remote(ys2.at[7], yr2.at[0, 0], send2.at[10], recv2.at[7], (g, gx_high, gy_high)),
    ]
    lax.fori_loop(2, 6, rate_inner, 0)
    gossip_wait(1)
    gossip_send(2)
    for chunk in range(CHUNKS):
        for copy in x_first[chunk]:
            copy.wait_recv()
        x_unpack(state, xr1, STATE_SCALE, chunk)
        for x in (6, 7, 0, 1):
            first_rate(x, tuple(range(CHUNK_TILES * chunk, CHUNK_TILES * (chunk + 1))))
        if chunk == CHUNKS - 1:
            for side in range(2):
                x = 7 * side
                exz_s[side] = ends(pred, 0, x) * ends(pred, 1, x) * ends(pred, 2, x)
            for copy in second[5:]:
                copy.start()
        x_pack(pred, xs2, PRED_SCALE, chunk)
        for copy in x_second[chunk]:
            copy.start()

    z_pack(pred, zs2, PRED_SCALE)
    for copy in second[:3]:
        copy.start()
    edge = jnp.zeros((8, 128), jnp.float32)
    for x in range(8):
        product = packed_products(ys2[x])[1]
        both = jnp.where(lane < 4, product, roll_lane(product, -16))
        edge = jnp.where((lane >> 3) == x, roll_lane(both, 8 * x), edge)
    ezy_s[...] = edge
    second[3].start()
    second[4].start()
    gossip_wait(2)
    gossip_send(3)

    second[0].wait_recv()
    z_unpack(pred, zr2, PRED_SCALE)
    for x in range(8):
        for part in (slice(0, 8), slice(56, 64)):
            rho, u0, u1, u2 = (pred[f, x + 2, part, :] for f in range(4))
            m1 = rho * u1
            s01[x + 1, part, :] = m1 * u0
            s11[x, part, :] = m1 * u1
            s12[x, part, :] = m1 * u2
    for copy in second[1:5]:
        copy.wait_recv()
    for x in range(8):
        ym2[x + 1] = y_merge(yr2[0, x + 1], yr2[1, x + 1])
    corners = y_merge(ezy_r[0], ezy_r[1])
    for x in range(8):
        ezy_x[x] = roll_lane(corners, -8 * x)

    def lighthill(x, carry):
        along_x = packed_products(ym2[x + 2])[0] - packed_products(ym2[x])[0]
        _, s12_halo, square = packed_products(ym2[x + 1])
        corner = ezy_x[x]
        next_tile = jnp.where(lane >= 20, roll_lane(corner, 20), roll_lane(s12_halo, -4))
        last_tile = jnp.where(lane < 4, roll_lane(corner, -4), roll_lane(s12_halo, 4))
        after = roll_row(jnp.where(row == 0, next_tile, s12_halo), -1)
        before = roll_row(jnp.where(row == 7, last_tile, s12_halo), 1)
        cross = along_x + (after - before)
        keep = mask_ref[0, x].astype(jnp.float32)
        for zt in range(ZT):
            part = pl.ds(8 * zt, 8)

            def z(ref, index, dz):
                return ref[index, pl.ds(8 + 8 * zt + dz, 8), :]

            direct = s00[x + 4, part, :] + s00[x, part, :] - 2.0 * s00[x + 2, part, :]
            direct = direct + (z(s11, x, 2) + z(s11, x, -2) - 2.0 * z(s11, x, 0))
            tile = s22[x, part, :]
            ((before, after),) = y_shifts(tile, square, zt, (2,))
            direct = direct + (before + after - 2.0 * tile)
            mixed = (z(s01, x + 2, 1) - z(s01, x + 2, -1)) - (z(s01, x, 1) - z(s01, x, -1))
            tile = (s02[x + 2, part, :] - s02[x, part, :]) + (z(s12, x, 1) - z(s12, x, -1))
            ((before, after),) = y_shifts(tile, cross, zt, (1,))
            mixed = mixed + (after - before)
            light[pl.ds(pl.multiple_of(x * CZ + 8 * zt, 8), 8), :] = (0.25 * direct + 0.5 * mixed) * keep
        return carry

    lax.fori_loop(2, 6, lighthill, 0)
    for chunk in range(CHUNKS):
        for copy in x_second[chunk]:
            copy.wait_recv()
        x_unpack(pred, xr2, PRED_SCALE, chunk)
    for index in (0, 1, 10, 11):
        s00[index] = pred[0, index, 8:56, :] * pred[1, index, 8:56, :] * pred[1, index, 8:56, :]
    for index, layer in ((0, 1), (9, 10)):
        m0 = pred[0, layer, 8:56, :] * pred[1, layer, 8:56, :]
        s01[index, 8:56, :] = m0 * pred[2, layer, 8:56, :]
        s02[index] = m0 * pred[3, layer, 8:56, :]
    for copy in second[5:]:
        copy.wait_recv()
    for index in (0, 9):
        ym2[index] = y_merge(yr2[0, index], yr2[1, index])
    for side, index in ((0, 0), (1, 9)):
        s01[index, 0:8, :] = exz_r[side]
        s01[index, 56:64, :] = exz_r[side]
    lax.fori_loop(0, 4, lambda j, carry: lighthill(lax.rem(j + 6, 8), carry), 0)

    pieces = []
    for zp in range(12):
        one, two = (
            light[pl.ds(4 * zp + 2 * i, 8, stride=CZ), :] + light[pl.ds(4 * zp + 2 * i + 1, 8, stride=CZ), :]
            for i in range(2)
        )
        one = one + roll_lane(one, -1)
        two = two + roll_lane(two, 1)
        pieces.append(jnp.where((lane & 1) == 0, one, two))
    merged = jnp.concatenate(pieces, axis=0).astype(jnp.bfloat16)
    source_lane = lax.broadcasted_iota(jnp.int32, (128, 128), 0)
    target_lane = lax.broadcasted_iota(jnp.int32, (128, 128), 1)
    order = jnp.where(target_lane == (source_lane & 1) * 64 + (source_lane >> 1), 1.0, 0.0).astype(jnp.bfloat16)
    sorted_rows = jnp.dot(merged, order, preferred_element_type=jnp.float32)
    tile_rows = jnp.concatenate([sorted_rows[8 * i:8 * i + 8, :] for i in range(12)], axis=1).astype(jnp.bfloat16)
    products = jnp.dot(tile_rows, ops_mat[...], preferred_element_type=jnp.float32)
    pairs = []
    for k in range(4):
        chosen = jnp.zeros((8, 128), jnp.float32)
        for w in range(4):
            chosen = jnp.where(weight_tiles[k] == w, products[:, w * 128:(w + 1) * 128], chosen)
        pairs.append(chosen)
    values = jnp.concatenate(pairs, axis=0)
    high = values.astype(jnp.bfloat16).astype(jnp.float32)
    middle = (values - high).astype(jnp.bfloat16).astype(jnp.float32)
    rest = values - high - middle
    stacked = jnp.concatenate([high, middle, rest, jnp.zeros((32, 128), jnp.float32)], axis=0).astype(jnp.bfloat16)
    sent[...] = labels[...] + jnp.dot(spread[...].astype(jnp.bfloat16), stacked, preferred_element_type=jnp.float32)

    gossip_wait(3)
    all_copies = []
    for d in far_order:
        owner = lax.rem(gx + d, n_gx)
        copy = remote(
            sent.at[pl.ds(pl.multiple_of(owner * 8, 8), 8), :], received.at[gx],
            all_send.at[0], all_recv.at[0], (g, owner, gy),
        )
        copy.start()
    received[gx] = sent[pl.ds(pl.multiple_of(gx * 8, 8), 8), :]

    around = [(dx, dr) for dx in (-1, 0, 1) for dr in (-1, 0, 1) if (dx, dr) != (0, 0)]

    def neighbour(dx, dr):
        there = lax.rem(rank + (n_rank + dr), n_rank)
        return (there // n_gy, lax.rem(gx + (n_gx + dx), n_gx), lax.rem(there, n_gy))

    def slot_of(dx, dr):
        return around.index((dx, dr))

    for dx, dr in around:
        remote(
            wave_ref, near_wave.at[slot_of(-dx, -dr)], wave_send.at[0], wave_recv.at[0], neighbour(dx, dr)
        ).start()

    def second_rate(x, carry):
        halo = ym2[x + 1]
        for zt in range(ZT):
            _, rates = rate_tile(pred, x, zt, halo)
            part = pl.ds(8 * zt, 8)
            for f in range(5):
                les_out[f, x, part, :] = base_sum[f, x, part, :] + (0.5 * LES_STEP) * rates[f]
        return carry

    lax.fori_loop(0, CX, second_rate, 0)

    others = received.at[0:n_gx - 1]
    pltpu.make_async_copy(others, others, all_recv.at[0]).wait()
    tags = jnp.concatenate([jnp.sum(received[h:h + 16], axis=0)[7:8, :] for h in (0, 16)], axis=1)
    tags = jnp.broadcast_to(tags, (24, 256))
    line = lax.broadcasted_iota(jnp.int32, (24, 256), 0)
    column = lax.broadcasted_iota(jnp.int32, (24, 256), 1)
    lands = tags + (8 * (column & 3) - 1 - line).astype(jnp.float32)
    gather = jnp.where((tags > 0.5) & (jnp.abs(lands) < 0.5), 1.0, 0.0).astype(jnp.bfloat16)
    arrived = received[...].reshape(n_gx * 8, 128)
    high = arrived.astype(jnp.bfloat16).astype(jnp.float32)
    middle = (arrived - high).astype(jnp.bfloat16).astype(jnp.float32)
    source_lines = jnp.zeros((24, 128), jnp.float32)
    for part in (arrived - high - middle, middle, high):
        source_lines = source_lines + jnp.dot(gather, part.astype(jnp.bfloat16), preferred_element_type=jnp.float32)
    own_source[...] = source_lines
    for i, dr in ((0, -1), (1, 1)):
        remote(own_source, near_source.at[1 - i], src_send.at[0], src_recv.at[0], neighbour(0, dr)).start()

    pltpu.make_async_copy(near_wave, near_wave, wave_recv.at[0]).wait()
    wide_row = lax.broadcasted_iota(jnp.int32, (24, 256), 0)
    wide_lane = lax.broadcasted_iota(jnp.int32, (24, 256), 1)

    def flag(yes):
        return yes.astype(jnp.int32).astype(jnp.float32)

    inside = jnp.where(wide_row < 8, flag(gx > 0), jnp.where(wide_row >= 16, flag(gx < n_gx - 1), 1.0))
    inside = inside * jnp.where(
        wide_lane < 128, 1.0, jnp.where(wide_lane < 192, flag(rank < n_rank - 1), flag(rank > 0))
    )
    column = jnp.where(wide_lane < 192, wide_lane, wide_lane - 256) + rank * 128
    inverse_radius = 1.0 / (column.astype(jnp.float32) + 0.5)

    def assemble(block):
        strips = []
        for dx in (-1, 0, 1):
            side = jnp.where(lane < 64, block(dx, 1), block(dx, -1))
            strips.append(jnp.concatenate([block(dx, 0), side], axis=1))
        return jnp.concatenate(strips, axis=0) * inside

    def wave_block(f):
        return lambda dx, dr: wave_ref[f] if (dx, dr) == (0, 0) else near_wave[slot_of(dx, dr), f]

    now = [assemble(wave_block(f)) for f in range(3)]
    pltpu.make_async_copy(near_source, near_source, src_recv.at[0]).wait()
    beside = jnp.where(wide_lane[:, 0:128] < 64, near_source[1], near_source[0])
    source = jnp.concatenate([own_source[...], beside], axis=1) * inside
    for _ in range(2):
        rate_one = wave_rates(now, source, inverse_radius)
        ahead = [(v + WAVE_STEP * r) * inside for v, r in zip(now, rate_one)]
        rate_two = wave_rates(ahead, source, inverse_radius)
        now = [(v + (0.5 * WAVE_STEP) * (a + b)) * inside for v, a, b in zip(now, rate_one, rate_two)]
    for f in range(3):
        wave_out[f] = now[f][8:16, 0:128]

    for copy in sum(x_first + x_second, first + second):
        copy.wait_send()
    pltpu.make_async_copy(others, others, all_send.at[0]).wait()
    pltpu.make_async_copy(near_wave, near_wave, wave_send.at[0]).wait()
    pltpu.make_async_copy(near_source, near_source, src_send.at[0]).wait()


def hand_on(les_in, wave_in, les_out, wave_out, sems):
    copies = [pltpu.make_async_copy(wave_in, wave_out, sems.at[5])]
    copies += [pltpu.make_async_copy(les_in.at[f], les_out.at[f], sems.at[f]) for f in range(5)]
    for copy in copies:
        copy.start()
    for copy in copies:
        copy.wait()


def on_device(sizes, les_state, wave_state, restriction_ops, pair_owner, pair_slot, pair_weight, tile_mask):
    n_gx = sizes[1]
    tile_len, op_count, width = restriction_ops.shape
    ops_flat = restriction_ops.reshape(tile_len * op_count, width)
    rounds = max(1, (n_gx // 2).bit_length() - 1)
    far_order = sorted(range(1, n_gx), key=lambda d: -(2 * min(d // 8, 4 - d // 8) + min(d % 8, 8 - d % 8)))
    f32, i32, bf16 = jnp.float32, jnp.int32, jnp.bfloat16
    vmem, smem, dma = pltpu.VMEM, pltpu.SMEM, pltpu.SemaphoreType.DMA
    scratch = [
        vmem((5, 12, 64, 128), f32), vmem((5, 12, 64, 128), f32), vmem((5, 8, 48, 128), f32),
        vmem((12, 48, 128), f32), vmem((8, 64, 128), f32), vmem((8, 48, 128), f32),
        vmem((10, 64, 128), f32), vmem((10, 48, 128), f32), vmem((8, 64, 128), f32),
        vmem((3, 8, 128), f32), smem((1, 4, 8), i32), smem((1, 4, 8), i32), smem((1, 4, 8), i32), smem((1, 8), i32),
        vmem((2, CHUNKS, 5, CHUNK_ROWS, 128), i32), vmem((2, CHUNKS, 5, CHUNK_ROWS, 128), i32),
        vmem((2, CHUNKS, 5, CHUNK_ROWS, 128), i32), vmem((2, CHUNKS, 5, CHUNK_ROWS, 128), i32),
        vmem((10, 8, 128), i32), vmem((10, 8, 128), i32), vmem((10, 8, 128), i32), vmem((10, 8, 128), i32),
        vmem((8, 8, 128), f32), vmem((2, 8, 8, 128), f32), vmem((8, 8, 128), f32), vmem((2, 10, 8, 128), f32),
        vmem((10, 8, 128), f32),
        vmem((2, 8, 128), f32), vmem((2, 8, 128), f32), vmem((8, 128), f32), vmem((2, 8, 128), f32),
        vmem((8, 8, 128), f32),
        vmem((CX * CZ, 128), f32), vmem((6144, 128), bf16), vmem((512, 128), f32), vmem((1536, 512), bf16),
        vmem((n_gx * 8, 128), f32), vmem((n_gx * 8, 128), f32), vmem((4, 8, 128), i32),
        vmem((n_gx * 8, 128), f32), vmem((n_gx, 8, 128), f32), vmem((24, 128), f32),
        vmem((2, 24, 128), f32), vmem((8, 3, 8, 128), f32),
        dma((7 + 2 * CHUNKS,)), dma((4 * CHUNKS,)), dma((4 * CHUNKS,)), dma((3,)), dma((3,)), dma((11,)), dma((11,)), dma((1,)), dma((1,)), dma((1,)), dma((1,)),
        dma((1,)), dma((1,)), pltpu.SemaphoreType.REGULAR((rounds,)),
    ]
    any_space = pl.BlockSpec(memory_space=pl.ANY)
    in_vmem = pl.BlockSpec(memory_space=pltpu.VMEM)
    results = pl.pallas_call(
        functools.partial(kernel, sizes, far_order),
        out_shape=(vmem(les_state.shape, f32), vmem(wave_state.shape, f32)),
        in_specs=[any_space] * 7,
        out_specs=(in_vmem, in_vmem),
        scratch_shapes=scratch,
        compiler_params=pltpu.CompilerParams(collective_id=0, has_side_effects=True),
        name="jet_step",
    )(les_state, wave_state, ops_flat, *(a.swapaxes(1, 2) for a in (pair_owner, pair_slot, pair_weight)), tile_mask)
    return pl.pallas_call(
        hand_on,
        out_shape=tuple(jax.ShapeDtypeStruct(r.shape, f32) for r in results),
        in_specs=[in_vmem] * 2,
        out_specs=(any_space,) * 2,
        scratch_shapes=[dma((6,))],
        name="hand_on",
    )(*(pltpu.with_memory_space_constraint(r, pltpu.VMEM) for r in results))


def solution(mesh):
    sizes = (mesh.shape["group"], mesh.shape["gx"], mesh.shape["gy"])
    return jax.shard_map(
        functools.partial(on_device, sizes),
        mesh=mesh,
        in_specs=(
            P(None, "gx", "group", "gy"),
            P(None, "gx", ("group", "gy")),
            P(),
            P(("group", "gy"), "gx", None),
            P(("group", "gy"), "gx", None),
            P(("group", "gy"), "gx", None),
            P(("group", "gy"), "gx"),
        ),
        out_specs=(P(None, "gx", "group", "gy"), P(None, "gx", ("group", "gy"))),
        check_vma=False,
    )
```

```python
import functools

import jax
import jax.numpy as jnp
from jax import lax
from jax.experimental import pallas as pl
from jax.experimental.pallas import tpu as pltpu
from jax.sharding import PartitionSpec as P

MESH = pl.DeviceIdType.MESH
VISCOSITY = 0.05
LES_STEP = 0.2
WAVE_STEP = 0.3
CX, CZ, CY = 8, 48, 128
ZT = CZ // 8
CHUNKS = 3
CHUNK_ROWS = CZ // CHUNKS
CHUNK_TILES = ZT // CHUNKS
OFFSETS = (1.0, 0.0, 0.0, 0.0, 1.0)
STATE_SCALE = (130816.0, 65408.0, 65408.0, 65408.0, 130816.0)
PRED_SCALE = (24576.0,) * 5


def encode(value, offset, scale):
    return ((value - offset) * scale + 32768.5).astype(jnp.int32)


def decode(code, offset, scale):
    return code.astype(jnp.float32) * (1.0 / scale) + (offset - 32768.0 / scale)


def pair_words(first, second, offset, scale):
    return (encode(first, offset, scale) << 16) | encode(second, offset, scale)


def split_words(words, offset, scale):
    first = decode(lax.shift_right_logical(words, 16), offset, scale)
    return first, decode(words & 0xFFFF, offset, scale)


def lanes():
    return lax.broadcasted_iota(jnp.int32, (8, 128), 1)


def rows():
    return lax.broadcasted_iota(jnp.int32, (8, 128), 0)


def roll_lane(tile, shift):
    shift = shift % tile.shape[1]
    return pltpu.roll(tile, shift, 1) if shift else tile


def roll_row(tile, shift):
    shift = shift % tile.shape[0]
    return pltpu.roll(tile, shift, 0) if shift else tile


def y_shifts(tile, halo, slot, reach):
    lane = lanes()
    halo = roll_lane(halo, -(4 * slot + 2))
    shifts = []
    for s in reach:
        before = roll_lane(jnp.where(lane >= 128 - s, halo, tile), s)
        after = roll_lane(jnp.where(lane < s, halo, tile), -s)
        shifts.append((before, after))
    return shifts


def rate_tile(buf, x, zt, halo):
    base = 8 + 8 * zt

    def at(f, dx, dz):
        return buf[f, x + (2 + dx), pl.ds(base + dz, 8), :]

    centre, grads, laps = [], [], []
    for f in range(5):
        c = at(f, 0, 0)
        xm1, xp1, zm1, zp1 = at(f, -1, 0), at(f, 1, 0), at(f, 0, -1), at(f, 0, 1)
        (ym1, yp1), (ym2, yp2) = y_shifts(c, halo, f * ZT + zt, (1, 2))
        dx = 8.0 * (xp1 - xm1) - (at(f, 2, 0) - at(f, -2, 0))
        dz = 8.0 * (zp1 - zm1) - (at(f, 0, 2) - at(f, 0, -2))
        dy = 8.0 * (yp1 - ym1) - (yp2 - ym2)
        centre.append(c)
        grads.append((dx, dz, dy))
        laps.append(((xm1 + xp1) + (zm1 + zp1)) + (ym1 + yp1) - 6.0 * c if 1 <= f <= 3 else None)
    rho, u0, u1, u2, p = centre
    div = grads[1][0] + grads[2][1] + grads[3][2]
    inverse = 1.0 / rho

    def advect(f):
        return u0 * grads[f][0] + u1 * grads[f][1] + u2 * grads[f][2]

    twelfth = -1.0 / 12.0
    rates = [(advect(0) + rho * div) * twelfth]
    for d in range(3):
        rates.append((advect(1 + d) + grads[4][d] * inverse) * twelfth + VISCOSITY * laps[1 + d])
    rates.append((advect(4) + 1.4 * (p * div)) * twelfth)
    return centre, rates


def packed_products(tile):
    momentum = tile * roll_lane(tile, -72)
    return (
        momentum * roll_lane(tile, -24),
        momentum * roll_lane(tile, -48),
        momentum * roll_lane(tile, -72),
    )


def wave_rates(state, source, inverse_radius):
    p, ux, ur = state

    def d(f, axis):
        size = f.shape[axis]
        one = pltpu.roll(f, size - 1, axis) - pltpu.roll(f, 1, axis)
        two = pltpu.roll(f, size - 2, axis) - pltpu.roll(f, 2, axis)
        return (8.0 * one - two) * (1.0 / 12.0)

    return (source - d(ux, 0) - d(ur, 1) - ur * inverse_radius, -d(p, 0), -d(p, 1))


def kernel(
    sizes, far_order,
    les_ref, wave_in, ops_ref, owner_in, slot_in, weight_in, mask_in,
    les_out, wave_out,
    state, pred, base_sum, s00, s11, s22, s01, s02, s12,
    wave_ref, owner_ref, slot_ref, weight_ref, mask_ref,
    xs1, xr1, xs2, xr2, zs1, zr1, zs2, zr2, ys1, yr1, ys2, yr2, ym2,
    exz_s, exz_r, ezy_s, ezy_r, ezy_x,
    light, ops_raw, ops_wide, ops_mat, spread, labels, weight_tiles,
    sent, received, own_source, near_source, near_wave,
    local_sems, x_send, x_recv, send1, recv1, send2, recv2, wave_send, wave_recv, all_send, all_recv, src_send, src_recv, gossip,
):
    n_group, n_gx, n_gy = sizes
    g, gx, gy = lax.axis_index("group"), lax.axis_index("gx"), lax.axis_index("gy")
    rank = g * n_gy + gy
    n_rank = n_group * n_gy
    gx_low, gx_high = lax.rem(gx + (n_gx - 1), n_gx), lax.rem(gx + 1, n_gx)
    gy_low, gy_high = lax.rem(gy + (n_gy - 1), n_gy), lax.rem(gy + 1, n_gy)
    other = 1 - g
    lane, row = lanes(), rows()

    def remote(src, dst, send_sem, recv_sem, device):
        return pltpu.make_async_remote_copy(
            src_ref=src, dst_ref=dst, send_sem=send_sem, recv_sem=recv_sem, device_id=device, device_id_type=MESH
        )

    barrier = pltpu.get_barrier_semaphore()
    for device in ((g, gx_low, gy), (g, gx_high, gy), (other, gx, gy), (g, gx, gy_low), (g, gx, gy_high)):
        pl.semaphore_signal(barrier, inc=1, device_id=device, device_id_type=MESH)

    def load(src, dst, i):
        copy = pltpu.make_async_copy(src, dst, local_sems.at[i])
        copy.start()
        return copy

    def face_rows(chunk):
        return slice(CHUNK_ROWS * chunk, CHUNK_ROWS * (chunk + 1)), slice(
            8 + CHUNK_ROWS * chunk, 8 + CHUNK_ROWS * (chunk + 1)
        )

    load_faces = []
    for chunk in range(CHUNKS):
        theirs, mine = face_rows(chunk)
        load_faces.append(
            [
                load(les_ref.at[:, 0:2, theirs], state.at[:, 2:4, mine, :], 7 + 2 * chunk),
                load(les_ref.at[:, 6:8, theirs], state.at[:, 8:10, mine, :], 8 + 2 * chunk),
            ]
        )
    load_inner = load(les_ref.at[:, 2:6], state.at[:, 4:8, 8:56, :], 0)
    load_small = [
        load(owner_in, owner_ref, 1),
        load(slot_in, slot_ref, 2),
        load(weight_in, weight_ref, 3),
        load(mask_in, mask_ref, 4),
        load(wave_in, wave_ref, 5),
    ]
    load_ops = load(ops_ref, ops_raw, 6)
    for copy in load_faces[0]:
        copy.wait()

    def gossip_send(r):
        if r < gossip.shape[0]:
            d = 1 << r
            for target in (lax.rem(gx + d, n_gx), lax.rem(gx + (n_gx - d), n_gx)):
                pl.semaphore_signal(gossip.at[r], inc=1, device_id=(g, target, gy), device_id_type=MESH)

    def gossip_wait(r):
        if r < gossip.shape[0]:
            pl.semaphore_wait(gossip.at[r], 2)

    def x_pack(buf, out, scales, chunk):
        part = slice(8 + CHUNK_ROWS * chunk, 8 + CHUNK_ROWS * (chunk + 1))
        for f in range(5):
            for side, first in ((0, 2), (1, 8)):
                out[side, chunk, f] = pair_words(
                    buf[f, first, part, :], buf[f, first + 1, part, :], OFFSETS[f], scales[f]
                )

    def x_unpack(buf, words, scales, chunk):
        part = slice(8 + CHUNK_ROWS * chunk, 8 + CHUNK_ROWS * (chunk + 1))
        for f in range(5):
            for side, first in ((0, 0), (1, 10)):
                one, two = split_words(words[side, chunk, f], OFFSETS[f], scales[f])
                buf[f, first, part, :] = one
                buf[f, first + 1, part, :] = two

    def x_copies(sent_words, words, stage, chunk):
        first = 2 * (CHUNKS * stage + chunk)
        return [
            remote(
                sent_words.at[0, chunk], words.at[1, chunk], x_send.at[first], x_recv.at[first + 1], (g, gx_low, gy)
            ),
            remote(
                sent_words.at[1, chunk], words.at[0, chunk], x_send.at[first + 1], x_recv.at[first], (g, gx_high, gy)
            ),
        ]

    def ends(buf, f, x):
        return jnp.where(row < 4, buf[f, x + 2, 8:16, :], buf[f, x + 2, 48:56, :])

    def z_pack(buf, out, scales):
        for f in range(5):
            for j in range(2):
                a = pair_words(ends(buf, f, 2 * j), ends(buf, f, 2 * j + 4), OFFSETS[f], scales[f])
                b = pair_words(ends(buf, f, 2 * j + 1), ends(buf, f, 2 * j + 5), OFFSETS[f], scales[f])
                out[2 * f + j] = jnp.where((row < 2) | (row >= 6), a, roll_row(b, 4))

    def z_unpack(buf, words, scales):
        for f in range(5):
            for j in range(2):
                word = words[2 * f + j]
                for i, part in enumerate((word, roll_row(word, 4))):
                    for x, tile in zip((2 * j + i, 2 * j + i + 4), split_words(part, OFFSETS[f], scales[f])):
                        buf[f, x + 2, 0:8, :] = tile
                        buf[f, x + 2, 56:64, :] = tile

    def y_add(packed, tile, slot):
        return jnp.where((lane >> 2) == slot, roll_lane(tile, 4 * slot + 2), packed)

    def y_merge(from_low, from_high):
        return jnp.where((lane & 2) == 0, from_low, from_high)

    def y_pack(x, carry):
        packed = jnp.zeros((8, 128), jnp.float32)
        for f in range(5):
            for zt in range(ZT):
                packed = y_add(packed, state[f, x + 2, pl.ds(8 + 8 * zt, 8), :], f * ZT + zt)
        ys1[x] = packed
        return carry

    x_pack(state, xs1, STATE_SCALE, 0)
    pl.semaphore_wait(barrier, 5)
    gossip_send(0)
    x_first = [x_copies(xs1, xr1, 0, chunk) for chunk in range(CHUNKS)]
    x_second = [x_copies(xs2, xr2, 1, chunk) for chunk in range(CHUNKS)]
    first = [
        remote(zs1, zr1, send1.at[0], recv1.at[0], (other, gx, gy)),
        remote(ys1, yr1.at[1], send1.at[1], recv1.at[2], (g, gx, gy_low)),
        remote(ys1, yr1.at[0], send1.at[2], recv1.at[1], (g, gx, gy_high)),
    ]
    for copy in x_first[0]:
        copy.start()
    for chunk in range(1, CHUNKS):
        for copy in load_faces[chunk]:
            copy.wait()
        x_pack(state, xs1, STATE_SCALE, chunk)
        for copy in x_first[chunk]:
            copy.start()
    load_inner.wait()
    z_pack(state, zs1, STATE_SCALE)
    first[0].start()
    lax.fori_loop(0, CX, y_pack, 0)
    first[1].start()
    first[2].start()

    load_ops.wait()
    for copy in load_small:
        copy.wait()

    def widen(i, carry):
        part = pl.ds(pl.multiple_of(i * 512, 512), 512)
        ops_wide[...] = ops_raw[part, :].astype(jnp.float32)
        for w in range(4):
            ops_mat[pl.ds(pl.multiple_of(i * 128, 128), 128), w * 128:(w + 1) * 128] = (
                ops_wide[pl.ds(w, 128, stride=4), :].astype(jnp.bfloat16)
            )
        return carry

    lax.fori_loop(0, 12, widen, 0)
    pair_lane = lane & 31
    owners = jnp.full((8, 128), -99, jnp.int32)
    first_slot, second_slot, seen = (jnp.zeros((8, 128), jnp.int32) for _ in range(3))
    for k in range(4):
        weights = jnp.zeros((8, 128), jnp.int32)
        for x in range(8):
            owner = owner_ref[0, k, x]
            owners = jnp.where((pair_lane == k * 8 + x) & (lane < 96), owner, owners)
            hit = lane == owner
            first_slot = jnp.where(hit & (seen == 0), slot_ref[0, k, x] + 1, first_slot)
            second_slot = jnp.where(hit & (seen == 1), slot_ref[0, k, x] + 1, second_slot)
            seen = jnp.where(hit, seen + 1, seen)
            weights = jnp.where(row == x, weight_ref[0, k, x], weights)
        weight_tiles[k] = weights
    rank_of = jnp.zeros((8, 128), jnp.int32)
    for k in range(4):
        for x in range(8):
            earlier = (owners == owner_ref[0, k, x]) & (pair_lane > k * 8 + x)
            rank_of = rank_of + jnp.where(earlier, 1, 0)
    own_lane = 8 * lax.rem(gx, 16)
    first_slot = pltpu.roll(first_slot.astype(jnp.float32), own_lane + 1, 1)
    second_slot = pltpu.roll(second_slot.astype(jnp.float32), own_lane + 5, 1)
    first_here = (row == 7) & (lane >= own_lane) & (lane < own_lane + 3)
    second_here = (row == 7) & (lane >= own_lane + 4) & (lane < own_lane + 7)
    for d in range(n_gx):
        near = (owners >= d - 1) & (owners <= d + 1)
        spread[d * 8:(d + 1) * 8, :] = jnp.where(near & (owners - (d - 1) + 4 * rank_of == row), 1.0, 0.0)
        slots = jnp.where(second_here, roll_lane(second_slot, -d), 0.0)
        labels[d * 8:(d + 1) * 8, :] = jnp.where(first_here, roll_lane(first_slot, -d), slots)

    gossip_wait(0)
    gossip_send(1)
    first[0].wait_recv()
    z_unpack(state, zr1, STATE_SCALE)
    first[1].wait_recv()
    first[2].wait_recv()

    def first_rate(x, tiles):
        halo = y_merge(yr1[0, x], yr1[1, x])
        packed = jnp.zeros((8, 128), jnp.float32) if tiles[0] == 0 else ys2[x]
        for zt in tiles:
            centre, rates = rate_tile(state, x, zt, halo)
            part = pl.ds(8 * zt, 8)
            inner = pl.ds(8 + 8 * zt, 8)
            new = []
            for f in range(5):
                value = centre[f] + LES_STEP * rates[f]
                pred[f, x + 2, inner, :] = value
                base_sum[f, x, part, :] = centre[f] + (0.5 * LES_STEP) * rates[f]
                packed = y_add(packed, value, f * ZT + zt)
                new.append(value)
            rho, u0, u1, u2, _ = new
            m0, m1 = rho * u0, rho * u1
            s00[x + 2, part, :] = m0 * u0
            s01[x + 1, inner, :] = m0 * u1
            s02[x + 1, part, :] = m0 * u2
            s11[x, inner, :] = m1 * u1
            s12[x, inner, :] = m1 * u2
            s22[x, part, :] = rho * u2 * u2
        ys2[x] = packed

    def rate_inner(x, carry):
        first_rate(x, tuple(range(ZT)))
        return carry

    second = [
        remote(zs2, zr2, send2.at[0], recv2.at[0], (other, gx, gy)),
        remote(ys2, yr2.at[1, 1:9], send2.at[1], recv2.at[2], (g, gx, gy_low)),
        remote(ys2, yr2.at[0, 1:9], send2.at[2], recv2.at[1], (g, gx, gy_high)),
        remote(ezy_s, ezy_r.at[1], send2.at[3], recv2.at[4], (other, gx, gy_low)),
        remote(ezy_s, ezy_r.at[0], send2.at[4], recv2.at[3], (other, gx, gy_high)),
        remote(exz_s.at[0], exz_r.at[1], send2.at[5], recv2.at[6], (other, gx_low, gy)),
        remote(exz_s.at[1], exz_r.at[0], send2.at[6], recv2.at[5], (other, gx_high, gy)),
        remote(ys2.at[0], yr2.at[1, 9], send2.at[7], recv2.at[10], (g, gx_low, gy_low)),
        remote(ys2.at[0], yr2.at[0, 9], send2.at[8], recv2.at[9], (g, gx_low, gy_high)),
        remote(ys2.at[7], yr2.at[1, 0], send2.at[9], recv2.at[8], (g, gx_high, gy_low)),
        remote(ys2.at[7], yr2.at[0, 0], send2.at[10], recv2.at[7], (g, gx_high, gy_high)),
    ]
    lax.fori_loop(2, 6, rate_inner, 0)

    around = [(dx, dr) for dx in (-1, 0, 1) for dr in (-1, 0, 1) if (dx, dr) != (0, 0)]

    def neighbour(dx, dr):
        there = lax.rem(rank + (n_rank + dr), n_rank)
        return (there // n_gy, lax.rem(gx + (n_gx + dx), n_gx), lax.rem(there, n_gy))

    def slot_of(dx, dr):
        return around.index((dx, dr))

    def send_wave(corner):
        for dx, dr in around:
            if (dx * dr != 0) == corner:
                slot = near_wave.at[slot_of(-dx, -dr)]
                remote(wave_ref, slot, wave_send.at[0], wave_recv.at[0], neighbour(dx, dr)).start()

    send_wave(False)
    gossip_wait(1)
    gossip_send(2)
    for chunk in range(CHUNKS):
        for copy in x_first[chunk]:
            copy.wait_recv()
        x_unpack(state, xr1, STATE_SCALE, chunk)
        for x in (6, 7, 0, 1):
            first_rate(x, tuple(range(CHUNK_TILES * chunk, CHUNK_TILES * (chunk + 1))))
        if chunk == CHUNKS - 1:
            for side in range(2):
                x = 7 * side
                exz_s[side] = ends(pred, 0, x) * ends(pred, 1, x) * ends(pred, 2, x)
            for copy in second[5:]:
                copy.start()
        x_pack(pred, xs2, PRED_SCALE, chunk)
        for copy in x_second[chunk]:
            copy.start()

    z_pack(pred, zs2, PRED_SCALE)
    for copy in second[:3]:
        copy.start()
    edge = jnp.zeros((8, 128), jnp.float32)
    for x in range(8):
        product = packed_products(ys2[x])[1]
        both = jnp.where(lane < 4, product, roll_lane(product, -16))
        edge = jnp.where((lane >> 3) == x, roll_lane(both, 8 * x), edge)
    ezy_s[...] = edge
    second[3].start()
    second[4].start()
    gossip_wait(2)
    gossip_send(3)

    second[0].wait_recv()
    z_unpack(pred, zr2, PRED_SCALE)
    for x in range(8):
        for part in (slice(0, 8), slice(56, 64)):
            rho, u0, u1, u2 = (pred[f, x + 2, part, :] for f in range(4))
            m1 = rho * u1
            s01[x + 1, part, :] = m1 * u0
            s11[x, part, :] = m1 * u1
            s12[x, part, :] = m1 * u2
    for copy in second[1:5]:
        copy.wait_recv()
    for x in range(8):
        ym2[x + 1] = y_merge(yr2[0, x + 1], yr2[1, x + 1])
    corners = y_merge(ezy_r[0], ezy_r[1])
    for x in range(8):
        ezy_x[x] = roll_lane(corners, -8 * x)

    def lighthill(x, carry):
        along_x = packed_products(ym2[x + 2])[0] - packed_products(ym2[x])[0]
        _, s12_halo, square = packed_products(ym2[x + 1])
        corner = ezy_x[x]
        next_tile = jnp.where(lane >= 20, roll_lane(corner, 20), roll_lane(s12_halo, -4))
        last_tile = jnp.where(lane < 4, roll_lane(corner, -4), roll_lane(s12_halo, 4))
        after = roll_row(jnp.where(row == 0, next_tile, s12_halo), -1)
        before = roll_row(jnp.where(row == 7, last_tile, s12_halo), 1)
        cross = along_x + (after - before)
        keep = mask_ref[0, x].astype(jnp.float32)
        for zt in range(ZT):
            part = pl.ds(8 * zt, 8)

            def z(ref, index, dz):
                return ref[index, pl.ds(8 + 8 * zt + dz, 8), :]

            direct = s00[x + 4, part, :] + s00[x, part, :] - 2.0 * s00[x + 2, part, :]
            direct = direct + (z(s11, x, 2) + z(s11, x, -2) - 2.0 * z(s11, x, 0))
            tile = s22[x, part, :]
            ((before, after),) = y_shifts(tile, square, zt, (2,))
            direct = direct + (before + after - 2.0 * tile)
            mixed = (z(s01, x + 2, 1) - z(s01, x + 2, -1)) - (z(s01, x, 1) - z(s01, x, -1))
            tile = (s02[x + 2, part, :] - s02[x, part, :]) + (z(s12, x, 1) - z(s12, x, -1))
            ((before, after),) = y_shifts(tile, cross, zt, (1,))
            mixed = mixed + (after - before)
            light[pl.ds(pl.multiple_of(x * CZ + 8 * zt, 8), 8), :] = (0.25 * direct + 0.5 * mixed) * keep
        return carry

    lax.fori_loop(2, 6, lighthill, 0)
    for chunk in range(CHUNKS):
        for copy in x_second[chunk]:
            copy.wait_recv()
        x_unpack(pred, xr2, PRED_SCALE, chunk)
    for index in (0, 1, 10, 11):
        s00[index] = pred[0, index, 8:56, :] * pred[1, index, 8:56, :] * pred[1, index, 8:56, :]
    for index, layer in ((0, 1), (9, 10)):
        m0 = pred[0, layer, 8:56, :] * pred[1, layer, 8:56, :]
        s01[index, 8:56, :] = m0 * pred[2, layer, 8:56, :]
        s02[index] = m0 * pred[3, layer, 8:56, :]
    send_wave(True)
    for copy in second[5:]:
        copy.wait_recv()
    for index in (0, 9):
        ym2[index] = y_merge(yr2[0, index], yr2[1, index])
    for side, index in ((0, 0), (1, 9)):
        s01[index, 0:8, :] = exz_r[side]
        s01[index, 56:64, :] = exz_r[side]
    lax.fori_loop(0, 4, lambda j, carry: lighthill(lax.rem(j + 6, 8), carry), 0)

    pieces = []
    for zp in range(12):
        one, two = (
            light[pl.ds(4 * zp + 2 * i, 8, stride=CZ), :] + light[pl.ds(4 * zp + 2 * i + 1, 8, stride=CZ), :]
            for i in range(2)
        )
        one = one + roll_lane(one, -1)
        two = two + roll_lane(two, 1)
        pieces.append(jnp.where((lane & 1) == 0, one, two))
    merged = jnp.concatenate(pieces, axis=0).astype(jnp.bfloat16)
    source_lane = lax.broadcasted_iota(jnp.int32, (128, 128), 0)
    target_lane = lax.broadcasted_iota(jnp.int32, (128, 128), 1)
    order = jnp.where(target_lane == (source_lane & 1) * 64 + (source_lane >> 1), 1.0, 0.0).astype(jnp.bfloat16)
    sorted_rows = jnp.dot(merged, order, preferred_element_type=jnp.float32)
    tile_rows = jnp.concatenate([sorted_rows[8 * i:8 * i + 8, :] for i in range(12)], axis=1).astype(jnp.bfloat16)
    products = jnp.dot(tile_rows, ops_mat[...], preferred_element_type=jnp.float32)
    pairs = []
    for k in range(4):
        chosen = jnp.zeros((8, 128), jnp.float32)
        for w in range(4):
            chosen = jnp.where(weight_tiles[k] == w, products[:, w * 128:(w + 1) * 128], chosen)
        pairs.append(chosen)
    values = jnp.concatenate(pairs, axis=0)
    high = values.astype(jnp.bfloat16).astype(jnp.float32)
    middle = (values - high).astype(jnp.bfloat16).astype(jnp.float32)
    rest = values - high - middle
    stacked = jnp.concatenate([high, middle, rest, jnp.zeros((32, 128), jnp.float32)], axis=0).astype(jnp.bfloat16)
    sent[...] = labels[...] + jnp.dot(spread[...].astype(jnp.bfloat16), stacked, preferred_element_type=jnp.float32)

    gossip_wait(3)
    all_copies = []
    for d in far_order:
        owner = lax.rem(gx + d, n_gx)
        copy = remote(
            sent.at[pl.ds(pl.multiple_of(owner * 8, 8), 8), :], received.at[gx],
            all_send.at[0], all_recv.at[0], (g, owner, gy),
        )
        copy.start()
    received[gx] = sent[pl.ds(pl.multiple_of(gx * 8, 8), 8), :]

    def second_rate(x, carry):
        halo = ym2[x + 1]
        for zt in range(ZT):
            _, rates = rate_tile(pred, x, zt, halo)
            part = pl.ds(8 * zt, 8)
            for f in range(5):
                les_out[f, x, part, :] = base_sum[f, x, part, :] + (0.5 * LES_STEP) * rates[f]
        return carry

    lax.fori_loop(0, CX, second_rate, 0)

    others = received.at[0:n_gx - 1]
    pltpu.make_async_copy(others, others, all_recv.at[0]).wait()
    tags = jnp.concatenate([jnp.sum(received[h:h + 16], axis=0)[7:8, :] for h in (0, 16)], axis=1)
    tags = jnp.broadcast_to(tags, (24, 256))
    line = lax.broadcasted_iota(jnp.int32, (24, 256), 0)
    column = lax.broadcasted_iota(jnp.int32, (24, 256), 1)
    lands = tags + (8 * (column & 3) - 1 - line).astype(jnp.float32)
    gather = jnp.where((tags > 0.5) & (jnp.abs(lands) < 0.5), 1.0, 0.0).astype(jnp.bfloat16)
    arrived = received[...].reshape(n_gx * 8, 128)
    high = arrived.astype(jnp.bfloat16).astype(jnp.float32)
    middle = (arrived - high).astype(jnp.bfloat16).astype(jnp.float32)
    source_lines = jnp.zeros((24, 128), jnp.float32)
    for part in (arrived - high - middle, middle, high):
        source_lines = source_lines + jnp.dot(gather, part.astype(jnp.bfloat16), preferred_element_type=jnp.float32)
    own_source[...] = source_lines
    for i, dr in ((0, -1), (1, 1)):
        remote(own_source, near_source.at[1 - i], src_send.at[0], src_recv.at[0], neighbour(0, dr)).start()

    pltpu.make_async_copy(near_wave, near_wave, wave_recv.at[0]).wait()
    wide_row = lax.broadcasted_iota(jnp.int32, (24, 256), 0)
    wide_lane = lax.broadcasted_iota(jnp.int32, (24, 256), 1)

    def flag(yes):
        return yes.astype(jnp.int32).astype(jnp.float32)

    inside = jnp.where(wide_row < 8, flag(gx > 0), jnp.where(wide_row >= 16, flag(gx < n_gx - 1), 1.0))
    inside = inside * jnp.where(
        wide_lane < 128, 1.0, jnp.where(wide_lane < 192, flag(rank < n_rank - 1), flag(rank > 0))
    )
    column = jnp.where(wide_lane < 192, wide_lane, wide_lane - 256) + rank * 128
    inverse_radius = 1.0 / (column.astype(jnp.float32) + 0.5)

    def assemble(block):
        strips = []
        for dx in (-1, 0, 1):
            side = jnp.where(lane < 64, block(dx, 1), block(dx, -1))
            strips.append(jnp.concatenate([block(dx, 0), side], axis=1))
        return jnp.concatenate(strips, axis=0) * inside

    def wave_block(f):
        return lambda dx, dr: wave_ref[f] if (dx, dr) == (0, 0) else near_wave[slot_of(dx, dr), f]

    now = [assemble(wave_block(f)) for f in range(3)]
    no_source = jnp.zeros((24, 256), jnp.float32)
    opening = wave_rates(now, no_source, inverse_radius)
    pltpu.make_async_copy(near_source, near_source, src_recv.at[0]).wait()
    beside = jnp.where(wide_lane[:, 0:128] < 64, near_source[1], near_source[0])
    source = jnp.concatenate([own_source[...], beside], axis=1) * inside
    for step in range(2):
        if step == 0:
            rate_one = (opening[0] + source, opening[1], opening[2])
        else:
            rate_one = wave_rates(now, source, inverse_radius)
        ahead = [(v + WAVE_STEP * r) * inside for v, r in zip(now, rate_one)]
        rate_two = wave_rates(ahead, source, inverse_radius)
        now = [(v + (0.5 * WAVE_STEP) * (a + b)) * inside for v, a, b in zip(now, rate_one, rate_two)]
    for f in range(3):
        wave_out[f] = now[f][8:16, 0:128]

    for copy in sum(x_first + x_second, first + second):
        copy.wait_send()
    pltpu.make_async_copy(others, others, all_send.at[0]).wait()
    pltpu.make_async_copy(near_wave, near_wave, wave_send.at[0]).wait()
    pltpu.make_async_copy(near_source, near_source, src_send.at[0]).wait()


def hand_on(les_in, wave_in, les_out, wave_out, sems):
    copies = [pltpu.make_async_copy(wave_in, wave_out, sems.at[5])]
    copies += [pltpu.make_async_copy(les_in.at[f], les_out.at[f], sems.at[f]) for f in range(5)]
    for copy in copies:
        copy.start()
    for copy in copies:
        copy.wait()


def on_device(sizes, les_state, wave_state, restriction_ops, pair_owner, pair_slot, pair_weight, tile_mask):
    n_gx = sizes[1]
    tile_len, op_count, width = restriction_ops.shape
    ops_flat = restriction_ops.reshape(tile_len * op_count, width)
    rounds = max(1, (n_gx // 2).bit_length() - 1)
    far_order = sorted(range(1, n_gx), key=lambda d: -(2 * min(d // 8, 4 - d // 8) + min(d % 8, 8 - d % 8)))
    f32, i32, bf16 = jnp.float32, jnp.int32, jnp.bfloat16
    vmem, smem, dma = pltpu.VMEM, pltpu.SMEM, pltpu.SemaphoreType.DMA
    scratch = [
        vmem((5, 12, 64, 128), f32), vmem((5, 12, 64, 128), f32), vmem((5, 8, 48, 128), f32),
        vmem((12, 48, 128), f32), vmem((8, 64, 128), f32), vmem((8, 48, 128), f32),
        vmem((10, 64, 128), f32), vmem((10, 48, 128), f32), vmem((8, 64, 128), f32),
        vmem((3, 8, 128), f32), smem((1, 4, 8), i32), smem((1, 4, 8), i32), smem((1, 4, 8), i32), smem((1, 8), i32),
        vmem((2, CHUNKS, 5, CHUNK_ROWS, 128), i32), vmem((2, CHUNKS, 5, CHUNK_ROWS, 128), i32),
        vmem((2, CHUNKS, 5, CHUNK_ROWS, 128), i32), vmem((2, CHUNKS, 5, CHUNK_ROWS, 128), i32),
        vmem((10, 8, 128), i32), vmem((10, 8, 128), i32), vmem((10, 8, 128), i32), vmem((10, 8, 128), i32),
        vmem((8, 8, 128), f32), vmem((2, 8, 8, 128), f32), vmem((8, 8, 128), f32), vmem((2, 10, 8, 128), f32),
        vmem((10, 8, 128), f32),
        vmem((2, 8, 128), f32), vmem((2, 8, 128), f32), vmem((8, 128), f32), vmem((2, 8, 128), f32),
        vmem((8, 8, 128), f32),
        vmem((CX * CZ, 128), f32), vmem((6144, 128), bf16), vmem((512, 128), f32), vmem((1536, 512), bf16),
        vmem((n_gx * 8, 128), f32), vmem((n_gx * 8, 128), f32), vmem((4, 8, 128), i32),
        vmem((n_gx * 8, 128), f32), vmem((n_gx, 8, 128), f32), vmem((24, 128), f32),
        vmem((2, 24, 128), f32), vmem((8, 3, 8, 128), f32),
        dma((7 + 2 * CHUNKS,)), dma((4 * CHUNKS,)), dma((4 * CHUNKS,)), dma((3,)), dma((3,)), dma((11,)), dma((11,)), dma((1,)), dma((1,)), dma((1,)), dma((1,)),
        dma((1,)), dma((1,)), pltpu.SemaphoreType.REGULAR((rounds,)),
    ]
    any_space = pl.BlockSpec(memory_space=pl.ANY)
    in_vmem = pl.BlockSpec(memory_space=pltpu.VMEM)
    results = pl.pallas_call(
        functools.partial(kernel, sizes, far_order),
        out_shape=(vmem(les_state.shape, f32), vmem(wave_state.shape, f32)),
        in_specs=[any_space] * 7,
        out_specs=(in_vmem, in_vmem),
        scratch_shapes=scratch,
        compiler_params=pltpu.CompilerParams(collective_id=0, has_side_effects=True),
        name="jet_step",
    )(les_state, wave_state, ops_flat, *(a.swapaxes(1, 2) for a in (pair_owner, pair_slot, pair_weight)), tile_mask)
    return pl.pallas_call(
        hand_on,
        out_shape=tuple(jax.ShapeDtypeStruct(r.shape, f32) for r in results),
        in_specs=[in_vmem] * 2,
        out_specs=(any_space,) * 2,
        scratch_shapes=[dma((6,))],
        name="hand_on",
    )(*(pltpu.with_memory_space_constraint(r, pltpu.VMEM) for r in results))


def solution(mesh):
    sizes = (mesh.shape["group"], mesh.shape["gx"], mesh.shape["gy"])
    return jax.shard_map(
        functools.partial(on_device, sizes),
        mesh=mesh,
        in_specs=(
            P(None, "gx", "group", "gy"),
            P(None, "gx", ("group", "gy")),
            P(),
            P(("group", "gy"), "gx", None),
            P(("group", "gy"), "gx", None),
            P(("group", "gy"), "gx", None),
            P(("group", "gy"), "gx"),
        ),
        out_specs=(P(None, "gx", "group", "gy"), P(None, "gx", ("group", "gy"))),
        check_vma=False,
    )
```

```python
import functools

import jax
import jax.numpy as jnp
from jax import lax
from jax.experimental import pallas as pl
from jax.experimental.pallas import tpu as pltpu
from jax.sharding import PartitionSpec as P

MESH = pl.DeviceIdType.MESH
VISCOSITY = 0.05
LES_STEP = 0.2
WAVE_STEP = 0.3
CX, CZ, CY = 8, 48, 128
ZT = CZ // 8
CHUNKS = 3
CHUNK_ROWS = CZ // CHUNKS
CHUNK_TILES = ZT // CHUNKS
OFFSETS = (1.0, 0.0, 0.0, 0.0, 1.0)
STATE_SCALE = (130816.0, 65408.0, 65408.0, 65408.0, 130816.0)
PRED_SCALE = (24576.0,) * 5


def encode(value, offset, scale):
    return ((value - offset) * scale + 32768.5).astype(jnp.int32)


def decode(code, offset, scale):
    return code.astype(jnp.float32) * (1.0 / scale) + (offset - 32768.0 / scale)


def pair_words(first, second, offset, scale):
    return (encode(first, offset, scale) << 16) | encode(second, offset, scale)


def split_words(words, offset, scale):
    first = decode(lax.shift_right_logical(words, 16), offset, scale)
    return first, decode(words & 0xFFFF, offset, scale)


def lanes():
    return lax.broadcasted_iota(jnp.int32, (8, 128), 1)


def rows():
    return lax.broadcasted_iota(jnp.int32, (8, 128), 0)


def roll_lane(tile, shift):
    shift = shift % tile.shape[1]
    return pltpu.roll(tile, shift, 1) if shift else tile


def roll_row(tile, shift):
    shift = shift % tile.shape[0]
    return pltpu.roll(tile, shift, 0) if shift else tile


def y_shifts(tile, halo, slot, reach):
    lane = lanes()
    halo = roll_lane(halo, -(4 * slot + 2))
    shifts = []
    for s in reach:
        before = roll_lane(jnp.where(lane >= 128 - s, halo, tile), s)
        after = roll_lane(jnp.where(lane < s, halo, tile), -s)
        shifts.append((before, after))
    return shifts


def rate_tile(buf, x, zt, halo):
    base = 8 + 8 * zt

    def at(f, dx, dz):
        return buf[f, x + (2 + dx), pl.ds(base + dz, 8), :]

    centre, grads, laps = [], [], []
    for f in range(5):
        c = at(f, 0, 0)
        xm1, xp1, zm1, zp1 = at(f, -1, 0), at(f, 1, 0), at(f, 0, -1), at(f, 0, 1)
        (ym1, yp1), (ym2, yp2) = y_shifts(c, halo, f * ZT + zt, (1, 2))
        dx = 8.0 * (xp1 - xm1) - (at(f, 2, 0) - at(f, -2, 0))
        dz = 8.0 * (zp1 - zm1) - (at(f, 0, 2) - at(f, 0, -2))
        dy = 8.0 * (yp1 - ym1) - (yp2 - ym2)
        centre.append(c)
        grads.append((dx, dz, dy))
        laps.append(((xm1 + xp1) + (zm1 + zp1)) + (ym1 + yp1) - 6.0 * c if 1 <= f <= 3 else None)
    rho, u0, u1, u2, p = centre
    div = grads[1][0] + grads[2][1] + grads[3][2]
    inverse = 1.0 / rho

    def advect(f):
        return u0 * grads[f][0] + u1 * grads[f][1] + u2 * grads[f][2]

    twelfth = -1.0 / 12.0
    rates = [(advect(0) + rho * div) * twelfth]
    for d in range(3):
        rates.append((advect(1 + d) + grads[4][d] * inverse) * twelfth + VISCOSITY * laps[1 + d])
    rates.append((advect(4) + 1.4 * (p * div)) * twelfth)
    return centre, rates


def packed_products(tile):
    momentum = tile * roll_lane(tile, -72)
    return (
        momentum * roll_lane(tile, -24),
        momentum * roll_lane(tile, -48),
        momentum * roll_lane(tile, -72),
    )


def wave_rates(state, source, inverse_radius):
    p, ux, ur = state

    def d(f, axis):
        size = f.shape[axis]
        one = pltpu.roll(f, size - 1, axis) - pltpu.roll(f, 1, axis)
        two = pltpu.roll(f, size - 2, axis) - pltpu.roll(f, 2, axis)
        return (8.0 * one - two) * (1.0 / 12.0)

    return (source - d(ux, 0) - d(ur, 1) - ur * inverse_radius, -d(p, 0), -d(p, 1))


def kernel(
    sizes, far_order,
    les_ref, wave_in, ops_ref, owner_in, slot_in, weight_in, mask_in,
    les_out, wave_out,
    state, pred, base_sum, s00, s11, s22, s01, s02, s12,
    wave_ref, owner_ref, slot_ref, weight_ref, mask_ref,
    xs1, xr1, xs2, xr2, zs1, zr1, zs2, zr2, ys1, yr1, ys2, yr2, ym2,
    exz_s, exz_r, ezy_s, ezy_r, ezy_x,
    light, ops_raw, ops_wide, ops_mat, spread, labels, weight_tiles,
    sent, received, own_source, near_source, near_wave,
    local_sems, x_send, x_recv, send1, recv1, send2, recv2, wave_send, wave_recv, all_send, all_recv, src_send, src_recv, gossip,
):
    n_group, n_gx, n_gy = sizes
    g, gx, gy = lax.axis_index("group"), lax.axis_index("gx"), lax.axis_index("gy")
    rank = g * n_gy + gy
    n_rank = n_group * n_gy
    gx_low, gx_high = lax.rem(gx + (n_gx - 1), n_gx), lax.rem(gx + 1, n_gx)
    gy_low, gy_high = lax.rem(gy + (n_gy - 1), n_gy), lax.rem(gy + 1, n_gy)
    other = 1 - g
    lane, row = lanes(), rows()

    def remote(src, dst, send_sem, recv_sem, device):
        return pltpu.make_async_remote_copy(
            src_ref=src, dst_ref=dst, send_sem=send_sem, recv_sem=recv_sem, device_id=device, device_id_type=MESH
        )

    barrier = pltpu.get_barrier_semaphore()
    for device in ((g, gx_low, gy), (g, gx_high, gy), (other, gx, gy), (g, gx, gy_low), (g, gx, gy_high)):
        pl.semaphore_signal(barrier, inc=1, device_id=device, device_id_type=MESH)

    def load(src, dst, i):
        copy = pltpu.make_async_copy(src, dst, local_sems.at[i])
        copy.start()
        return copy

    def face_rows(chunk):
        return slice(CHUNK_ROWS * chunk, CHUNK_ROWS * (chunk + 1)), slice(
            8 + CHUNK_ROWS * chunk, 8 + CHUNK_ROWS * (chunk + 1)
        )

    load_faces = []
    for chunk in range(CHUNKS):
        theirs, mine = face_rows(chunk)
        load_faces.append(
            [
                load(les_ref.at[:, 0:2, theirs], state.at[:, 2:4, mine, :], 7 + 2 * chunk),
                load(les_ref.at[:, 6:8, theirs], state.at[:, 8:10, mine, :], 8 + 2 * chunk),
            ]
        )
    load_inner = load(les_ref.at[:, 2:6], state.at[:, 4:8, 8:56, :], 0)
    load_small = [
        load(owner_in, owner_ref, 1),
        load(slot_in, slot_ref, 2),
        load(weight_in, weight_ref, 3),
        load(mask_in, mask_ref, 4),
        load(wave_in, wave_ref, 5),
    ]
    load_ops = load(ops_ref, ops_raw, 6)
    for copy in load_faces[0]:
        copy.wait()

    def gossip_send(r):
        if r < gossip.shape[0]:
            d = 1 << r
            for target in (lax.rem(gx + d, n_gx), lax.rem(gx + (n_gx - d), n_gx)):
                pl.semaphore_signal(gossip.at[r], inc=1, device_id=(g, target, gy), device_id_type=MESH)

    def gossip_wait(r):
        if r < gossip.shape[0]:
            pl.semaphore_wait(gossip.at[r], 2)

    def x_pack(buf, out, scales, chunk):
        part = slice(8 + CHUNK_ROWS * chunk, 8 + CHUNK_ROWS * (chunk + 1))
        for f in range(5):
            for side, first in ((0, 2), (1, 8)):
                out[side, chunk, f] = pair_words(
                    buf[f, first, part, :], buf[f, first + 1, part, :], OFFSETS[f], scales[f]
                )

    def x_unpack(buf, words, scales, chunk):
        part = slice(8 + CHUNK_ROWS * chunk, 8 + CHUNK_ROWS * (chunk + 1))
        for f in range(5):
            for side, first in ((0, 0), (1, 10)):
                one, two = split_words(words[side, chunk, f], OFFSETS[f], scales[f])
                buf[f, first, part, :] = one
                buf[f, first + 1, part, :] = two

    def x_copies(sent_words, words, stage, chunk):
        first = 2 * (CHUNKS * stage + chunk)
        return [
            remote(
                sent_words.at[0, chunk], words.at[1, chunk], x_send.at[first], x_recv.at[first + 1], (g, gx_low, gy)
            ),
            remote(
                sent_words.at[1, chunk], words.at[0, chunk], x_send.at[first + 1], x_recv.at[first], (g, gx_high, gy)
            ),
        ]

    def ends(buf, f, x):
        return jnp.where(row < 4, buf[f, x + 2, 8:16, :], buf[f, x + 2, 48:56, :])

    def z_pack(buf, out, scales):
        for f in range(5):
            for j in range(2):
                a = pair_words(ends(buf, f, 2 * j), ends(buf, f, 2 * j + 4), OFFSETS[f], scales[f])
                b = pair_words(ends(buf, f, 2 * j + 1), ends(buf, f, 2 * j + 5), OFFSETS[f], scales[f])
                out[2 * f + j] = jnp.where((row < 2) | (row >= 6), a, roll_row(b, 4))

    def z_unpack(buf, words, scales):
        for f in range(5):
            for j in range(2):
                word = words[2 * f + j]
                for i, part in enumerate((word, roll_row(word, 4))):
                    for x, tile in zip((2 * j + i, 2 * j + i + 4), split_words(part, OFFSETS[f], scales[f])):
                        buf[f, x + 2, 0:8, :] = tile
                        buf[f, x + 2, 56:64, :] = tile

    def y_add(packed, tile, slot):
        return jnp.where((lane >> 2) == slot, roll_lane(tile, 4 * slot + 2), packed)

    def y_merge(from_low, from_high):
        return jnp.where((lane & 2) == 0, from_low, from_high)

    def y_pack(x, carry):
        packed = jnp.zeros((8, 128), jnp.float32)
        for f in range(5):
            for zt in range(ZT):
                packed = y_add(packed, state[f, x + 2, pl.ds(8 + 8 * zt, 8), :], f * ZT + zt)
        ys1[x] = packed
        return carry

    x_pack(state, xs1, STATE_SCALE, 0)
    pl.semaphore_wait(barrier, 5)
    gossip_send(0)
    x_first = [x_copies(xs1, xr1, 0, chunk) for chunk in range(CHUNKS)]
    x_second = [x_copies(xs2, xr2, 1, chunk) for chunk in range(CHUNKS)]
    first = [
        remote(zs1, zr1, send1.at[0], recv1.at[0], (other, gx, gy)),
        remote(ys1, yr1.at[1], send1.at[1], recv1.at[2], (g, gx, gy_low)),
        remote(ys1, yr1.at[0], send1.at[2], recv1.at[1], (g, gx, gy_high)),
    ]
    for copy in x_first[0]:
        copy.start()
    for chunk in range(1, CHUNKS):
        for copy in load_faces[chunk]:
            copy.wait()
        x_pack(state, xs1, STATE_SCALE, chunk)
        for copy in x_first[chunk]:
            copy.start()
    load_inner.wait()
    z_pack(state, zs1, STATE_SCALE)
    first[0].start()
    lax.fori_loop(0, CX, y_pack, 0)
    first[1].start()
    first[2].start()

    load_ops.wait()
    for copy in load_small:
        copy.wait()

    def widen(i, carry):
        part = pl.ds(pl.multiple_of(i * 512, 512), 512)
        ops_wide[...] = ops_raw[part, :].astype(jnp.float32)
        for w in range(4):
            ops_mat[pl.ds(pl.multiple_of(i * 128, 128), 128), w * 128:(w + 1) * 128] = (
                ops_wide[pl.ds(w, 128, stride=4), :].astype(jnp.bfloat16)
            )
        return carry

    lax.fori_loop(0, 12, widen, 0)
    pair_lane = lane & 31
    owners = jnp.full((8, 128), -99, jnp.int32)
    first_slot, second_slot, seen = (jnp.zeros((8, 128), jnp.int32) for _ in range(3))
    for k in range(4):
        weights = jnp.zeros((8, 128), jnp.int32)
        for x in range(8):
            owner = owner_ref[0, k, x]
            owners = jnp.where((pair_lane == k * 8 + x) & (lane < 96), owner, owners)
            hit = lane == owner
            first_slot = jnp.where(hit & (seen == 0), slot_ref[0, k, x] + 1, first_slot)
            second_slot = jnp.where(hit & (seen == 1), slot_ref[0, k, x] + 1, second_slot)
            seen = jnp.where(hit, seen + 1, seen)
            weights = jnp.where(row == x, weight_ref[0, k, x], weights)
        weight_tiles[k] = weights
    rank_of = jnp.zeros((8, 128), jnp.int32)
    for k in range(4):
        for x in range(8):
            earlier = (owners == owner_ref[0, k, x]) & (pair_lane > k * 8 + x)
            rank_of = rank_of + jnp.where(earlier, 1, 0)
    own_lane = 8 * lax.rem(gx, 16)
    first_slot = pltpu.roll(first_slot.astype(jnp.float32), own_lane + 1, 1)
    second_slot = pltpu.roll(second_slot.astype(jnp.float32), own_lane + 5, 1)
    first_here = (row == 7) & (lane >= own_lane) & (lane < own_lane + 3)
    second_here = (row == 7) & (lane >= own_lane + 4) & (lane < own_lane + 7)
    for d in range(n_gx):
        near = (owners >= d - 1) & (owners <= d + 1)
        spread[d * 8:(d + 1) * 8, :] = jnp.where(near & (owners - (d - 1) + 4 * rank_of == row), 1.0, 0.0)
        slots = jnp.where(second_here, roll_lane(second_slot, -d), 0.0)
        labels[d * 8:(d + 1) * 8, :] = jnp.where(first_here, roll_lane(first_slot, -d), slots)

    gossip_wait(0)
    gossip_send(1)
    first[0].wait_recv()
    z_unpack(state, zr1, STATE_SCALE)
    first[1].wait_recv()
    first[2].wait_recv()

    def first_rate(x, tiles):
        halo = y_merge(yr1[0, x], yr1[1, x])
        packed = jnp.zeros((8, 128), jnp.float32) if tiles[0] == 0 else ys2[x]
        for zt in tiles:
            centre, rates = rate_tile(state, x, zt, halo)
            part = pl.ds(8 * zt, 8)
            inner = pl.ds(8 + 8 * zt, 8)
            new = []
            for f in range(5):
                value = centre[f] + LES_STEP * rates[f]
                pred[f, x + 2, inner, :] = value
                base_sum[f, x, part, :] = centre[f] + (0.5 * LES_STEP) * rates[f]
                packed = y_add(packed, value, f * ZT + zt)
                new.append(value)
            rho, u0, u1, u2, _ = new
            m0, m1 = rho * u0, rho * u1
            s00[x + 2, part, :] = m0 * u0
            s01[x + 1, inner, :] = m0 * u1
            s02[x + 1, part, :] = m0 * u2
            s11[x, inner, :] = m1 * u1
            s12[x, inner, :] = m1 * u2
            s22[x, part, :] = rho * u2 * u2
        ys2[x] = packed

    def rate_inner(x, carry):
        first_rate(x, tuple(range(ZT)))
        return carry

    second = [
        remote(zs2, zr2, send2.at[0], recv2.at[0], (other, gx, gy)),
        remote(ys2, yr2.at[1, 1:9], send2.at[1], recv2.at[2], (g, gx, gy_low)),
        remote(ys2, yr2.at[0, 1:9], send2.at[2], recv2.at[1], (g, gx, gy_high)),
        remote(ezy_s, ezy_r.at[1], send2.at[3], recv2.at[4], (other, gx, gy_low)),
        remote(ezy_s, ezy_r.at[0], send2.at[4], recv2.at[3], (other, gx, gy_high)),
        remote(exz_s.at[0], exz_r.at[1], send2.at[5], recv2.at[6], (other, gx_low, gy)),
        remote(exz_s.at[1], exz_r.at[0], send2.at[6], recv2.at[5], (other, gx_high, gy)),
        remote(ys2.at[0], yr2.at[1, 9], send2.at[7], recv2.at[10], (g, gx_low, gy_low)),
        remote(ys2.at[0], yr2.at[0, 9], send2.at[8], recv2.at[9], (g, gx_low, gy_high)),
        remote(ys2.at[7], yr2.at[1, 0], send2.at[9], recv2.at[8], (g, gx_high, gy_low)),
        remote(ys2.at[7], yr2.at[0, 0], send2.at[10], recv2.at[7], (g, gx_high, gy_high)),
    ]
    lax.fori_loop(2, 6, rate_inner, 0)

    around = [(dx, dr) for dx in (-1, 0, 1) for dr in (-1, 0, 1) if (dx, dr) != (0, 0)]

    def neighbour(dx, dr):
        there = lax.rem(rank + (n_rank + dr), n_rank)
        return (there // n_gy, lax.rem(gx + (n_gx + dx), n_gx), lax.rem(there, n_gy))

    def slot_of(dx, dr):
        return around.index((dx, dr))

    def send_wave(corner):
        for dx, dr in around:
            if (dx * dr != 0) == corner:
                slot = near_wave.at[slot_of(-dx, -dr)]
                remote(wave_ref, slot, wave_send.at[0], wave_recv.at[0], neighbour(dx, dr)).start()

    send_wave(False)
    gossip_wait(1)
    gossip_send(2)
    for chunk in range(CHUNKS):
        for copy in x_first[chunk]:
            copy.wait_recv()
        x_unpack(state, xr1, STATE_SCALE, chunk)
        for x in (6, 7, 0, 1):
            first_rate(x, tuple(range(CHUNK_TILES * chunk, CHUNK_TILES * (chunk + 1))))
        if chunk == CHUNKS - 1:
            for side in range(2):
                x = 7 * side
                exz_s[side] = ends(pred, 0, x) * ends(pred, 1, x) * ends(pred, 2, x)
            for copy in second[5:]:
                copy.start()
        x_pack(pred, xs2, PRED_SCALE, chunk)
        for copy in x_second[chunk]:
            copy.start()

    z_pack(pred, zs2, PRED_SCALE)
    for copy in second[:3]:
        copy.start()
    edge = jnp.zeros((8, 128), jnp.float32)
    for x in range(8):
        product = packed_products(ys2[x])[1]
        both = jnp.where(lane < 4, product, roll_lane(product, -16))
        edge = jnp.where((lane >> 3) == x, roll_lane(both, 8 * x), edge)
    ezy_s[...] = edge
    second[3].start()
    second[4].start()
    gossip_wait(2)
    gossip_send(3)

    second[0].wait_recv()
    z_unpack(pred, zr2, PRED_SCALE)
    for x in range(8):
        for part in (slice(0, 8), slice(56, 64)):
            rho, u0, u1, u2 = (pred[f, x + 2, part, :] for f in range(4))
            m1 = rho * u1
            s01[x + 1, part, :] = m1 * u0
            s11[x, part, :] = m1 * u1
            s12[x, part, :] = m1 * u2
    for copy in second[1:5]:
        copy.wait_recv()
    for x in range(8):
        ym2[x + 1] = y_merge(yr2[0, x + 1], yr2[1, x + 1])
    corners = y_merge(ezy_r[0], ezy_r[1])
    for x in range(8):
        ezy_x[x] = roll_lane(corners, -8 * x)

    def lighthill(x, tiles):
        along_x = packed_products(ym2[x + 2])[0] - packed_products(ym2[x])[0]
        _, s12_halo, square = packed_products(ym2[x + 1])
        corner = ezy_x[x]
        next_tile = jnp.where(lane >= 20, roll_lane(corner, 20), roll_lane(s12_halo, -4))
        last_tile = jnp.where(lane < 4, roll_lane(corner, -4), roll_lane(s12_halo, 4))
        after = roll_row(jnp.where(row == 0, next_tile, s12_halo), -1)
        before = roll_row(jnp.where(row == 7, last_tile, s12_halo), 1)
        cross = along_x + (after - before)
        keep = mask_ref[0, x].astype(jnp.float32)
        for zt in tiles:
            part = pl.ds(8 * zt, 8)

            def z(ref, index, dz):
                return ref[index, pl.ds(8 + 8 * zt + dz, 8), :]

            direct = s00[x + 4, part, :] + s00[x, part, :] - 2.0 * s00[x + 2, part, :]
            direct = direct + (z(s11, x, 2) + z(s11, x, -2) - 2.0 * z(s11, x, 0))
            tile = s22[x, part, :]
            ((before, after),) = y_shifts(tile, square, zt, (2,))
            direct = direct + (before + after - 2.0 * tile)
            mixed = (z(s01, x + 2, 1) - z(s01, x + 2, -1)) - (z(s01, x, 1) - z(s01, x, -1))
            tile = (s02[x + 2, part, :] - s02[x, part, :]) + (z(s12, x, 1) - z(s12, x, -1))
            ((before, after),) = y_shifts(tile, cross, zt, (1,))
            mixed = mixed + (after - before)
            light[pl.ds(pl.multiple_of(x * CZ + 8 * zt, 8), 8), :] = (0.25 * direct + 0.5 * mixed) * keep
        return 0

    lax.fori_loop(2, 6, lambda x, carry: lighthill(x, range(ZT)), 0)
    for chunk in range(CHUNKS):
        for copy in x_second[chunk]:
            copy.wait_recv()
        x_unpack(pred, xr2, PRED_SCALE, chunk)
        part = slice(CHUNK_ROWS * chunk, CHUNK_ROWS * (chunk + 1))
        inner = slice(8 + CHUNK_ROWS * chunk, 8 + CHUNK_ROWS * (chunk + 1))
        for index in (0, 1, 10, 11):
            s00[index, part, :] = pred[0, index, inner, :] * pred[1, index, inner, :] * pred[1, index, inner, :]
        for index, layer in ((0, 1), (9, 10)):
            m0 = pred[0, layer, inner, :] * pred[1, layer, inner, :]
            s01[index, inner, :] = m0 * pred[2, layer, inner, :]
            s02[index, part, :] = m0 * pred[3, layer, inner, :]
        if chunk == CHUNKS - 2:
            for copy in second[5:]:
                copy.wait_recv()
            for index in (0, 9):
                ym2[index] = y_merge(yr2[0, index], yr2[1, index])
            for side, index in ((0, 0), (1, 9)):
                s01[index, 0:8, :] = exz_r[side]
                s01[index, 56:64, :] = exz_r[side]
            ready = range(CHUNK_TILES * (chunk + 1) - 1)
            lax.fori_loop(0, 4, lambda j, carry: lighthill(lax.rem(j + 6, 8), ready), 0)
    send_wave(True)
    late = range(CHUNK_TILES * (CHUNKS - 1) - 1, ZT)
    lax.fori_loop(0, 4, lambda j, carry: lighthill(lax.rem(j + 6, 8), late), 0)

    pieces = []
    for zp in range(12):
        one, two = (
            light[pl.ds(4 * zp + 2 * i, 8, stride=CZ), :] + light[pl.ds(4 * zp + 2 * i + 1, 8, stride=CZ), :]
            for i in range(2)
        )
        one = one + roll_lane(one, -1)
        two = two + roll_lane(two, 1)
        pieces.append(jnp.where((lane & 1) == 0, one, two))
    merged = jnp.concatenate(pieces, axis=0).astype(jnp.bfloat16)
    source_lane = lax.broadcasted_iota(jnp.int32, (128, 128), 0)
    target_lane = lax.broadcasted_iota(jnp.int32, (128, 128), 1)
    order = jnp.where(target_lane == (source_lane & 1) * 64 + (source_lane >> 1), 1.0, 0.0).astype(jnp.bfloat16)
    sorted_rows = jnp.dot(merged, order, preferred_element_type=jnp.float32)
    tile_rows = jnp.concatenate([sorted_rows[8 * i:8 * i + 8, :] for i in range(12)], axis=1).astype(jnp.bfloat16)
    products = jnp.dot(tile_rows, ops_mat[...], preferred_element_type=jnp.float32)
    pairs = []
    for k in range(4):
        chosen = jnp.zeros((8, 128), jnp.float32)
        for w in range(4):
            chosen = jnp.where(weight_tiles[k] == w, products[:, w * 128:(w + 1) * 128], chosen)
        pairs.append(chosen)
    values = jnp.concatenate(pairs, axis=0)
    high = values.astype(jnp.bfloat16).astype(jnp.float32)
    middle = (values - high).astype(jnp.bfloat16).astype(jnp.float32)
    rest = values - high - middle
    stacked = jnp.concatenate([high, middle, rest, jnp.zeros((32, 128), jnp.float32)], axis=0).astype(jnp.bfloat16)
    sent[...] = labels[...] + jnp.dot(spread[...].astype(jnp.bfloat16), stacked, preferred_element_type=jnp.float32)

    gossip_wait(3)
    all_copies = []
    for d in far_order:
        owner = lax.rem(gx + d, n_gx)
        copy = remote(
            sent.at[pl.ds(pl.multiple_of(owner * 8, 8), 8), :], received.at[gx],
            all_send.at[0], all_recv.at[0], (g, owner, gy),
        )
        copy.start()
    received[gx] = sent[pl.ds(pl.multiple_of(gx * 8, 8), 8), :]

    def second_rate(x, carry):
        halo = ym2[x + 1]
        for zt in range(ZT):
            _, rates = rate_tile(pred, x, zt, halo)
            part = pl.ds(8 * zt, 8)
            for f in range(5):
                les_out[f, x, part, :] = base_sum[f, x, part, :] + (0.5 * LES_STEP) * rates[f]
        return carry

    lax.fori_loop(0, CX, second_rate, 0)

    others = received.at[0:n_gx - 1]
    pltpu.make_async_copy(others, others, all_recv.at[0]).wait()
    tags = jnp.concatenate([jnp.sum(received[h:h + 16], axis=0)[7:8, :] for h in (0, 16)], axis=1)
    tags = jnp.broadcast_to(tags, (24, 256))
    line = lax.broadcasted_iota(jnp.int32, (24, 256), 0)
    column = lax.broadcasted_iota(jnp.int32, (24, 256), 1)
    lands = tags + (8 * (column & 3) - 1 - line).astype(jnp.float32)
    gather = jnp.where((tags > 0.5) & (jnp.abs(lands) < 0.5), 1.0, 0.0).astype(jnp.bfloat16)
    arrived = received[...].reshape(n_gx * 8, 128)
    high = arrived.astype(jnp.bfloat16).astype(jnp.float32)
    middle = (arrived - high).astype(jnp.bfloat16).astype(jnp.float32)
    source_lines = jnp.zeros((24, 128), jnp.float32)
    for part in (arrived - high - middle, middle, high):
        source_lines = source_lines + jnp.dot(gather, part.astype(jnp.bfloat16), preferred_element_type=jnp.float32)
    own_source[...] = source_lines
    for i, dr in ((0, -1), (1, 1)):
        remote(own_source, near_source.at[1 - i], src_send.at[0], src_recv.at[0], neighbour(0, dr)).start()

    pltpu.make_async_copy(near_wave, near_wave, wave_recv.at[0]).wait()
    wide_row = lax.broadcasted_iota(jnp.int32, (24, 256), 0)
    wide_lane = lax.broadcasted_iota(jnp.int32, (24, 256), 1)

    def flag(yes):
        return yes.astype(jnp.int32).astype(jnp.float32)

    inside = jnp.where(wide_row < 8, flag(gx > 0), jnp.where(wide_row >= 16, flag(gx < n_gx - 1), 1.0))
    inside = inside * jnp.where(
        wide_lane < 128, 1.0, jnp.where(wide_lane < 192, flag(rank < n_rank - 1), flag(rank > 0))
    )
    column = jnp.where(wide_lane < 192, wide_lane, wide_lane - 256) + rank * 128
    inverse_radius = 1.0 / (column.astype(jnp.float32) + 0.5)

    def assemble(block):
        strips = []
        for dx in (-1, 0, 1):
            side = jnp.where(lane < 64, block(dx, 1), block(dx, -1))
            strips.append(jnp.concatenate([block(dx, 0), side], axis=1))
        return jnp.concatenate(strips, axis=0) * inside

    def wave_block(f):
        return lambda dx, dr: wave_ref[f] if (dx, dr) == (0, 0) else near_wave[slot_of(dx, dr), f]

    now = [assemble(wave_block(f)) for f in range(3)]
    no_source = jnp.zeros((24, 256), jnp.float32)
    opening = wave_rates(now, no_source, inverse_radius)
    pltpu.make_async_copy(near_source, near_source, src_recv.at[0]).wait()
    beside = jnp.where(wide_lane[:, 0:128] < 64, near_source[1], near_source[0])
    source = jnp.concatenate([own_source[...], beside], axis=1) * inside
    for step in range(2):
        if step == 0:
            rate_one = (opening[0] + source, opening[1], opening[2])
        else:
            rate_one = wave_rates(now, source, inverse_radius)
        ahead = [(v + WAVE_STEP * r) * inside for v, r in zip(now, rate_one)]
        rate_two = wave_rates(ahead, source, inverse_radius)
        now = [(v + (0.5 * WAVE_STEP) * (a + b)) * inside for v, a, b in zip(now, rate_one, rate_two)]
    for f in range(3):
        wave_out[f] = now[f][8:16, 0:128]

    for copy in sum(x_first + x_second, first + second):
        copy.wait_send()
    pltpu.make_async_copy(others, others, all_send.at[0]).wait()
    pltpu.make_async_copy(near_wave, near_wave, wave_send.at[0]).wait()
    pltpu.make_async_copy(near_source, near_source, src_send.at[0]).wait()


def hand_on(les_in, wave_in, les_out, wave_out, sems):
    copies = [pltpu.make_async_copy(wave_in, wave_out, sems.at[5])]
    copies += [pltpu.make_async_copy(les_in.at[f], les_out.at[f], sems.at[f]) for f in range(5)]
    for copy in copies:
        copy.start()
    for copy in copies:
        copy.wait()


def on_device(sizes, les_state, wave_state, restriction_ops, pair_owner, pair_slot, pair_weight, tile_mask):
    n_gx = sizes[1]
    tile_len, op_count, width = restriction_ops.shape
    ops_flat = restriction_ops.reshape(tile_len * op_count, width)
    rounds = max(1, (n_gx // 2).bit_length() - 1)
    far_order = sorted(range(1, n_gx), key=lambda d: -(2 * min(d // 8, 4 - d // 8) + min(d % 8, 8 - d % 8)))
    f32, i32, bf16 = jnp.float32, jnp.int32, jnp.bfloat16
    vmem, smem, dma = pltpu.VMEM, pltpu.SMEM, pltpu.SemaphoreType.DMA
    scratch = [
        vmem((5, 12, 64, 128), f32), vmem((5, 12, 64, 128), f32), vmem((5, 8, 48, 128), f32),
        vmem((12, 48, 128), f32), vmem((8, 64, 128), f32), vmem((8, 48, 128), f32),
        vmem((10, 64, 128), f32), vmem((10, 48, 128), f32), vmem((8, 64, 128), f32),
        vmem((3, 8, 128), f32), smem((1, 4, 8), i32), smem((1, 4, 8), i32), smem((1, 4, 8), i32), smem((1, 8), i32),
        vmem((2, CHUNKS, 5, CHUNK_ROWS, 128), i32), vmem((2, CHUNKS, 5, CHUNK_ROWS, 128), i32),
        vmem((2, CHUNKS, 5, CHUNK_ROWS, 128), i32), vmem((2, CHUNKS, 5, CHUNK_ROWS, 128), i32),
        vmem((10, 8, 128), i32), vmem((10, 8, 128), i32), vmem((10, 8, 128), i32), vmem((10, 8, 128), i32),
        vmem((8, 8, 128), f32), vmem((2, 8, 8, 128), f32), vmem((8, 8, 128), f32), vmem((2, 10, 8, 128), f32),
        vmem((10, 8, 128), f32),
        vmem((2, 8, 128), f32), vmem((2, 8, 128), f32), vmem((8, 128), f32), vmem((2, 8, 128), f32),
        vmem((8, 8, 128), f32),
        vmem((CX * CZ, 128), f32), vmem((6144, 128), bf16), vmem((512, 128), f32), vmem((1536, 512), bf16),
        vmem((n_gx * 8, 128), f32), vmem((n_gx * 8, 128), f32), vmem((4, 8, 128), i32),
        vmem((n_gx * 8, 128), f32), vmem((n_gx, 8, 128), f32), vmem((24, 128), f32),
        vmem((2, 24, 128), f32), vmem((8, 3, 8, 128), f32),
        dma((7 + 2 * CHUNKS,)), dma((4 * CHUNKS,)), dma((4 * CHUNKS,)), dma((3,)), dma((3,)), dma((11,)), dma((11,)), dma((1,)), dma((1,)), dma((1,)), dma((1,)),
        dma((1,)), dma((1,)), pltpu.SemaphoreType.REGULAR((rounds,)),
    ]
    any_space = pl.BlockSpec(memory_space=pl.ANY)
    in_vmem = pl.BlockSpec(memory_space=pltpu.VMEM)
    results = pl.pallas_call(
        functools.partial(kernel, sizes, far_order),
        out_shape=(vmem(les_state.shape, f32), vmem(wave_state.shape, f32)),
        in_specs=[any_space] * 7,
        out_specs=(in_vmem, in_vmem),
        scratch_shapes=scratch,
        compiler_params=pltpu.CompilerParams(collective_id=0, has_side_effects=True),
        name="jet_step",
    )(les_state, wave_state, ops_flat, *(a.swapaxes(1, 2) for a in (pair_owner, pair_slot, pair_weight)), tile_mask)
    return pl.pallas_call(
        hand_on,
        out_shape=tuple(jax.ShapeDtypeStruct(r.shape, f32) for r in results),
        in_specs=[in_vmem] * 2,
        out_specs=(any_space,) * 2,
        scratch_shapes=[dma((6,))],
        name="hand_on",
    )(*(pltpu.with_memory_space_constraint(r, pltpu.VMEM) for r in results))


def solution(mesh):
    sizes = (mesh.shape["group"], mesh.shape["gx"], mesh.shape["gy"])
    return jax.shard_map(
        functools.partial(on_device, sizes),
        mesh=mesh,
        in_specs=(
            P(None, "gx", "group", "gy"),
            P(None, "gx", ("group", "gy")),
            P(),
            P(("group", "gy"), "gx", None),
            P(("group", "gy"), "gx", None),
            P(("group", "gy"), "gx", None),
            P(("group", "gy"), "gx"),
        ),
        out_specs=(P(None, "gx", "group", "gy"), P(None, "gx", ("group", "gy"))),
        check_vma=False,
    )
```

```python
import functools

import jax
import jax.numpy as jnp
from jax import lax
from jax.experimental import pallas as pl
from jax.experimental.pallas import tpu as pltpu
from jax.sharding import PartitionSpec as P

MESH = pl.DeviceIdType.MESH
VISCOSITY = 0.05
LES_STEP = 0.2
WAVE_STEP = 0.3
CX, CZ, CY = 8, 48, 128
ZT = CZ // 8
CHUNKS = 3
CHUNK_ROWS = CZ // CHUNKS
CHUNK_TILES = ZT // CHUNKS
OFFSETS = (1.0, 0.0, 0.0, 0.0, 1.0)
STATE_SCALE = (130816.0, 65408.0, 65408.0, 65408.0, 130816.0)
PRED_SCALE = (24576.0,) * 5


def encode(value, offset, scale):
    return ((value - offset) * scale + 32768.5).astype(jnp.int32)


def decode(code, offset, scale):
    return code.astype(jnp.float32) * (1.0 / scale) + (offset - 32768.0 / scale)


def pair_words(first, second, offset, scale):
    return (encode(first, offset, scale) << 16) | encode(second, offset, scale)


def split_words(words, offset, scale):
    first = decode(lax.shift_right_logical(words, 16), offset, scale)
    return first, decode(words & 0xFFFF, offset, scale)


def lanes():
    return lax.broadcasted_iota(jnp.int32, (8, 128), 1)


def rows():
    return lax.broadcasted_iota(jnp.int32, (8, 128), 0)


def roll_lane(tile, shift):
    shift = shift % tile.shape[1]
    return pltpu.roll(tile, shift, 1) if shift else tile


def roll_row(tile, shift):
    shift = shift % tile.shape[0]
    return pltpu.roll(tile, shift, 0) if shift else tile


def y_shifts(tile, halo, slot, reach):
    lane = lanes()
    halo = roll_lane(halo, -(4 * slot + 2))
    shifts = []
    for s in reach:
        before = roll_lane(jnp.where(lane >= 128 - s, halo, tile), s)
        after = roll_lane(jnp.where(lane < s, halo, tile), -s)
        shifts.append((before, after))
    return shifts


def rate_tile(buf, x, zt, halo):
    base = 8 + 8 * zt

    def at(f, dx, dz):
        return buf[f, x + (2 + dx), pl.ds(base + dz, 8), :]

    centre, grads, laps = [], [], []
    for f in range(5):
        c = at(f, 0, 0)
        xm1, xp1, zm1, zp1 = at(f, -1, 0), at(f, 1, 0), at(f, 0, -1), at(f, 0, 1)
        (ym1, yp1), (ym2, yp2) = y_shifts(c, halo, f * ZT + zt, (1, 2))
        dx = 8.0 * (xp1 - xm1) - (at(f, 2, 0) - at(f, -2, 0))
        dz = 8.0 * (zp1 - zm1) - (at(f, 0, 2) - at(f, 0, -2))
        dy = 8.0 * (yp1 - ym1) - (yp2 - ym2)
        centre.append(c)
        grads.append((dx, dz, dy))
        laps.append(((xm1 + xp1) + (zm1 + zp1)) + (ym1 + yp1) - 6.0 * c if 1 <= f <= 3 else None)
    rho, u0, u1, u2, p = centre
    div = grads[1][0] + grads[2][1] + grads[3][2]
    inverse = 1.0 / rho

    def advect(f):
        return u0 * grads[f][0] + u1 * grads[f][1] + u2 * grads[f][2]

    twelfth = -1.0 / 12.0
    rates = [(advect(0) + rho * div) * twelfth]
    for d in range(3):
        rates.append((advect(1 + d) + grads[4][d] * inverse) * twelfth + VISCOSITY * laps[1 + d])
    rates.append((advect(4) + 1.4 * (p * div)) * twelfth)
    return centre, rates


def packed_products(tile):
    momentum = tile * roll_lane(tile, -72)
    return (
        momentum * roll_lane(tile, -24),
        momentum * roll_lane(tile, -48),
        momentum * roll_lane(tile, -72),
    )


def wave_rates(state, source, inverse_radius):
    p, ux, ur = state

    def d(f, axis):
        size = f.shape[axis]
        one = pltpu.roll(f, size - 1, axis) - pltpu.roll(f, 1, axis)
        two = pltpu.roll(f, size - 2, axis) - pltpu.roll(f, 2, axis)
        return (8.0 * one - two) * (1.0 / 12.0)

    return (source - d(ux, 0) - d(ur, 1) - ur * inverse_radius, -d(p, 0), -d(p, 1))


def kernel(
    sizes, far_order,
    les_ref, wave_in, ops_ref, owner_in, slot_in, weight_in, mask_in,
    les_out, wave_out,
    state, pred, base_sum, s00, s11, s22, s01, s02, s12,
    wave_ref, owner_ref, slot_ref, weight_ref, mask_ref,
    xs1, xr1, xs2, xr2, zs1, zr1, zs2, zr2, ys1, yr1, ys2, yr2, ym2,
    exz_s, exz_r, ezy_s, ezy_r, ezy_x,
    light, ops_raw, ops_wide, ops_mat, spread, labels, weight_tiles,
    sent, received, own_source, near_source, near_wave,
    local_sems, x_send, x_recv, send1, recv1, send2, recv2, wave_send, wave_recv, all_send, all_recv, src_send, src_recv, gossip,
):
    n_group, n_gx, n_gy = sizes
    g, gx, gy = lax.axis_index("group"), lax.axis_index("gx"), lax.axis_index("gy")
    rank = g * n_gy + gy
    n_rank = n_group * n_gy
    gx_low, gx_high = lax.rem(gx + (n_gx - 1), n_gx), lax.rem(gx + 1, n_gx)
    gy_low, gy_high = lax.rem(gy + (n_gy - 1), n_gy), lax.rem(gy + 1, n_gy)
    other = 1 - g
    lane, row = lanes(), rows()

    def remote(src, dst, send_sem, recv_sem, device):
        return pltpu.make_async_remote_copy(
            src_ref=src, dst_ref=dst, send_sem=send_sem, recv_sem=recv_sem, device_id=device, device_id_type=MESH
        )

    barrier = pltpu.get_barrier_semaphore()
    for device in ((g, gx_low, gy), (g, gx_high, gy), (other, gx, gy), (g, gx, gy_low), (g, gx, gy_high)):
        pl.semaphore_signal(barrier, inc=1, device_id=device, device_id_type=MESH)

    def load(src, dst, i):
        copy = pltpu.make_async_copy(src, dst, local_sems.at[i])
        copy.start()
        return copy

    def face_rows(chunk):
        return slice(CHUNK_ROWS * chunk, CHUNK_ROWS * (chunk + 1)), slice(
            8 + CHUNK_ROWS * chunk, 8 + CHUNK_ROWS * (chunk + 1)
        )

    load_faces = []
    for chunk in range(CHUNKS):
        theirs, mine = face_rows(chunk)
        load_faces.append(
            [
                load(les_ref.at[:, 0:2, theirs], state.at[:, 2:4, mine, :], 7 + 2 * chunk),
                load(les_ref.at[:, 6:8, theirs], state.at[:, 8:10, mine, :], 8 + 2 * chunk),
            ]
        )
    load_inner = load(les_ref.at[:, 2:6], state.at[:, 4:8, 8:56, :], 0)
    load_small = [
        load(owner_in, owner_ref, 1),
        load(slot_in, slot_ref, 2),
        load(weight_in, weight_ref, 3),
        load(mask_in, mask_ref, 4),
        load(wave_in, wave_ref, 5),
    ]
    load_ops = load(ops_ref, ops_raw, 6)
    for copy in load_faces[0]:
        copy.wait()

    def gossip_send(r):
        if r < gossip.shape[0]:
            d = 1 << r
            for target in (lax.rem(gx + d, n_gx), lax.rem(gx + (n_gx - d), n_gx)):
                pl.semaphore_signal(gossip.at[r], inc=1, device_id=(g, target, gy), device_id_type=MESH)

    def gossip_wait(r):
        if r < gossip.shape[0]:
            pl.semaphore_wait(gossip.at[r], 2)

    def x_pack(buf, out, scales, chunk):
        part = slice(8 + CHUNK_ROWS * chunk, 8 + CHUNK_ROWS * (chunk + 1))
        for f in range(5):
            for side, first in ((0, 2), (1, 8)):
                out[side, chunk, f] = pair_words(
                    buf[f, first, part, :], buf[f, first + 1, part, :], OFFSETS[f], scales[f]
                )

    def x_unpack(buf, words, scales, chunk):
        part = slice(8 + CHUNK_ROWS * chunk, 8 + CHUNK_ROWS * (chunk + 1))
        for f in range(5):
            for side, first in ((0, 0), (1, 10)):
                one, two = split_words(words[side, chunk, f], OFFSETS[f], scales[f])
                buf[f, first, part, :] = one
                buf[f, first + 1, part, :] = two

    def x_copies(sent_words, words, stage, chunk):
        first = 2 * (CHUNKS * stage + chunk)
        return [
            remote(
                sent_words.at[0, chunk], words.at[1, chunk], x_send.at[first], x_recv.at[first + 1], (g, gx_low, gy)
            ),
            remote(
                sent_words.at[1, chunk], words.at[0, chunk], x_send.at[first + 1], x_recv.at[first], (g, gx_high, gy)
            ),
        ]

    def ends(buf, f, x):
        return jnp.where(row < 4, buf[f, x + 2, 8:16, :], buf[f, x + 2, 48:56, :])

    def z_pack(buf, out, scales):
        for f in range(5):
            for j in range(2):
                a = pair_words(ends(buf, f, 2 * j), ends(buf, f, 2 * j + 4), OFFSETS[f], scales[f])
                b = pair_words(ends(buf, f, 2 * j + 1), ends(buf, f, 2 * j + 5), OFFSETS[f], scales[f])
                out[2 * f + j] = jnp.where((row < 2) | (row >= 6), a, roll_row(b, 4))

    def z_unpack(buf, words, scales):
        for f in range(5):
            for j in range(2):
                word = words[2 * f + j]
                for i, part in enumerate((word, roll_row(word, 4))):
                    for x, tile in zip((2 * j + i, 2 * j + i + 4), split_words(part, OFFSETS[f], scales[f])):
                        buf[f, x + 2, 0:8, :] = tile
                        buf[f, x + 2, 56:64, :] = tile

    def y_add(packed, tile, slot):
        return jnp.where((lane >> 2) == slot, roll_lane(tile, 4 * slot + 2), packed)

    def y_merge(from_low, from_high):
        return jnp.where((lane & 2) == 0, from_low, from_high)

    def y_pack(x, carry):
        packed = jnp.zeros((8, 128), jnp.float32)
        for f in range(5):
            for zt in range(ZT):
                packed = y_add(packed, state[f, x + 2, pl.ds(8 + 8 * zt, 8), :], f * ZT + zt)
        ys1[x] = packed
        return carry

    x_pack(state, xs1, STATE_SCALE, 0)
    pl.semaphore_wait(barrier, 5)
    gossip_send(0)
    x_first = [x_copies(xs1, xr1, 0, chunk) for chunk in range(CHUNKS)]
    x_second = [x_copies(xs2, xr2, 1, chunk) for chunk in range(CHUNKS)]
    first = [
        remote(zs1, zr1, send1.at[0], recv1.at[0], (other, gx, gy)),
        remote(ys1, yr1.at[1], send1.at[1], recv1.at[2], (g, gx, gy_low)),
        remote(ys1, yr1.at[0], send1.at[2], recv1.at[1], (g, gx, gy_high)),
    ]
    for copy in x_first[0]:
        copy.start()
    for chunk in range(1, CHUNKS):
        for copy in load_faces[chunk]:
            copy.wait()
        x_pack(state, xs1, STATE_SCALE, chunk)
        for copy in x_first[chunk]:
            copy.start()
    load_inner.wait()
    z_pack(state, zs1, STATE_SCALE)
    first[0].start()
    lax.fori_loop(0, CX, y_pack, 0)
    first[1].start()
    first[2].start()

    load_ops.wait()
    for copy in load_small:
        copy.wait()

    def widen(i, carry):
        part = pl.ds(pl.multiple_of(i * 512, 512), 512)
        ops_wide[...] = ops_raw[part, :].astype(jnp.float32)
        for w in range(4):
            ops_mat[pl.ds(pl.multiple_of(i * 128, 128), 128), w * 128:(w + 1) * 128] = (
                ops_wide[pl.ds(w, 128, stride=4), :].astype(jnp.bfloat16)
            )
        return carry

    lax.fori_loop(0, 12, widen, 0)
    pair_lane = lane & 31
    owners = jnp.full((8, 128), -99, jnp.int32)
    first_slot, second_slot, seen = (jnp.zeros((8, 128), jnp.int32) for _ in range(3))
    for k in range(4):
        weights = jnp.zeros((8, 128), jnp.int32)
        for x in range(8):
            owner = owner_ref[0, k, x]
            owners = jnp.where((pair_lane == k * 8 + x) & (lane < 96), owner, owners)
            hit = lane == owner
            first_slot = jnp.where(hit & (seen == 0), slot_ref[0, k, x] + 1, first_slot)
            second_slot = jnp.where(hit & (seen == 1), slot_ref[0, k, x] + 1, second_slot)
            seen = jnp.where(hit, seen + 1, seen)
            weights = jnp.where(row == x, weight_ref[0, k, x], weights)
        weight_tiles[k] = weights
    rank_of = jnp.zeros((8, 128), jnp.int32)
    for k in range(4):
        for x in range(8):
            earlier = (owners == owner_ref[0, k, x]) & (pair_lane > k * 8 + x)
            rank_of = rank_of + jnp.where(earlier, 1, 0)
    own_lane = 8 * lax.rem(gx, 16)
    first_slot = pltpu.roll(first_slot.astype(jnp.float32), own_lane + 1, 1)
    second_slot = pltpu.roll(second_slot.astype(jnp.float32), own_lane + 5, 1)
    first_here = (row == 7) & (lane >= own_lane) & (lane < own_lane + 3)
    second_here = (row == 7) & (lane >= own_lane + 4) & (lane < own_lane + 7)
    for d in range(n_gx):
        near = (owners >= d - 1) & (owners <= d + 1)
        spread[d * 8:(d + 1) * 8, :] = jnp.where(near & (owners - (d - 1) + 4 * rank_of == row), 1.0, 0.0)
        slots = jnp.where(second_here, roll_lane(second_slot, -d), 0.0)
        labels[d * 8:(d + 1) * 8, :] = jnp.where(first_here, roll_lane(first_slot, -d), slots)

    gossip_wait(0)
    gossip_send(1)
    first[0].wait_recv()
    z_unpack(state, zr1, STATE_SCALE)
    first[1].wait_recv()
    first[2].wait_recv()

    def first_rate(x, tiles):
        halo = y_merge(yr1[0, x], yr1[1, x])
        packed = jnp.zeros((8, 128), jnp.float32) if tiles[0] == 0 else ys2[x]
        for zt in tiles:
            centre, rates = rate_tile(state, x, zt, halo)
            part = pl.ds(8 * zt, 8)
            inner = pl.ds(8 + 8 * zt, 8)
            new = []
            for f in range(5):
                value = centre[f] + LES_STEP * rates[f]
                pred[f, x + 2, inner, :] = value
                base_sum[f, x, part, :] = centre[f] + (0.5 * LES_STEP) * rates[f]
                packed = y_add(packed, value, f * ZT + zt)
                new.append(value)
            rho, u0, u1, u2, _ = new
            m0, m1 = rho * u0, rho * u1
            s00[x + 2, part, :] = m0 * u0
            s01[x + 1, inner, :] = m0 * u1
            s02[x + 1, part, :] = m0 * u2
            s11[x, inner, :] = m1 * u1
            s12[x, inner, :] = m1 * u2
            s22[x, part, :] = rho * u2 * u2
        ys2[x] = packed

    def rate_inner(x, carry):
        first_rate(x, tuple(range(ZT)))
        return carry

    second = [
        remote(zs2, zr2, send2.at[0], recv2.at[0], (other, gx, gy)),
        remote(ys2, yr2.at[1, 1:9], send2.at[1], recv2.at[2], (g, gx, gy_low)),
        remote(ys2, yr2.at[0, 1:9], send2.at[2], recv2.at[1], (g, gx, gy_high)),
        remote(ezy_s, ezy_r.at[1], send2.at[3], recv2.at[4], (other, gx, gy_low)),
        remote(ezy_s, ezy_r.at[0], send2.at[4], recv2.at[3], (other, gx, gy_high)),
        remote(exz_s.at[0], exz_r.at[1], send2.at[5], recv2.at[6], (other, gx_low, gy)),
        remote(exz_s.at[1], exz_r.at[0], send2.at[6], recv2.at[5], (other, gx_high, gy)),
        remote(ys2.at[0], yr2.at[1, 9], send2.at[7], recv2.at[10], (g, gx_low, gy_low)),
        remote(ys2.at[0], yr2.at[0, 9], send2.at[8], recv2.at[9], (g, gx_low, gy_high)),
        remote(ys2.at[7], yr2.at[1, 0], send2.at[9], recv2.at[8], (g, gx_high, gy_low)),
        remote(ys2.at[7], yr2.at[0, 0], send2.at[10], recv2.at[7], (g, gx_high, gy_high)),
    ]
    lax.fori_loop(2, 6, rate_inner, 0)

    around = [(dx, dr) for dx in (-1, 0, 1) for dr in (-1, 0, 1) if (dx, dr) != (0, 0)]

    def neighbour(dx, dr):
        there = lax.rem(rank + (n_rank + dr), n_rank)
        return (there // n_gy, lax.rem(gx + (n_gx + dx), n_gx), lax.rem(there, n_gy))

    def slot_of(dx, dr):
        return around.index((dx, dr))

    def send_wave(corner):
        for dx, dr in around:
            if (dx * dr != 0) == corner:
                slot = near_wave.at[slot_of(-dx, -dr)]
                remote(wave_ref, slot, wave_send.at[0], wave_recv.at[0], neighbour(dx, dr)).start()

    send_wave(False)
    gossip_wait(1)
    gossip_send(2)
    for chunk in range(CHUNKS):
        for copy in x_first[chunk]:
            copy.wait_recv()
        x_unpack(state, xr1, STATE_SCALE, chunk)
        for x in (6, 7, 0, 1):
            first_rate(x, tuple(range(CHUNK_TILES * chunk, CHUNK_TILES * (chunk + 1))))
        if chunk == CHUNKS - 1:
            for side in range(2):
                x = 7 * side
                exz_s[side] = ends(pred, 0, x) * ends(pred, 1, x) * ends(pred, 2, x)
            for copy in second[5:]:
                copy.start()
        x_pack(pred, xs2, PRED_SCALE, chunk)
        for copy in x_second[chunk]:
            copy.start()

    z_pack(pred, zs2, PRED_SCALE)
    for copy in second[:3]:
        copy.start()
    edge = jnp.zeros((8, 128), jnp.float32)
    for x in range(8):
        product = packed_products(ys2[x])[1]
        both = jnp.where(lane < 4, product, roll_lane(product, -16))
        edge = jnp.where((lane >> 3) == x, roll_lane(both, 8 * x), edge)
    ezy_s[...] = edge
    second[3].start()
    second[4].start()
    gossip_wait(2)
    gossip_send(3)

    second[0].wait_recv()
    z_unpack(pred, zr2, PRED_SCALE)
    for x in range(8):
        for part in (slice(0, 8), slice(56, 64)):
            rho, u0, u1, u2 = (pred[f, x + 2, part, :] for f in range(4))
            m1 = rho * u1
            s01[x + 1, part, :] = m1 * u0
            s11[x, part, :] = m1 * u1
            s12[x, part, :] = m1 * u2
    for copy in second[1:5]:
        copy.wait_recv()
    for x in range(8):
        ym2[x + 1] = y_merge(yr2[0, x + 1], yr2[1, x + 1])
    corners = y_merge(ezy_r[0], ezy_r[1])
    for x in range(8):
        ezy_x[x] = roll_lane(corners, -8 * x)

    def lighthill(x, carry):
        along_x = packed_products(ym2[x + 2])[0] - packed_products(ym2[x])[0]
        _, s12_halo, square = packed_products(ym2[x + 1])
        corner = ezy_x[x]
        next_tile = jnp.where(lane >= 20, roll_lane(corner, 20), roll_lane(s12_halo, -4))
        last_tile = jnp.where(lane < 4, roll_lane(corner, -4), roll_lane(s12_halo, 4))
        after = roll_row(jnp.where(row == 0, next_tile, s12_halo), -1)
        before = roll_row(jnp.where(row == 7, last_tile, s12_halo), 1)
        cross = along_x + (after - before)
        keep = mask_ref[0, x].astype(jnp.float32)
        for zt in range(ZT):
            part = pl.ds(8 * zt, 8)

            def z(ref, index, dz):
                return ref[index, pl.ds(8 + 8 * zt + dz, 8), :]

            direct = s00[x + 4, part, :] + s00[x, part, :] - 2.0 * s00[x + 2, part, :]
            direct = direct + (z(s11, x, 2) + z(s11, x, -2) - 2.0 * z(s11, x, 0))
            tile = s22[x, part, :]
            ((before, after),) = y_shifts(tile, square, zt, (2,))
            direct = direct + (before + after - 2.0 * tile)
            mixed = (z(s01, x + 2, 1) - z(s01, x + 2, -1)) - (z(s01, x, 1) - z(s01, x, -1))
            tile = (s02[x + 2, part, :] - s02[x, part, :]) + (z(s12, x, 1) - z(s12, x, -1))
            ((before, after),) = y_shifts(tile, cross, zt, (1,))
            mixed = mixed + (after - before)
            light[pl.ds(pl.multiple_of(x * CZ + 8 * zt, 8), 8), :] = (0.25 * direct + 0.5 * mixed) * keep
        return carry

    lax.fori_loop(2, 6, lighthill, 0)
    for chunk in range(CHUNKS):
        for copy in x_second[chunk]:
            copy.wait_recv()
        x_unpack(pred, xr2, PRED_SCALE, chunk)
    for index in (0, 1, 10, 11):
        s00[index] = pred[0, index, 8:56, :] * pred[1, index, 8:56, :] * pred[1, index, 8:56, :]
    for index, layer in ((0, 1), (9, 10)):
        m0 = pred[0, layer, 8:56, :] * pred[1, layer, 8:56, :]
        s01[index, 8:56, :] = m0 * pred[2, layer, 8:56, :]
        s02[index] = m0 * pred[3, layer, 8:56, :]
    send_wave(True)
    for copy in second[5:]:
        copy.wait_recv()
    for index in (0, 9):
        ym2[index] = y_merge(yr2[0, index], yr2[1, index])
    for side, index in ((0, 0), (1, 9)):
        s01[index, 0:8, :] = exz_r[side]
        s01[index, 56:64, :] = exz_r[side]
    lax.fori_loop(0, 4, lambda j, carry: lighthill(lax.rem(j + 6, 8), carry), 0)

    pieces = []
    for zp in range(12):
        one, two = (
            light[pl.ds(4 * zp + 2 * i, 8, stride=CZ), :] + light[pl.ds(4 * zp + 2 * i + 1, 8, stride=CZ), :]
            for i in range(2)
        )
        one = one + roll_lane(one, -1)
        two = two + roll_lane(two, 1)
        pieces.append(jnp.where((lane & 1) == 0, one, two))
    merged = jnp.concatenate(pieces, axis=0).astype(jnp.bfloat16)
    source_lane = lax.broadcasted_iota(jnp.int32, (128, 128), 0)
    target_lane = lax.broadcasted_iota(jnp.int32, (128, 128), 1)
    order = jnp.where(target_lane == (source_lane & 1) * 64 + (source_lane >> 1), 1.0, 0.0).astype(jnp.bfloat16)
    sorted_rows = jnp.dot(merged, order, preferred_element_type=jnp.float32)
    tile_rows = jnp.concatenate([sorted_rows[8 * i:8 * i + 8, :] for i in range(12)], axis=1).astype(jnp.bfloat16)
    products = jnp.dot(tile_rows, ops_mat[...], preferred_element_type=jnp.float32)
    pairs = []
    for k in range(4):
        chosen = jnp.zeros((8, 128), jnp.float32)
        for w in range(4):
            chosen = jnp.where(weight_tiles[k] == w, products[:, w * 128:(w + 1) * 128], chosen)
        pairs.append(chosen)
    values = jnp.concatenate(pairs, axis=0)
    high = values.astype(jnp.bfloat16).astype(jnp.float32)
    middle = (values - high).astype(jnp.bfloat16).astype(jnp.float32)
    rest = values - high - middle
    stacked = jnp.concatenate([high, middle, rest, jnp.zeros((32, 128), jnp.float32)], axis=0).astype(jnp.bfloat16)
    sent[...] = labels[...] + jnp.dot(spread[...].astype(jnp.bfloat16), stacked, preferred_element_type=jnp.float32)

    gossip_wait(3)
    all_copies = []
    for d in far_order:
        owner = lax.rem(gx + d, n_gx)
        copy = remote(
            sent.at[pl.ds(pl.multiple_of(owner * 8, 8), 8), :], received.at[gx],
            all_send.at[0], all_recv.at[0], (g, owner, gy),
        )
        copy.start()
    received[gx] = sent[pl.ds(pl.multiple_of(gx * 8, 8), 8), :]

    def second_rate(x, carry):
        halo = ym2[x + 1]
        for zt in range(ZT):
            _, rates = rate_tile(pred, x, zt, halo)
            part = pl.ds(8 * zt, 8)
            for f in range(5):
                les_out[f, x, part, :] = base_sum[f, x, part, :] + (0.5 * LES_STEP) * rates[f]
        return carry

    lax.fori_loop(0, CX, second_rate, 0)

    others = received.at[0:n_gx - 1]
    pltpu.make_async_copy(others, others, all_recv.at[0]).wait()
    tags = jnp.concatenate([jnp.sum(received[h:h + 16], axis=0)[7:8, :] for h in (0, 16)], axis=1)
    tags = jnp.broadcast_to(tags, (24, 256))
    line = lax.broadcasted_iota(jnp.int32, (24, 256), 0)
    column = lax.broadcasted_iota(jnp.int32, (24, 256), 1)
    lands = tags + (8 * (column & 3) - 1 - line).astype(jnp.float32)
    gather = jnp.where((tags > 0.5) & (jnp.abs(lands) < 0.5), 1.0, 0.0).astype(jnp.bfloat16)
    arrived = received[...].reshape(n_gx * 8, 128)
    high = arrived.astype(jnp.bfloat16).astype(jnp.float32)
    middle = (arrived - high).astype(jnp.bfloat16).astype(jnp.float32)
    source_lines = jnp.zeros((24, 128), jnp.float32)
    for part in (arrived - high - middle, middle, high):
        source_lines = source_lines + jnp.dot(gather, part.astype(jnp.bfloat16), preferred_element_type=jnp.float32)
    own_source[...] = source_lines
    for i, dr in ((0, -1), (1, 1)):
        remote(own_source, near_source.at[1 - i], src_send.at[0], src_recv.at[0], neighbour(0, dr)).start()

    pltpu.make_async_copy(near_wave, near_wave, wave_recv.at[0]).wait()
    wide_row = lax.broadcasted_iota(jnp.int32, (24, 256), 0)
    wide_lane = lax.broadcasted_iota(jnp.int32, (24, 256), 1)

    def flag(yes):
        return yes.astype(jnp.int32).astype(jnp.float32)

    inside = jnp.where(wide_row < 8, flag(gx > 0), jnp.where(wide_row >= 16, flag(gx < n_gx - 1), 1.0))
    inside = inside * jnp.where(
        wide_lane < 128, 1.0, jnp.where(wide_lane < 192, flag(rank < n_rank - 1), flag(rank > 0))
    )
    column = jnp.where(wide_lane < 192, wide_lane, wide_lane - 256) + rank * 128
    inverse_radius = 1.0 / (column.astype(jnp.float32) + 0.5)

    def assemble(block):
        strips = []
        for dx in (-1, 0, 1):
            side = jnp.where(lane < 64, block(dx, 1), block(dx, -1))
            strips.append(jnp.concatenate([block(dx, 0), side], axis=1))
        return jnp.concatenate(strips, axis=0) * inside

    def wave_block(f):
        return lambda dx, dr: wave_ref[f] if (dx, dr) == (0, 0) else near_wave[slot_of(dx, dr), f]

    now = [assemble(wave_block(f)) for f in range(3)]
    no_source = jnp.zeros((24, 256), jnp.float32)
    opening = wave_rates(now, no_source, inverse_radius)
    for copy in sum(x_first + x_second, first + second):
        copy.wait_send()
    pltpu.make_async_copy(others, others, all_send.at[0]).wait()
    pltpu.make_async_copy(near_wave, near_wave, wave_send.at[0]).wait()
    pltpu.make_async_copy(near_source, near_source, src_recv.at[0]).wait()
    beside = jnp.where(wide_lane[:, 0:128] < 64, near_source[1], near_source[0])
    source = jnp.concatenate([own_source[...], beside], axis=1) * inside
    for step in range(2):
        if step == 0:
            rate_one = (opening[0] + source, opening[1], opening[2])
        else:
            rate_one = wave_rates(now, source, inverse_radius)
        ahead = [(v + WAVE_STEP * r) * inside for v, r in zip(now, rate_one)]
        rate_two = wave_rates(ahead, source, inverse_radius)
        now = [(v + (0.5 * WAVE_STEP) * (a + b)) * inside for v, a, b in zip(now, rate_one, rate_two)]
    for f in range(3):
        wave_out[f] = now[f][8:16, 0:128]

    pltpu.make_async_copy(near_source, near_source, src_send.at[0]).wait()


def hand_on(les_in, wave_in, les_out, wave_out, sems):
    copies = [pltpu.make_async_copy(wave_in, wave_out, sems.at[5])]
    copies += [pltpu.make_async_copy(les_in.at[f], les_out.at[f], sems.at[f]) for f in range(5)]
    for copy in copies:
        copy.start()
    for copy in copies:
        copy.wait()


def on_device(sizes, les_state, wave_state, restriction_ops, pair_owner, pair_slot, pair_weight, tile_mask):
    n_gx = sizes[1]
    tile_len, op_count, width = restriction_ops.shape
    ops_flat = restriction_ops.reshape(tile_len * op_count, width)
    rounds = max(1, (n_gx // 2).bit_length() - 1)
    far_order = sorted(range(1, n_gx), key=lambda d: -(2 * min(d // 8, 4 - d // 8) + min(d % 8, 8 - d % 8)))
    f32, i32, bf16 = jnp.float32, jnp.int32, jnp.bfloat16
    vmem, smem, dma = pltpu.VMEM, pltpu.SMEM, pltpu.SemaphoreType.DMA
    scratch = [
        vmem((5, 12, 64, 128), f32), vmem((5, 12, 64, 128), f32), vmem((5, 8, 48, 128), f32),
        vmem((12, 48, 128), f32), vmem((8, 64, 128), f32), vmem((8, 48, 128), f32),
        vmem((10, 64, 128), f32), vmem((10, 48, 128), f32), vmem((8, 64, 128), f32),
        vmem((3, 8, 128), f32), smem((1, 4, 8), i32), smem((1, 4, 8), i32), smem((1, 4, 8), i32), smem((1, 8), i32),
        vmem((2, CHUNKS, 5, CHUNK_ROWS, 128), i32), vmem((2, CHUNKS, 5, CHUNK_ROWS, 128), i32),
        vmem((2, CHUNKS, 5, CHUNK_ROWS, 128), i32), vmem((2, CHUNKS, 5, CHUNK_ROWS, 128), i32),
        vmem((10, 8, 128), i32), vmem((10, 8, 128), i32), vmem((10, 8, 128), i32), vmem((10, 8, 128), i32),
        vmem((8, 8, 128), f32), vmem((2, 8, 8, 128), f32), vmem((8, 8, 128), f32), vmem((2, 10, 8, 128), f32),
        vmem((10, 8, 128), f32),
        vmem((2, 8, 128), f32), vmem((2, 8, 128), f32), vmem((8, 128), f32), vmem((2, 8, 128), f32),
        vmem((8, 8, 128), f32),
        vmem((CX * CZ, 128), f32), vmem((6144, 128), bf16), vmem((512, 128), f32), vmem((1536, 512), bf16),
        vmem((n_gx * 8, 128), f32), vmem((n_gx * 8, 128), f32), vmem((4, 8, 128), i32),
        vmem((n_gx * 8, 128), f32), vmem((n_gx, 8, 128), f32), vmem((24, 128), f32),
        vmem((2, 24, 128), f32), vmem((8, 3, 8, 128), f32),
        dma((7 + 2 * CHUNKS,)), dma((4 * CHUNKS,)), dma((4 * CHUNKS,)), dma((3,)), dma((3,)), dma((11,)), dma((11,)), dma((1,)), dma((1,)), dma((1,)), dma((1,)),
        dma((1,)), dma((1,)), pltpu.SemaphoreType.REGULAR((rounds,)),
    ]
    any_space = pl.BlockSpec(memory_space=pl.ANY)
    in_vmem = pl.BlockSpec(memory_space=pltpu.VMEM)
    results = pl.pallas_call(
        functools.partial(kernel, sizes, far_order),
        out_shape=(vmem(les_state.shape, f32), vmem(wave_state.shape, f32)),
        in_specs=[any_space] * 7,
        out_specs=(in_vmem, in_vmem),
        scratch_shapes=scratch,
        compiler_params=pltpu.CompilerParams(collective_id=0, has_side_effects=True),
        name="jet_step",
    )(les_state, wave_state, ops_flat, *(a.swapaxes(1, 2) for a in (pair_owner, pair_slot, pair_weight)), tile_mask)
    return pl.pallas_call(
        hand_on,
        out_shape=tuple(jax.ShapeDtypeStruct(r.shape, f32) for r in results),
        in_specs=[in_vmem] * 2,
        out_specs=(any_space,) * 2,
        scratch_shapes=[dma((6,))],
        name="hand_on",
    )(*(pltpu.with_memory_space_constraint(r, pltpu.VMEM) for r in results))


def solution(mesh):
    sizes = (mesh.shape["group"], mesh.shape["gx"], mesh.shape["gy"])
    return jax.shard_map(
        functools.partial(on_device, sizes),
        mesh=mesh,
        in_specs=(
            P(None, "gx", "group", "gy"),
            P(None, "gx", ("group", "gy")),
            P(),
            P(("group", "gy"), "gx", None),
            P(("group", "gy"), "gx", None),
            P(("group", "gy"), "gx", None),
            P(("group", "gy"), "gx"),
        ),
        out_specs=(P(None, "gx", "group", "gy"), P(None, "gx", ("group", "gy"))),
        check_vma=False,
    )
```
